128 devices in a mesh: dp: 4 (over x), fsdp: 32 (over z, y, core).
Axes of the slice: x: 4, y: 4, z: 4, core: 2. Of those that a mesh axis runs over, the one named last changes fastest.
Arguments:
- mlp_input: bfloat16 [1024, 4096], P('dp', 'fsdp'), may hold values from -6 to 6
- residual_in: bfloat16 [1024, 4096], P(('dp', 'fsdp')), may hold values from -6 to 6
- gate_weight: bfloat16 [4096, 14336], P(None, 'fsdp'), may hold values from -0.09375 to 0.09375
- up_weight: bfloat16 [4096, 14336], P(None, 'fsdp'), may hold values from -0.09375 to 0.09375
- down_weight: bfloat16 [14336, 4096], P('fsdp'), may hold values from -0.046875 to 0.046875
- span_index: bfloat16 [65536, 4096], P(('dp', 'fsdp')), may hold values from -6 to 6
- positive_keys: bfloat16 [1024, 4096], P(('dp', 'fsdp')), may hold values from -6 to 6
- request_rows: int32 [128, 128, 8], P(None, ('dp', 'fsdp')), may hold values from 0 to 511, as said below
- request_counts: int32 [128, 128], P(None, ('dp', 'fsdp')), may hold values from 0 to 8, as said below
- negative_slots: int32 [1024, 64], P(('dp', 'fsdp')), may hold values from 0 to 1023, as said below
Outputs:
- query_loss: float32 [1024], P(('dp', 'fsdp'))
- input_grad: bfloat16 [1024, 4096], P('dp', 'fsdp')
- gate_grad: bfloat16 [4096, 14336], P('dp', 'fsdp')
- up_grad: bfloat16 [4096, 14336], P('dp', 'fsdp')
- down_grad: bfloat16 [14336, 4096], P('fsdp', 'dp')
The draws below stay inside these ranges and needn't reach their ends.
Inputs may be any that keep to these rules, and one draw needn't show every extreme that they name: `request_rows`: entry [r, o, s] is a local row of shard o; it is read only where s < request_counts[r, o]. `request_counts`: for each requesting device r the counts over the 128 shards sum to 512, and some shard gets exactly 8. `negative_slots`: rows q of device r = q // 8; an entry o * 8 + s names slot s of shard o with s < request_counts[r, o]; the 512 entries of a device use each such slot exactly once.
All inputs are finite; a program needn't handle non-finite values.
Results may differ from the reference program's by a relative error of at most 0.017.
Values may be sent and summed in bfloat16 or wider, within the bound.
A program may use at most 128 MiB of HBM per device.

```python
import jax
import jax.numpy as jnp
from jax import lax

D = 4096
FF = 14336
NEG = 64
QD = 8
CH_DEV = 512
OWNERS = 128
QUERIES = 1024
CAP = 8
SPANS = 65536
N_DP = 4


def request_plan(key):
    half_cap = QD * NEG // OWNERS
    slot_cap = 2 * half_cap

    def plan_one(sub_key):
        key_order, key_lift, key_rank = jax.random.split(sub_key, 3)
        middle = (jax.random.permutation(key_order, OWNERS - 2) + 1).astype(jnp.int32)
        owner_order = jnp.concatenate([jnp.array([OWNERS - 1], jnp.int32), middle[:1], jnp.array([0], jnp.int32), middle[1:]])
        count_lift = jax.random.randint(key_lift, (OWNERS // 2,), 0, half_cap + 1)
        count_lift = count_lift.at[0].set(half_cap)
        pattern = jnp.stack([half_cap + count_lift, half_cap - count_lift], axis=1).reshape(-1).astype(jnp.int32)
        counts = jnp.zeros((OWNERS,), jnp.int32).at[owner_order].set(pattern)
        places = jnp.arange(OWNERS * slot_cap, dtype=jnp.int32)
        live_mask = places % slot_cap < counts[places // slot_cap]
        slot_rank = jax.random.permutation(key_rank, OWNERS * slot_cap).astype(jnp.int32)
        sort_key = jnp.where(live_mask, slot_rank, slot_rank + OWNERS * slot_cap)
        chosen = jnp.argsort(sort_key, stable=True)[:QD * NEG].astype(jnp.int32)
        return (counts, chosen.reshape(QD, NEG))
    device_keys = jax.random.split(jax.random.fold_in(key, 7), OWNERS)
    return jax.vmap(plan_one)(device_keys)


def draw_request_counts(key, part):
    counts, chosen = request_plan(key)
    return counts


def draw_negative_slots(key, part):
    counts, chosen = request_plan(key)
    return chosen.reshape(OWNERS * QD, NEG)


def draw_request_rows(key, part):
    return jax.random.randint(jax.random.fold_in(key, 11), (OWNERS, OWNERS, CAP), 0, CH_DEV).astype(jnp.int32)


def block_scale(key, shape, pieces, least, high):
    gain = 1.0
    for position, blocks in pieces:
        draws = jax.random.uniform(jax.random.fold_in(jax.random.fold_in(key, 6), position), (blocks,), jnp.float32, least / len(pieces), high / len(pieces))
        gain = gain * jnp.repeat(jnp.exp(draws), shape[position] // blocks).reshape((-1,) + (1,) * (len(shape) - 1 - position))
    return gain


def centred(stream_key, extent, width, bound, pieces=(), kind=jnp.bfloat16):
    level = block_scale(stream_key, extent, pieces, -0.22, 0.18) if pieces else 1.0
    values = jax.random.normal(stream_key, extent, jnp.float32) * width * level
    return jnp.minimum(jnp.maximum(values, -bound), bound).astype(kind)


def setup_inputs(seed: int = 0) -> dict:
    seeds = jax.random.split(jax.random.key(seed), 11)
    mlp_input = centred(seeds[0], (QUERIES, D), 1.0, 6.0, ((0, 4), (1, 32)))
    residual_in = centred(seeds[1], (QUERIES, D), 1.0, 6.0, ((0, 128),))
    gate_weight = centred(seeds[2], (D, FF), D ** -0.5, 0.09375, ((1, 32),))
    up_weight = centred(seeds[3], (D, FF), D ** -0.5, 0.09375, ((1, 32),))
    down_weight = centred(seeds[4], (FF, D), FF ** -0.5, 0.046875, ((0, 32),))
    span_index = centred(seeds[5], (SPANS, D), 1.0, 6.0, ((0, 128),))
    positive_keys = centred(seeds[6], (QUERIES, D), 1.0, 6.0, ((0, 128),))
    request_rows = draw_request_rows(jax.random.fold_in(seeds[10], 71), 0)
    request_counts = draw_request_counts(jax.random.fold_in(seeds[10], 71), 0)
    negative_slots = draw_negative_slots(jax.random.fold_in(seeds[10], 71), 0)
    return dict(mlp_input=mlp_input, residual_in=residual_in, gate_weight=gate_weight, up_weight=up_weight, down_weight=down_weight, span_index=span_index, positive_keys=positive_keys, request_rows=request_rows, request_counts=request_counts, negative_slots=negative_slots)


inverse_temp = 50.0
eps = 1e-06

def silu_grad(gate_act):
    sigmoid_gate = jax.nn.sigmoid(gate_act)
    return sigmoid_gate * (1.0 + gate_act * (1.0 - sigmoid_gate))

def contrast(unit_rows, row_norm, key_block):
    key_unit = key_block / jnp.sqrt(lax.optimization_barrier(jnp.sum(key_block * key_block, axis=-1, keepdims=True)) + eps)
    scores = inverse_temp * jnp.einsum('qd,qnd->qn', unit_rows, key_unit, precision=lax.Precision.HIGHEST)
    weights = jnp.exp(scores)
    exp_total = lax.optimization_barrier(jnp.sum(weights, axis=-1))
    query_loss = jnp.log(exp_total) - scores[:, 0]
    column = lax.broadcasted_iota(jnp.int32, scores.shape, 1)
    coeffs = weights / exp_total[:, None] - (column == 0).astype(scores.dtype)
    pull_term = inverse_temp * jnp.einsum('qn,qnd->qd', coeffs, key_unit, precision=lax.Precision.HIGHEST)
    inner_term = lax.optimization_barrier(jnp.sum(coeffs * scores, axis=-1))
    head_grad = ((pull_term - inner_term[:, None] * unit_rows) / row_norm[:, None]).astype(jnp.bfloat16)
    return (query_loss, head_grad)

def group_sum(left_rows, right_rows, groups):
    group_rows = left_rows.shape[0] // groups
    result = jnp.zeros((left_rows.shape[1], right_rows.shape[1]), jnp.float32)
    for group_index in range(groups):
        lower = group_index * group_rows
        partial_term = lax.dot_general(left_rows[lower:lower + group_rows], right_rows[lower:lower + group_rows], (((0,), (0,)), ((), ())), preferred_element_type=jnp.float32)
        rounded = lax.optimization_barrier(partial_term.astype(jnp.bfloat16))
        result = result + rounded.astype(jnp.float32)
    return result.astype(jnp.bfloat16)

def reference(mlp_input, residual_in, gate_weight, up_weight, down_weight, span_index, positive_keys, request_rows, request_counts, negative_slots):
    gate_act = jnp.dot(mlp_input, gate_weight, preferred_element_type=jnp.float32)
    up_act = jnp.dot(mlp_input, up_weight, preferred_element_type=jnp.float32)
    hidden = (jax.nn.silu(gate_act) * up_act).astype(jnp.bfloat16)
    top_state = jnp.dot(hidden, down_weight, preferred_element_type=jnp.float32) + residual_in.astype(jnp.float32)
    row_norm = jnp.sqrt(lax.optimization_barrier(jnp.sum(top_state * top_state, axis=-1)) + eps)
    unit_rows = top_state / row_norm[:, None]

    def per_device(block_args):
        unit_block, norm_block, positive_block, slot_block, row_table, count_table = block_args
        owner_of = slot_block // CAP
        place_of = slot_block % CAP
        local_row = row_table[owner_of, place_of]
        live_mask = place_of < count_table[owner_of]
        fetched = jnp.take(span_index, (owner_of * CH_DEV + local_row).astype(jnp.int32), axis=0).astype(jnp.float32)
        fetched = jnp.where(live_mask[..., None], fetched, jnp.zeros_like(fetched))
        key_block = jnp.concatenate([positive_block.astype(jnp.float32)[:, None, :], fetched], axis=1)
        return contrast(unit_block, norm_block, key_block)
    query_loss, head_grad = lax.map(per_device, (unit_rows.reshape(OWNERS, QD, D), row_norm.reshape(OWNERS, QD), positive_keys.reshape(OWNERS, QD, D), negative_slots.reshape(OWNERS, QD, NEG), request_rows, request_counts))
    query_loss = query_loss.reshape(-1)
    head_grad = head_grad.reshape(-1, D)
    hidden_grad = jnp.dot(head_grad, down_weight.T, preferred_element_type=jnp.float32)
    gate_grad_act = (hidden_grad * up_act * silu_grad(gate_act)).astype(jnp.bfloat16)
    up_grad_act = (hidden_grad * jax.nn.silu(gate_act)).astype(jnp.bfloat16)
    input_grad = (jnp.dot(gate_grad_act, gate_weight.T, preferred_element_type=jnp.float32) + jnp.dot(up_grad_act, up_weight.T, preferred_element_type=jnp.float32)).astype(jnp.bfloat16)
    gate_grad = group_sum(mlp_input, gate_grad_act, N_DP)
    up_grad = group_sum(mlp_input, up_grad_act, N_DP)
    down_grad = group_sum(hidden, head_grad, N_DP)
    return (query_loss, input_grad, gate_grad, up_grad, down_grad)
```

```python
import jax
import jax.numpy as jnp
from jax import lax
from jax.sharding import PartitionSpec as P

inverse_temp = 50.0
eps = 1e-06
contract_first = (((0,), (0,)), ((), ()))
contract_last = (((1,), (1,)), ((), ()))


def split3(v):
    hi = lax.reduce_precision(v, 8, 7)
    mid = lax.reduce_precision(v - hi, 8, 7)
    return jnp.concatenate([hi, mid, v - hi - mid], axis=0).astype(jnp.bfloat16)


def contrast(top_state, positive_keys, buffer, negative_slots):
    rows = top_state.shape[0]
    slots = buffer.shape[0]
    row_norm = jnp.sqrt(jnp.sum(top_state * top_state, axis=-1) + eps)
    unit_rows = top_state / row_norm[:, None]
    positive = positive_keys.astype(jnp.float32)
    positive_unit = positive / jnp.sqrt(jnp.sum(positive * positive, axis=-1, keepdims=True) + eps)
    positive_score = inverse_temp * jnp.sum(unit_rows * positive_unit, axis=-1)

    wide = buffer.astype(jnp.float32)
    key_scale = lax.rsqrt(jnp.sum(wide * wide, axis=-1) + eps)
    raw = lax.dot_general(
        split3(unit_rows), buffer, contract_last, preferred_element_type=jnp.float32
    )
    raw = raw[:rows] + raw[rows : 2 * rows] + raw[2 * rows :]
    scores = inverse_temp * raw * key_scale[None, :]
    slot_ids = lax.broadcasted_iota(jnp.int32, (1, 1, slots), 2)
    uses = jnp.sum((negative_slots[:, :, None] == slot_ids).astype(jnp.float32), axis=1)
    weights = jnp.where(uses > 0, uses * jnp.exp(scores), 0.0)
    positive_weight = jnp.exp(positive_score)
    exp_total = jnp.sum(weights, axis=-1) + positive_weight
    query_loss = jnp.log(exp_total) - positive_score
    coeffs = weights / exp_total[:, None]
    positive_coeff = positive_weight / exp_total - 1.0
    pull = lax.dot_general(
        split3(coeffs * key_scale[None, :]),
        buffer,
        (((1,), (0,)), ((), ())),
        preferred_element_type=jnp.float32,
    )
    pull = pull[:rows] + pull[rows : 2 * rows] + pull[2 * rows :]
    pull = inverse_temp * (pull + positive_coeff[:, None] * positive_unit)
    inner = jnp.sum(coeffs * scores, axis=-1) + positive_coeff * positive_score
    head_grad = ((pull - inner[:, None] * unit_rows) / row_norm[:, None]).astype(jnp.bfloat16)
    return query_loss, head_grad


def shards(
    mlp_input,
    residual_in,
    gate_weight,
    up_weight,
    down_weight,
    span_index,
    positive_keys,
    request_rows,
    request_counts,
    negative_slots,
):
    owners = lax.axis_size("dp") * lax.axis_size("fsdp")
    slot_cap = request_rows.shape[2]
    width = span_index.shape[1]

    row_table = request_rows[:, 0, :]
    live = lax.broadcasted_iota(jnp.int32, row_table.shape, 1) < request_counts
    wanted = jnp.where(live, row_table, -1).reshape(-1)
    pick = (wanted[:, None] == lax.broadcasted_iota(jnp.int32, (1, span_index.shape[0]), 1)).astype(
        jnp.bfloat16
    )
    picked = jnp.dot(pick, span_index, preferred_element_type=jnp.bfloat16)
    buffer = lax.all_to_all(
        picked.reshape(owners, slot_cap, width),
        ("dp", "fsdp"),
        split_axis=0,
        concat_axis=0,
        tiled=True,
    ).reshape(owners * slot_cap, width)

    whole_input = lax.all_gather(mlp_input, "fsdp", axis=1, tiled=True)
    gate_act = jnp.dot(whole_input, gate_weight, preferred_element_type=jnp.float32)
    up_act = jnp.dot(whole_input, up_weight, preferred_element_type=jnp.float32)
    sigmoid_gate = jax.nn.sigmoid(gate_act)
    silu_gate = gate_act * sigmoid_gate
    hidden = (silu_gate * up_act).astype(jnp.bfloat16)
    branch = lax.psum_scatter(
        jnp.dot(hidden, down_weight, preferred_element_type=jnp.float32).astype(jnp.bfloat16),
        "fsdp",
        scatter_dimension=0,
        tiled=True,
    ).astype(jnp.float32)
    top_state = branch + residual_in.astype(jnp.float32)
    all_hidden = lax.all_gather(hidden, "dp", axis=0, tiled=True)
    input_cols = lax.all_to_all(whole_input, "dp", split_axis=1, concat_axis=0, tiled=True)

    query_loss, head_grad = contrast(top_state, positive_keys, buffer, negative_slots)

    gathered_grad = lax.all_gather(head_grad, "fsdp", axis=0, tiled=True)
    hidden_grad = lax.dot_general(
        gathered_grad, down_weight, contract_last, preferred_element_type=jnp.float32
    )
    silu_slope = sigmoid_gate * (1.0 + gate_act * (1.0 - sigmoid_gate))
    gate_grad_act = (hidden_grad * up_act * silu_slope).astype(jnp.bfloat16)
    up_grad_act = (hidden_grad * silu_gate).astype(jnp.bfloat16)
    both_acts = lax.all_gather(
        jnp.concatenate([gate_grad_act, up_grad_act], axis=1), "dp", axis=0, tiled=True
    )
    input_term = lax.dot_general(
        gate_grad_act, gate_weight, contract_last, preferred_element_type=jnp.float32
    ) + lax.dot_general(up_grad_act, up_weight, contract_last, preferred_element_type=jnp.float32)
    input_grad = lax.psum_scatter(
        input_term.astype(jnp.bfloat16), "fsdp", scatter_dimension=1, tiled=True
    )
    head_cols = lax.all_to_all(gathered_grad, "dp", split_axis=1, concat_axis=0, tiled=True)
    down_grad = lax.dot_general(
        all_hidden, head_cols, contract_first, preferred_element_type=jnp.float32
    ).astype(jnp.bfloat16)
    units = gate_weight.shape[1]
    gate_grad = lax.dot_general(
        input_cols, both_acts[:, :units], contract_first, preferred_element_type=jnp.float32
    ).astype(jnp.bfloat16)
    up_grad = lax.dot_general(
        input_cols, both_acts[:, units:], contract_first, preferred_element_type=jnp.float32
    ).astype(jnp.bfloat16)
    return (query_loss, input_grad, gate_grad, up_grad, down_grad)


def solution(mesh):
    return jax.shard_map(
        shards,
        mesh=mesh,
        in_specs=(
            P("dp", "fsdp"),
            P(("dp", "fsdp"), None),
            P(None, "fsdp"),
            P(None, "fsdp"),
            P("fsdp", None),
            P(("dp", "fsdp"), None),
            P(("dp", "fsdp"), None),
            P(None, ("dp", "fsdp"), None),
            P(None, ("dp", "fsdp")),
            P(("dp", "fsdp"), None),
        ),
        out_specs=(
            P(("dp", "fsdp")),
            P("dp", "fsdp"),
            P("dp", "fsdp"),
            P("dp", "fsdp"),
            P("fsdp", "dp"),
        ),
        check_vma=False,
    )
```

```python
import functools

import jax
import jax.numpy as jnp
from jax import lax
from jax.experimental import pallas as pl
from jax.experimental.pallas import tpu as pltpu
from jax.sharding import PartitionSpec as P

inverse_temp = 50.0
eps = 1e-06
contract_first = (((0,), (0,)), ((), ()))
contract_last = (((1,), (1,)), ((), ()))
ANY = pl.BlockSpec(memory_space=pl.ANY)
VMEM = pl.BlockSpec(memory_space=pltpu.VMEM)
DMA = pltpu.SemaphoreType.DMA
near_first = (1, 3, 2)


class Place:
    def __init__(self):
        self.x = lax.axis_index("dp")
        self.f = lax.axis_index("fsdp")
        self.z = self.f // 8
        self.y = (self.f // 2) % 4
        self.c = self.f % 2
        self.a = self.y * (1 - self.c) + self.z * self.c
        self.b = self.z * (1 - self.c) + self.y * self.c
        self.partner = self.f + 1 - 2 * self.c

    def at(self, b, a, c):
        z = b * (1 - c) + a * c
        y = a * (1 - c) + b * c
        return (z * 4 + y) * 2 + c

    def a_peer(self, j):
        return self.at(self.b, (self.a + j) % 4, self.c)

    def b_peer(self, j):
        return self.at((self.b + j) % 4, self.a, self.c)


def copy_to(src, dst, send, recv, x, f):
    return pltpu.make_async_remote_copy(
        src_ref=src,
        dst_ref=dst,
        send_sem=send,
        recv_sem=recv,
        device_id=(x, f),
        device_id_type=pl.DeviceIdType.MESH,
    )


def meet(place, across):
    barrier = pltpu.get_barrier_semaphore()
    peers = [(place.x, place.partner)]
    peers += [(place.x, place.a_peer(j)) for j in near_first]
    peers += [(place.x, place.b_peer(j)) for j in near_first]
    if across:
        peers += [((place.x + j) % 4, place.f) for j in near_first]
    for x, f in peers:
        pl.semaphore_signal(barrier, inc=1, device_id=(x, f), device_id_type=pl.DeviceIdType.MESH)
    pl.semaphore_wait(barrier, len(peers))


class PlaneGather:
    copies = 32

    def __init__(self, place, src, out, view, send, recv):
        self.place, self.src, self.out, self.view = place, src, out, view
        self.send, self.recv = send, recv
        self.sent = []

    def push(self, ref, origin, f):
        copy = copy_to(
            ref,
            self.view(self.out, origin),
            self.send.at[len(self.sent)],
            self.recv.at[origin],
            self.place.x,
            f,
        )
        copy.start()
        self.sent.append(copy)

    def arrive(self, origin):
        block = self.view(self.out, origin)
        copy_to(
            block, block, self.send.at[31], self.recv.at[origin], self.place.x, self.place.partner
        ).wait_recv()
        return block

    def start(self):
        p = self.place
        self.own = pltpu.make_async_copy(self.src, self.view(self.out, p.f), self.send.at[31])
        for j in near_first:
            self.push(self.src, p.f, p.a_peer(j))
        for j in near_first:
            self.push(self.src, p.f, p.b_peer(j))
        self.push(self.src, p.f, p.partner)
        self.own.start()

    def relay(self):
        p = self.place
        for j in near_first:
            origin = p.a_peer(j)
            block = self.arrive(origin)
            for i in near_first:
                self.push(block, origin, p.b_peer(i))
            self.push(block, origin, p.partner)

    def finish(self):
        p = self.place
        for j in (0,) + near_first:
            for i in near_first:
                origin = p.at((p.b + i) % 4, (p.a + j) % 4, p.c)
                self.push(self.arrive(origin), origin, p.partner)
        for j in (0,) + near_first:
            for i in (0,) + near_first:
                z, y = (p.z + i) % 4, (p.y + j) % 4
                self.arrive((z * 4 + y) * 2 + 1 - p.c)
        self.own.wait()
        for copy in self.sent:
            copy.wait_send()


class PlaneScatter:
    def __init__(self, place, src, view, scratch):
        self.place, self.src, self.view = place, src, view
        (self.got1, self.sum1, self.got2, self.sum2, self.got3, self.send1, self.recv1,
         self.send2, self.recv2, self.send3, self.recv3) = scratch

    @staticmethod
    def scratch(block):
        wide = lambda *lead: pltpu.VMEM(lead + block, jnp.bfloat16)
        return [wide(16), wide(4, 4), wide(4, 4), wide(4), wide(4), DMA((16,)), DMA((16,)),
                DMA((4,)), DMA((4,)), DMA((4,)), DMA((4,))]

    def start(self):
        p = self.place
        self.sent1 = []
        for i in (2, 1, 3, 0):
            for a in range(4):
                b = (p.a + i) % 4
                k = b * 4 + a
                copy = copy_to(
                    self.view(self.src, p.at(b, a, 1 - p.c)),
                    self.got1.at[k],
                    self.send1.at[k],
                    self.recv1.at[k],
                    p.x,
                    p.partner,
                )
                copy.start()
                self.sent1.append(copy)

    def middle(self):
        p = self.place
        sent2 = []
        for i in (2, 1, 3, 0):
            b = (p.b + i) % 4
            for a in range(4):
                k = b * 4 + a
                copy_to(
                    self.got1.at[k], self.got1.at[k], self.send1.at[k], self.recv1.at[k],
                    p.x, p.partner,
                ).wait_recv()
                own = self.view(self.src, p.at(b, a, p.c))[...].astype(jnp.float32)
                self.sum1[b, a] = (own + self.got1[k].astype(jnp.float32)).astype(jnp.bfloat16)
            if i:
                copy = copy_to(
                    self.sum1.at[b], self.got2.at[p.b], self.send2.at[i], self.recv2.at[p.b],
                    p.x, p.b_peer(i),
                )
                copy.start()
                sent2.append(copy)
        for i in near_first:
            b = (p.b + i) % 4
            copy_to(
                self.got2.at[b], self.got2.at[b], self.send2.at[i], self.recv2.at[b],
                p.x, p.b_peer(i),
            ).wait_recv()
        sent3 = []
        for j in (2, 1, 3, 0):
            a = (p.a + j) % 4
            total = self.sum1[p.b, a].astype(jnp.float32)
            for i in near_first:
                total += self.got2[(p.b + i) % 4, a].astype(jnp.float32)
            if j:
                self.sum2[a] = total.astype(jnp.bfloat16)
                copy = copy_to(
                    self.sum2.at[a], self.got3.at[p.a], self.send3.at[j], self.recv3.at[p.a],
                    p.x, p.a_peer(j),
                )
                copy.start()
                sent3.append(copy)
        for j in near_first:
            a = (p.a + j) % 4
            copy_to(
                self.got3.at[a], self.got3.at[a], self.send3.at[j], self.recv3.at[a],
                p.x, p.a_peer(j),
            ).wait_recv()
            total += self.got3[a].astype(jnp.float32)
        for copy in self.sent1 + sent2 + sent3:
            copy.wait_send()
        return total


def across_gather(place, src, out, send, recv):
    own = pltpu.make_async_copy(src, out.at[place.x], send.at[0])
    own.start()
    sent = []
    for j in near_first:
        copy = copy_to(src, out.at[place.x], send.at[j], recv.at[place.x], (place.x + j) % 4, place.f)
        copy.start()
        sent.append(copy)

    def finish():
        for j in near_first:
            x = (place.x + j) % 4
            copy_to(out.at[x], out.at[x], send.at[j], recv.at[x], x, place.f).wait_recv()
        own.wait()
        for copy in sent:
            copy.wait_send()

    return finish


def params(collective_id):
    return pltpu.CompilerParams(
        collective_id=collective_id, has_side_effects=True, vmem_limit_bytes=40 * 1024 * 1024
    )


def column_block(ref, f):
    return ref.at[:, pl.ds(pl.multiple_of(f * 128, 128), 128)]


def row_block(ref, f):
    return ref.at[f]


def gather_input(mlp_input):
    def kernel(src, out, send, recv):
        place = Place()
        meet(place, False)
        gather = PlaneGather(place, src, out, column_block, send, recv)
        gather.start()
        gather.relay()
        gather.finish()

    rows, cols = mlp_input.shape
    return pl.pallas_call(
        kernel,
        out_shape=jax.ShapeDtypeStruct((rows, cols * 32), jnp.bfloat16),
        in_specs=[ANY],
        out_specs=ANY,
        scratch_shapes=[DMA((32,)), DMA((32,))],
        compiler_params=params(0),
        name="gather_input",
    )(mlp_input)


def scatter_branch(partial):
    def kernel(src, out, *scratch):
        place = Place()
        meet(place, False)
        scatter = PlaneScatter(place, src, row_block, scratch)
        scatter.start()
        out[...] = scatter.middle()

    return pl.pallas_call(
        kernel,
        out_shape=jax.ShapeDtypeStruct((8, 4096), jnp.float32),
        in_specs=[VMEM],
        out_specs=VMEM,
        scratch_shapes=PlaneScatter.scratch((8, 4096)),
        compiler_params=params(1),
        name="scatter_branch",
    )(partial.reshape(32, 8, 4096))


def gather_head(head_grad, hidden, whole_input):
    def kernel(head, hid, inp, out, head_x, hid_x, inp_x, send, recv, hx_send, hx_recv,
               h_send, h_recv, i_send, i_recv, pair_send, pair_recv):
        place = Place()
        p = place
        meet(place, True)
        gather = PlaneGather(place, head, out, row_block, send, recv)
        gather.start()
        wide = lambda x: pl.ds(pl.multiple_of(x * 1024, 1024), 1024)
        half = lambda c: pl.ds(pl.multiple_of(c * 512, 512), 512)
        own_h = pltpu.make_async_copy(head.at[:, wide(p.x)], head_x.at[p.x], hx_send.at[0])
        own_h.start()
        own_i = pltpu.make_async_copy(inp.at[:, wide(p.x)], inp_x.at[p.x], i_send.at[0])
        own_i.start()
        sent = []
        for j in near_first:
            x = (p.x + j) % 4
            copy = copy_to(head.at[:, wide(x)], head_x.at[p.x], hx_send.at[j], hx_recv.at[p.x], x, p.f)
            copy.start()
            sent.append(copy)
        finish_hidden = across_gather(place, hid, hid_x, h_send, h_recv)
        for j in near_first:
            x = (p.x + j) % 4
            copy = copy_to(
                inp.at[:, pl.ds(pl.multiple_of(x * 1024 + p.c * 512, 512), 512)],
                inp_x.at[p.x, :, half(p.c)], i_send.at[j], i_recv.at[p.x], x, p.f,
            )
            copy.start()
            sent.append(copy)
        gather.relay()
        gather.finish()
        for j in near_first:
            x = (p.x + j) % 4
            copy_to(
                head_x.at[x], head_x.at[x], hx_send.at[j], hx_recv.at[x], x, p.f
            ).wait_recv()
        for j in near_first:
            x = (p.x + j) % 4
            region = inp_x.at[x, :, half(p.c)]
            copy_to(region, region, i_send.at[j], i_recv.at[x], x, p.f).wait_recv()
            copy = copy_to(region, region, pair_send.at[j], pair_recv.at[x], p.x, p.partner)
            copy.start()
            sent.append(copy)
        for j in near_first:
            x = (p.x + j) % 4
            region = inp_x.at[x, :, half(1 - p.c)]
            copy_to(region, region, pair_send.at[j], pair_recv.at[x], p.x, p.partner).wait_recv()
        finish_hidden()
        own_h.wait()
        own_i.wait()
        for copy in sent:
            copy.wait_send()

    bf = lambda *shape: jax.ShapeDtypeStruct(shape, jnp.bfloat16)
    out, head_x, hid_x, inp_x = pl.pallas_call(
        kernel,
        out_shape=(bf(32, 8, 4096), bf(4, 8, 1024), bf(4, *hidden.shape), bf(4, 256, 1024)),
        in_specs=[ANY] * 3,
        out_specs=[ANY] * 4,
        scratch_shapes=[DMA((32,)), DMA((32,))] + [DMA((4,))] * 8,
        compiler_params=params(2),
        name="gather_head",
    )(head_grad, hidden, whole_input)
    return out.reshape(256, 4096), head_x, hid_x, inp_x


def finish_links(partial, acts, head_x):
    def kernel(src, act, hx, out, act_x, head_cols, send, recv, x_send, x_recv, *scratch):
        place = Place()
        meet(place, True)
        finish_acts = across_gather(place, act, act_x, x_send, x_recv)
        scatter = PlaneScatter(place, src, column_block, scratch)
        scatter.start()
        gather = PlaneGather(
            place, hx, head_cols, lambda ref, f: ref.at[:, f], send, recv
        )
        out[...] = scatter.middle().astype(jnp.bfloat16)
        gather.start()
        gather.relay()
        gather.finish()
        finish_acts()

    bf = lambda *shape: jax.ShapeDtypeStruct(shape, jnp.bfloat16)
    return pl.pallas_call(
        kernel,
        out_shape=(bf(256, 128), bf(4, *acts.shape), bf(4, 32, 8, 1024)),
        in_specs=[VMEM, ANY, ANY],
        out_specs=[VMEM, ANY, ANY],
        scratch_shapes=[DMA((32,)), DMA((32,)), DMA((4,)), DMA((4,))]
        + PlaneScatter.scratch((256, 128)),
        compiler_params=params(3),
        name="finish_links",
    )(partial, acts, head_x)


def split3(v):
    hi = lax.reduce_precision(v, 8, 7)
    mid = lax.reduce_precision(v - hi, 8, 7)
    return jnp.concatenate([hi, mid, v - hi - mid], axis=0).astype(jnp.bfloat16)


def contrast(top_state, positive_keys, buffer, negative_slots):
    rows = top_state.shape[0]
    slots = buffer.shape[0]
    row_norm = jnp.sqrt(jnp.sum(top_state * top_state, axis=-1) + eps)
    unit_rows = top_state / row_norm[:, None]
    positive = positive_keys.astype(jnp.float32)
    positive_unit = positive / jnp.sqrt(jnp.sum(positive * positive, axis=-1, keepdims=True) + eps)
    positive_score = inverse_temp * jnp.sum(unit_rows * positive_unit, axis=-1)

    wide = buffer.astype(jnp.float32)
    key_scale = lax.rsqrt(jnp.sum(wide * wide, axis=-1) + eps)
    raw = lax.dot_general(
        split3(unit_rows), buffer, contract_last, preferred_element_type=jnp.float32
    )
    raw = raw[:rows] + raw[rows : 2 * rows] + raw[2 * rows :]
    scores = inverse_temp * raw * key_scale[None, :]
    slot_ids = lax.broadcasted_iota(jnp.int32, (1, 1, slots), 2)
    uses = jnp.sum((negative_slots[:, :, None] == slot_ids).astype(jnp.float32), axis=1)
    weights = jnp.where(uses > 0, uses * jnp.exp(scores), 0.0)
    positive_weight = jnp.exp(positive_score)
    exp_total = jnp.sum(weights, axis=-1) + positive_weight
    query_loss = jnp.log(exp_total) - positive_score
    coeffs = weights / exp_total[:, None]
    positive_coeff = positive_weight / exp_total - 1.0
    pull = lax.dot_general(
        split3(coeffs * key_scale[None, :]),
        buffer,
        (((1,), (0,)), ((), ())),
        preferred_element_type=jnp.float32,
    )
    pull = pull[:rows] + pull[rows : 2 * rows] + pull[2 * rows :]
    pull = inverse_temp * (pull + positive_coeff[:, None] * positive_unit)
    inner = jnp.sum(coeffs * scores, axis=-1) + positive_coeff * positive_score
    head_grad = ((pull - inner[:, None] * unit_rows) / row_norm[:, None]).astype(jnp.bfloat16)
    return query_loss, head_grad


def shards(
    mlp_input,
    residual_in,
    gate_weight,
    up_weight,
    down_weight,
    span_index,
    positive_keys,
    request_rows,
    request_counts,
    negative_slots,
):
    owners = lax.axis_size("dp") * lax.axis_size("fsdp")
    slot_cap = request_rows.shape[2]
    width = span_index.shape[1]

    row_table = request_rows[:, 0, :]
    live = lax.broadcasted_iota(jnp.int32, row_table.shape, 1) < request_counts
    wanted = jnp.where(live, row_table, -1).reshape(-1)
    pick = (wanted[:, None] == lax.broadcasted_iota(jnp.int32, (1, span_index.shape[0]), 1)).astype(
        jnp.bfloat16
    )
    picked = jnp.dot(pick, span_index, preferred_element_type=jnp.bfloat16)
    buffer = lax.all_to_all(
        picked.reshape(owners, slot_cap, width),
        ("dp", "fsdp"),
        split_axis=0,
        concat_axis=0,
        tiled=True,
    ).reshape(owners * slot_cap, width)

    whole_input = gather_input(mlp_input)
    gate_act = jnp.dot(whole_input, gate_weight, preferred_element_type=jnp.float32)
    up_act = jnp.dot(whole_input, up_weight, preferred_element_type=jnp.float32)
    sigmoid_gate = jax.nn.sigmoid(gate_act)
    silu_gate = gate_act * sigmoid_gate
    hidden = (silu_gate * up_act).astype(jnp.bfloat16)
    branch = scatter_branch(jnp.dot(hidden, down_weight, preferred_element_type=jnp.bfloat16))
    top_state = branch + residual_in.astype(jnp.float32)

    query_loss, head_grad = contrast(top_state, positive_keys, buffer, negative_slots)

    gathered_grad, head_x, hidden_x, input_x = gather_head(head_grad, hidden.T, whole_input)
    hidden_grad = lax.dot_general(
        gathered_grad, down_weight, contract_last, preferred_element_type=jnp.float32
    )
    silu_slope = sigmoid_gate * (1.0 + gate_act * (1.0 - sigmoid_gate))
    gate_grad_act = (hidden_grad * up_act * silu_slope).astype(jnp.bfloat16)
    up_grad_act = (hidden_grad * silu_gate).astype(jnp.bfloat16)
    input_term = lax.dot_general(
        gate_grad_act, gate_weight, contract_last, preferred_element_type=jnp.float32
    ) + lax.dot_general(up_grad_act, up_weight, contract_last, preferred_element_type=jnp.float32)
    input_grad, acts_x, head_cols = finish_links(
        input_term.astype(jnp.bfloat16),
        jnp.concatenate([gate_grad_act.T, up_grad_act.T], axis=0),
        head_x,
    )
    units = gate_weight.shape[1]
    over_groups = (((0, 2), (0, 1)), ((), ()))
    down_grad = lax.dot_general(
        hidden_x, head_cols.reshape(4, 256, 1024), over_groups, preferred_element_type=jnp.float32
    ).astype(jnp.bfloat16)
    both = lax.dot_general(
        acts_x, input_x, over_groups, preferred_element_type=jnp.float32
    ).astype(jnp.bfloat16)
    return (query_loss, input_grad, both[:units].T, both[units:].T, down_grad)


def solution(mesh):
    return jax.shard_map(
        shards,
        mesh=mesh,
        in_specs=(
            P("dp", "fsdp"),
            P(("dp", "fsdp"), None),
            P(None, "fsdp"),
            P(None, "fsdp"),
            P("fsdp", None),
            P(("dp", "fsdp"), None),
            P(("dp", "fsdp"), None),
            P(None, ("dp", "fsdp"), None),
            P(None, ("dp", "fsdp")),
            P(("dp", "fsdp"), None),
        ),
        out_specs=(
            P(("dp", "fsdp")),
            P("dp", "fsdp"),
            P("dp", "fsdp"),
            P("dp", "fsdp"),
            P("fsdp", "dp"),
        ),
        check_vma=False,
    )
```

```python
import functools

import jax
import jax.numpy as jnp
from jax import lax
from jax.experimental import pallas as pl
from jax.experimental.pallas import tpu as pltpu
from jax.sharding import PartitionSpec as P

inverse_temp = 50.0
eps = 1e-06
contract_first = (((0,), (0,)), ((), ()))
contract_last = (((1,), (1,)), ((), ()))
ANY = pl.BlockSpec(memory_space=pl.ANY)
VMEM = pl.BlockSpec(memory_space=pltpu.VMEM)
DMA = pltpu.SemaphoreType.DMA
near_first = (1, 3, 2)


class Place:
    def __init__(self):
        self.x = lax.axis_index("dp")
        self.f = lax.axis_index("fsdp")
        self.z = self.f // 8
        self.y = (self.f // 2) % 4
        self.c = self.f % 2
        self.a = self.y * (1 - self.c) + self.z * self.c
        self.b = self.z * (1 - self.c) + self.y * self.c
        self.partner = self.f + 1 - 2 * self.c

    def at(self, b, a, c):
        z = b * (1 - c) + a * c
        y = a * (1 - c) + b * c
        return (z * 4 + y) * 2 + c

    def a_peer(self, j):
        return self.at(self.b, (self.a + j) % 4, self.c)

    def b_peer(self, j):
        return self.at((self.b + j) % 4, self.a, self.c)


def copy_to(src, dst, send, recv, x, f):
    return pltpu.make_async_remote_copy(
        src_ref=src,
        dst_ref=dst,
        send_sem=send,
        recv_sem=recv,
        device_id=(x, f),
        device_id_type=pl.DeviceIdType.MESH,
    )


def meet(place, across):
    barrier = pltpu.get_barrier_semaphore()
    peers = [(place.x, place.partner)]
    peers += [(place.x, place.a_peer(j)) for j in near_first]
    peers += [(place.x, place.b_peer(j)) for j in near_first]
    if across:
        peers += [((place.x + j) % 4, place.f) for j in near_first]
    for x, f in peers:
        pl.semaphore_signal(barrier, inc=1, device_id=(x, f), device_id_type=pl.DeviceIdType.MESH)
    pl.semaphore_wait(barrier, len(peers))


class PlaneGather:
    copies = 32

    def __init__(self, place, src, out, view, send, recv):
        self.place, self.src, self.out, self.view = place, src, out, view
        self.send, self.recv = send, recv
        self.sent = []

    def push(self, ref, origin, f):
        copy = copy_to(
            ref,
            self.view(self.out, origin),
            self.send.at[len(self.sent)],
            self.recv.at[origin],
            self.place.x,
            f,
        )
        copy.start()
        self.sent.append(copy)

    def arrive(self, origin):
        block = self.view(self.out, origin)
        copy_to(
            block, block, self.send.at[31], self.recv.at[origin], self.place.x, self.place.partner
        ).wait_recv()
        return block

    def start(self):
        p = self.place
        self.own = pltpu.make_async_copy(self.src, self.view(self.out, p.f), self.send.at[31])
        for j in near_first:
            self.push(self.src, p.f, p.a_peer(j))
        for j in near_first:
            self.push(self.src, p.f, p.b_peer(j))
        self.push(self.src, p.f, p.partner)
        self.own.start()

    def relay(self):
        p = self.place
        for j in near_first:
            origin = p.a_peer(j)
            block = self.arrive(origin)
            for i in near_first:
                self.push(block, origin, p.b_peer(i))
            self.push(block, origin, p.partner)

    def finish(self):
        p = self.place
        for j in (0,) + near_first:
            for i in near_first:
                origin = p.at((p.b + i) % 4, (p.a + j) % 4, p.c)
                self.push(self.arrive(origin), origin, p.partner)
        for j in (0,) + near_first:
            for i in (0,) + near_first:
                z, y = (p.z + i) % 4, (p.y + j) % 4
                self.arrive((z * 4 + y) * 2 + 1 - p.c)
        self.own.wait()
        for copy in self.sent:
            copy.wait_send()


class PlaneScatter:
    def __init__(self, place, src, view, scratch):
        self.place, self.src, self.view = place, src, view
        (self.got1, self.sum1, self.got2, self.sum2, self.got3, self.send1, self.recv1,
         self.send2, self.recv2, self.send3, self.recv3) = scratch

    @staticmethod
    def scratch(block, dtype=jnp.bfloat16):
        wide = lambda *lead: pltpu.VMEM(lead + block, dtype)
        return [wide(16), wide(4, 4), wide(4, 4), wide(4), wide(4), DMA((16,)), DMA((16,)),
                DMA((4,)), DMA((4,)), DMA((4,)), DMA((4,))]

    def start(self):
        p = self.place
        self.sent1 = []
        for i in (2, 1, 3, 0):
            for a in range(4):
                b = (p.a + i) % 4
                k = b * 4 + a
                copy = copy_to(
                    self.view(self.src, p.at(b, a, 1 - p.c)),
                    self.got1.at[k],
                    self.send1.at[k],
                    self.recv1.at[k],
                    p.x,
                    p.partner,
                )
                copy.start()
                self.sent1.append(copy)

    def middle(self):
        p = self.place
        sent2 = []
        for i in (2, 1, 3, 0):
            b = (p.b + i) % 4
            for a in range(4):
                k = b * 4 + a
                copy_to(
                    self.got1.at[k], self.got1.at[k], self.send1.at[k], self.recv1.at[k],
                    p.x, p.partner,
                ).wait_recv()
                own = self.view(self.src, p.at(b, a, p.c))[...].astype(jnp.float32)
                self.sum1[b, a] = (own + self.got1[k].astype(jnp.float32)).astype(self.sum1.dtype)
            if i:
                copy = copy_to(
                    self.sum1.at[b], self.got2.at[p.b], self.send2.at[i], self.recv2.at[p.b],
                    p.x, p.b_peer(i),
                )
                copy.start()
                sent2.append(copy)
        for i in near_first:
            b = (p.b + i) % 4
            copy_to(
                self.got2.at[b], self.got2.at[b], self.send2.at[i], self.recv2.at[b],
                p.x, p.b_peer(i),
            ).wait_recv()
        sent3 = []
        for j in (2, 1, 3, 0):
            a = (p.a + j) % 4
            total = self.sum1[p.b, a].astype(jnp.float32)
            for i in near_first:
                total += self.got2[(p.b + i) % 4, a].astype(jnp.float32)
            if j:
                self.sum2[a] = total.astype(self.sum2.dtype)
                copy = copy_to(
                    self.sum2.at[a], self.got3.at[p.a], self.send3.at[j], self.recv3.at[p.a],
                    p.x, p.a_peer(j),
                )
                copy.start()
                sent3.append(copy)
        for j in near_first:
            a = (p.a + j) % 4
            copy_to(
                self.got3.at[a], self.got3.at[a], self.send3.at[j], self.recv3.at[a],
                p.x, p.a_peer(j),
            ).wait_recv()
            total += self.got3[a].astype(jnp.float32)
        for copy in self.sent1 + sent2 + sent3:
            copy.wait_send()
        return total


def across_gather(place, src, out, send, recv):
    own = pltpu.make_async_copy(src, out.at[place.x], send.at[0])
    own.start()
    sent = []
    for j in near_first:
        copy = copy_to(src, out.at[place.x], send.at[j], recv.at[place.x], (place.x + j) % 4, place.f)
        copy.start()
        sent.append(copy)

    def finish():
        for j in near_first:
            x = (place.x + j) % 4
            copy_to(out.at[x], out.at[x], send.at[j], recv.at[x], x, place.f).wait_recv()
        own.wait()
        for copy in sent:
            copy.wait_send()

    return finish


def params(collective_id):
    return pltpu.CompilerParams(
        collective_id=collective_id, has_side_effects=True, vmem_limit_bytes=40 * 1024 * 1024
    )


def column_block(ref, f):
    return ref.at[:, pl.ds(pl.multiple_of(f * 128, 128), 128)]


def row_block(ref, f):
    return ref.at[f]


def gather_input(mlp_input):
    def kernel(src, out, send, recv):
        place = Place()
        meet(place, False)
        gather = PlaneGather(place, src, out, column_block, send, recv)
        gather.start()
        gather.relay()
        gather.finish()

    rows, cols = mlp_input.shape
    return pl.pallas_call(
        kernel,
        out_shape=jax.ShapeDtypeStruct((rows, cols * 32), jnp.bfloat16),
        in_specs=[ANY],
        out_specs=ANY,
        scratch_shapes=[DMA((32,)), DMA((32,))],
        compiler_params=params(0),
        name="gather_input",
    )(mlp_input)


def scatter_branch(partial):
    def kernel(src, out, *scratch):
        place = Place()
        meet(place, False)
        scatter = PlaneScatter(place, src, row_block, scratch)
        scatter.start()
        out[...] = scatter.middle()

    return pl.pallas_call(
        kernel,
        out_shape=jax.ShapeDtypeStruct((8, 4096), jnp.float32),
        in_specs=[VMEM],
        out_specs=VMEM,
        scratch_shapes=PlaneScatter.scratch((8, 4096)),
        compiler_params=params(1),
        name="scatter_branch",
    )(partial.reshape(32, 8, 4096))


def gather_queries(unit_rows, hidden, whole_input):
    def kernel(unit, hid, inp, out, unit_x, hid_x, inp_x, send, recv, u_send, u_recv,
               h_send, h_recv, i_send, i_recv, pair_send, pair_recv):
        place = Place()
        p = place
        meet(place, True)
        finish_unit = across_gather(place, unit, unit_x, u_send, u_recv)
        finish_unit()
        gather = PlaneGather(place, unit_x, out, row_block, send, recv)
        gather.start()
        half = lambda c: pl.ds(pl.multiple_of(c * 512, 512), 512)
        own_i = pltpu.make_async_copy(
            inp.at[:, pl.ds(pl.multiple_of(p.x * 1024, 1024), 1024)], inp_x.at[p.x], i_send.at[0]
        )
        own_i.start()
        sent = []
        finish_hidden = across_gather(place, hid, hid_x, h_send, h_recv)
        for j in near_first:
            x = (p.x + j) % 4
            copy = copy_to(
                inp.at[:, pl.ds(pl.multiple_of(x * 1024 + p.c * 512, 512), 512)],
                inp_x.at[p.x, :, half(p.c)], i_send.at[j], i_recv.at[p.x], x, p.f,
            )
            copy.start()
            sent.append(copy)
        gather.relay()
        gather.finish()
        for j in near_first:
            x = (p.x + j) % 4
            region = inp_x.at[x, :, half(p.c)]
            copy_to(region, region, i_send.at[j], i_recv.at[x], x, p.f).wait_recv()
            copy = copy_to(region, region, pair_send.at[j], pair_recv.at[x], p.x, p.partner)
            copy.start()
            sent.append(copy)
        for j in near_first:
            x = (p.x + j) % 4
            region = inp_x.at[x, :, half(1 - p.c)]
            copy_to(region, region, pair_send.at[j], pair_recv.at[x], p.x, p.partner).wait_recv()
        finish_hidden()
        own_i.wait()
        for copy in sent:
            copy.wait_send()

    bf = lambda *shape: jax.ShapeDtypeStruct(shape, jnp.bfloat16)
    out, _, hid_x, inp_x = pl.pallas_call(
        kernel,
        out_shape=(bf(32, 4, 8, 4096), bf(4, 8, 4096), bf(4, *hidden.shape), bf(4, 256, 1024)),
        in_specs=[ANY] * 3,
        out_specs=[ANY] * 4,
        scratch_shapes=[DMA((32,)), DMA((32,))] + [DMA((4,))] * 8,
        compiler_params=params(4),
        name="gather_queries",
    )(unit_rows, hidden, whole_input)
    return out.reshape(1024, 4096), hid_x, inp_x


def across_sum(place, total, stage, got, send, recv):
    stage[...] = total.astype(stage.dtype)
    sent = []
    for j in near_first:
        x = (place.x + j) % 4
        copy = copy_to(stage.at[x], got.at[place.x], send.at[j], recv.at[place.x], x, place.f)
        copy.start()
        sent.append(copy)

    def finish():
        own = stage[place.x].astype(jnp.float32)
        for j in near_first:
            x = (place.x + j) % 4
            copy_to(got.at[x], got.at[x], send.at[j], recv.at[x], x, place.f).wait_recv()
            own += got[x].astype(jnp.float32)
        for copy in sent:
            copy.wait_send()
        return own

    return finish


def scatter_pull(pull, sums):
    n = 11

    def kernel(pull_ref, sums_ref, pull_out, sums_out, stage_p, got_p, sp, rp, stage_s, got_s, ss,
               rs, *scratch):
        place = Place()
        meet(place, True)
        first = PlaneScatter(place, pull_ref, row_block, scratch[:n])
        second = PlaneScatter(place, sums_ref, row_block, scratch[n:])
        first.start()
        second.start()
        finish_p = across_sum(place, first.middle(), stage_p, got_p, sp, rp)
        finish_s = across_sum(place, second.middle(), stage_s, got_s, ss, rs)
        pull_out[...] = finish_p()
        sums_out[...] = finish_s()

    return pl.pallas_call(
        kernel,
        out_shape=(
            jax.ShapeDtypeStruct((8, 4096), jnp.float32),
            jax.ShapeDtypeStruct((8, 128), jnp.float32),
        ),
        in_specs=[VMEM, VMEM],
        out_specs=[VMEM, VMEM],
        scratch_shapes=[
            pltpu.VMEM((4, 8, 4096), jnp.bfloat16), pltpu.VMEM((4, 8, 4096), jnp.bfloat16),
            DMA((4,)), DMA((4,)),
            pltpu.VMEM((4, 8, 128), jnp.float32), pltpu.VMEM((4, 8, 128), jnp.float32),
            DMA((4,)), DMA((4,)),
        ]
        + PlaneScatter.scratch((4, 8, 4096))
        + PlaneScatter.scratch((4, 8, 128), jnp.float32),
        compiler_params=params(5),
        name="scatter_pull",
    )(pull, sums)


def gather_head(head_grad):
    def kernel(head, out, head_x, send, recv, hx_send, hx_recv):
        place = Place()
        p = place
        meet(place, True)
        gather = PlaneGather(place, head, out, row_block, send, recv)
        gather.start()
        wide = lambda x: pl.ds(pl.multiple_of(x * 1024, 1024), 1024)
        own = pltpu.make_async_copy(head.at[:, wide(p.x)], head_x.at[p.x], hx_send.at[0])
        own.start()
        sent = []
        for j in near_first:
            x = (p.x + j) % 4
            copy = copy_to(head.at[:, wide(x)], head_x.at[p.x], hx_send.at[j], hx_recv.at[p.x], x, p.f)
            copy.start()
            sent.append(copy)
        gather.relay()
        gather.finish()
        for j in near_first:
            x = (p.x + j) % 4
            copy_to(
                head_x.at[x], head_x.at[x], hx_send.at[j], hx_recv.at[x], x, p.f
            ).wait_recv()
        own.wait()
        for copy in sent:
            copy.wait_send()

    bf = lambda *shape: jax.ShapeDtypeStruct(shape, jnp.bfloat16)
    out, head_x = pl.pallas_call(
        kernel,
        out_shape=(bf(32, 8, 4096), bf(4, 8, 1024)),
        in_specs=[ANY],
        out_specs=[ANY] * 2,
        scratch_shapes=[DMA((32,)), DMA((32,)), DMA((4,)), DMA((4,))],
        compiler_params=params(2),
        name="gather_head",
    )(head_grad)
    return out.reshape(256, 4096), head_x


def finish_links(partial, acts, head_x):
    def kernel(src, act, hx, out, act_x, head_cols, send, recv, x_send, x_recv, *scratch):
        place = Place()
        meet(place, True)
        finish_acts = across_gather(place, act, act_x, x_send, x_recv)
        scatter = PlaneScatter(place, src, column_block, scratch)
        scatter.start()
        gather = PlaneGather(
            place, hx, head_cols, lambda ref, f: ref.at[:, f], send, recv
        )
        gather.start()
        gather.relay()
        out[...] = scatter.middle().astype(jnp.bfloat16)
        gather.finish()
        finish_acts()

    bf = lambda *shape: jax.ShapeDtypeStruct(shape, jnp.bfloat16)
    return pl.pallas_call(
        kernel,
        out_shape=(bf(256, 128), bf(4, *acts.shape), bf(4, 32, 8, 1024)),
        in_specs=[VMEM, ANY, ANY],
        out_specs=[VMEM, ANY, ANY],
        scratch_shapes=[DMA((32,)), DMA((32,)), DMA((4,)), DMA((4,))]
        + PlaneScatter.scratch((256, 128)),
        compiler_params=params(3),
        name="finish_links",
    )(partial, acts, head_x)


def owner_sums(unit_rows, span_index, codes):
    shard_rows = span_index.shape[0]
    wide = span_index.astype(jnp.float32)
    key_scale = lax.rsqrt(jnp.sum(wide * wide, axis=-1) + eps)
    raw = lax.dot_general(
        unit_rows, span_index, contract_last, preferred_element_type=jnp.float32
    )
    scores = inverse_temp * raw * key_scale[None, :]
    groups, slots = codes.shape
    queries = unit_rows.shape[0] // groups
    here = lax.broadcasted_iota(jnp.int32, (groups, queries, shard_rows), 2)
    here += shard_rows * lax.broadcasted_iota(jnp.int32, (groups, queries, shard_rows), 1)
    uses = jnp.zeros(here.shape, jnp.float32)
    for slot in range(slots):
        uses += (codes[:, slot][:, None, None] == here).astype(jnp.float32)
    uses = uses.reshape(raw.shape)
    weights = uses * jnp.exp(scores)
    pull = jnp.dot(
        (weights * key_scale[None, :]).astype(jnp.bfloat16),
        span_index,
        preferred_element_type=jnp.bfloat16,
    )
    return pull, jnp.sum(weights, axis=-1), jnp.sum(weights * scores, axis=-1)


def shards(
    mlp_input,
    residual_in,
    gate_weight,
    up_weight,
    down_weight,
    span_index,
    positive_keys,
    request_rows,
    request_counts,
    negative_slots,
):
    dp_count = lax.axis_size("dp")
    fsdp_count = lax.axis_size("fsdp")
    owners = dp_count * fsdp_count
    slot_cap = request_rows.shape[2]
    rows, width = positive_keys.shape

    slot_ids = lax.broadcasted_iota(jnp.int32, (1, 1, owners * slot_cap), 2)
    used = jnp.any(negative_slots[:, :, None] == slot_ids, axis=1).astype(jnp.int32)
    ranks = lax.broadcasted_iota(jnp.int32, used.shape, 0) + 1
    user = (jnp.sum(used * ranks, axis=0) - 1).reshape(owners, slot_cap)
    user = lax.all_to_all(user, ("dp", "fsdp"), split_axis=0, concat_axis=0, tiled=True)
    row_table = request_rows[:, 0, :]
    live = lax.broadcasted_iota(jnp.int32, row_table.shape, 1) < request_counts
    codes = jnp.where(live & (user >= 0), row_table + span_index.shape[0] * user, -1)
    codes = codes.reshape(dp_count, fsdp_count, slot_cap).transpose(1, 0, 2)
    codes = codes.reshape(owners, slot_cap)

    whole_input = gather_input(mlp_input)
    gate_act = jnp.dot(whole_input, gate_weight, preferred_element_type=jnp.float32)
    up_act = jnp.dot(whole_input, up_weight, preferred_element_type=jnp.float32)
    sigmoid_gate = jax.nn.sigmoid(gate_act)
    silu_gate = gate_act * sigmoid_gate
    hidden = (silu_gate * up_act).astype(jnp.bfloat16)
    branch = scatter_branch(jnp.dot(hidden, down_weight, preferred_element_type=jnp.bfloat16))
    top_state = branch + residual_in.astype(jnp.float32)
    row_norm = jnp.sqrt(jnp.sum(top_state * top_state, axis=-1) + eps)
    unit_rows = top_state / row_norm[:, None]
    positive = positive_keys.astype(jnp.float32)
    positive_unit = positive / jnp.sqrt(jnp.sum(positive * positive, axis=-1, keepdims=True) + eps)
    positive_score = inverse_temp * jnp.sum(unit_rows * positive_unit, axis=-1)

    all_units, hidden_x, input_x = gather_queries(
        unit_rows.astype(jnp.bfloat16), hidden.T, whole_input
    )
    pull, exps, inners = owner_sums(all_units, span_index, codes)
    lanes = lax.broadcasted_iota(jnp.int32, (exps.shape[0], 128), 1)
    sums = jnp.where(lanes == 0, exps[:, None], jnp.where(lanes == 1, inners[:, None], 0.0))
    pull, sums = scatter_pull(
        pull.reshape(fsdp_count, dp_count, rows, width),
        sums.reshape(fsdp_count, dp_count, rows, 128),
    )
    positive_weight = jnp.exp(positive_score)
    exp_total = sums[:, 0] + positive_weight
    query_loss = jnp.log(exp_total) - positive_score
    positive_coeff = positive_weight / exp_total - 1.0
    inner = sums[:, 1] / exp_total + positive_coeff * positive_score
    pull = inverse_temp * (pull / exp_total[:, None] + positive_coeff[:, None] * positive_unit)
    head_grad = ((pull - inner[:, None] * unit_rows) / row_norm[:, None]).astype(jnp.bfloat16)

    gathered_grad, head_x = gather_head(head_grad)
    hidden_grad = lax.dot_general(
        gathered_grad, down_weight, contract_last, preferred_element_type=jnp.float32
    )
    silu_slope = sigmoid_gate * (1.0 + gate_act * (1.0 - sigmoid_gate))
    gate_grad_act = (hidden_grad * up_act * silu_slope).astype(jnp.bfloat16)
    up_grad_act = (hidden_grad * silu_gate).astype(jnp.bfloat16)
    input_term = lax.dot_general(
        gate_grad_act, gate_weight, contract_last, preferred_element_type=jnp.float32
    ) + lax.dot_general(up_grad_act, up_weight, contract_last, preferred_element_type=jnp.float32)
    input_grad, acts_x, head_cols = finish_links(
        input_term.astype(jnp.bfloat16),
        jnp.concatenate([gate_grad_act.T, up_grad_act.T], axis=0),
        head_x,
    )
    units = gate_weight.shape[1]
    over_groups = (((0, 2), (0, 1)), ((), ()))
    down_grad = lax.dot_general(
        hidden_x, head_cols.reshape(4, 256, 1024), over_groups, preferred_element_type=jnp.float32
    ).astype(jnp.bfloat16)
    both = lax.dot_general(
        acts_x, input_x, over_groups, preferred_element_type=jnp.float32
    ).astype(jnp.bfloat16)
    return (query_loss, input_grad, both[:units].T, both[units:].T, down_grad)


def solution(mesh):
    return jax.shard_map(
        shards,
        mesh=mesh,
        in_specs=(
            P("dp", "fsdp"),
            P(("dp", "fsdp"), None),
            P(None, "fsdp"),
            P(None, "fsdp"),
            P("fsdp", None),
            P(("dp", "fsdp"), None),
            P(("dp", "fsdp"), None),
            P(None, ("dp", "fsdp"), None),
            P(None, ("dp", "fsdp")),
            P(("dp", "fsdp"), None),
        ),
        out_specs=(
            P(("dp", "fsdp")),
            P("dp", "fsdp"),
            P("dp", "fsdp"),
            P("dp", "fsdp"),
            P("fsdp", "dp"),
        ),
        check_vma=False,
    )
```

```python
import functools

import jax
import jax.numpy as jnp
from jax import lax
from jax.experimental import pallas as pl
from jax.experimental.pallas import tpu as pltpu
from jax.sharding import PartitionSpec as P

inverse_temp = 50.0
eps = 1e-06
contract_first = (((0,), (0,)), ((), ()))
contract_last = (((1,), (1,)), ((), ()))
ANY = pl.BlockSpec(memory_space=pl.ANY)
VMEM = pl.BlockSpec(memory_space=pltpu.VMEM)
DMA = pltpu.SemaphoreType.DMA
near_first = (1, 3, 2)


class Place:
    def __init__(self):
        self.x = lax.axis_index("dp")
        self.f = lax.axis_index("fsdp")
        self.z = self.f // 8
        self.y = (self.f // 2) % 4
        self.c = self.f % 2
        self.a = self.y * (1 - self.c) + self.z * self.c
        self.b = self.z * (1 - self.c) + self.y * self.c
        self.partner = self.f + 1 - 2 * self.c

    def at(self, b, a, c):
        z = b * (1 - c) + a * c
        y = a * (1 - c) + b * c
        return (z * 4 + y) * 2 + c

    def a_peer(self, j):
        return self.at(self.b, (self.a + j) % 4, self.c)

    def b_peer(self, j):
        return self.at((self.b + j) % 4, self.a, self.c)


def copy_to(src, dst, send, recv, x, f):
    return pltpu.make_async_remote_copy(
        src_ref=src,
        dst_ref=dst,
        send_sem=send,
        recv_sem=recv,
        device_id=(x, f),
        device_id_type=pl.DeviceIdType.MESH,
    )


def meet(place, across):
    barrier = pltpu.get_barrier_semaphore()
    peers = [(place.x, place.partner)]
    peers += [(place.x, place.a_peer(j)) for j in near_first]
    peers += [(place.x, place.b_peer(j)) for j in near_first]
    if across:
        peers += [((place.x + j) % 4, place.f) for j in near_first]
    for x, f in peers:
        pl.semaphore_signal(barrier, inc=1, device_id=(x, f), device_id_type=pl.DeviceIdType.MESH)
    pl.semaphore_wait(barrier, len(peers))


class PlaneGather:
    copies = 32

    def __init__(self, place, src, out, view, send, recv):
        self.place, self.src, self.out, self.view = place, src, out, view
        self.send, self.recv = send, recv
        self.sent = []

    def push(self, ref, origin, f):
        copy = copy_to(
            ref,
            self.view(self.out, origin),
            self.send.at[len(self.sent)],
            self.recv.at[origin],
            self.place.x,
            f,
        )
        copy.start()
        self.sent.append(copy)

    def arrive(self, origin):
        block = self.view(self.out, origin)
        copy_to(
            block, block, self.send.at[31], self.recv.at[origin], self.place.x, self.place.partner
        ).wait_recv()
        return block

    def start(self):
        p = self.place
        self.own = pltpu.make_async_copy(self.src, self.view(self.out, p.f), self.send.at[31])
        for j in near_first:
            self.push(self.src, p.f, p.a_peer(j))
        for j in near_first:
            self.push(self.src, p.f, p.b_peer(j))
        self.push(self.src, p.f, p.partner)
        self.own.start()

    def relay(self):
        p = self.place
        for j in near_first:
            origin = p.a_peer(j)
            block = self.arrive(origin)
            for i in near_first:
                self.push(block, origin, p.b_peer(i))
            self.push(block, origin, p.partner)

    def finish(self):
        p = self.place
        for j in (0,) + near_first:
            for i in near_first:
                origin = p.at((p.b + i) % 4, (p.a + j) % 4, p.c)
                self.push(self.arrive(origin), origin, p.partner)
        for j in (0,) + near_first:
            for i in (0,) + near_first:
                z, y = (p.z + i) % 4, (p.y + j) % 4
                self.arrive((z * 4 + y) * 2 + 1 - p.c)
        self.own.wait()
        for copy in self.sent:
            copy.wait_send()


class PlaneScatter:
    def __init__(self, place, src, view, scratch):
        self.place, self.src, self.view = place, src, view
        (self.got1, self.sum1, self.got2, self.sum2, self.got3, self.send1, self.recv1,
         self.send2, self.recv2, self.send3, self.recv3) = scratch

    @staticmethod
    def scratch(block, dtype=jnp.bfloat16):
        wide = lambda *lead: pltpu.VMEM(lead + block, dtype)
        return [wide(16), wide(4, 4), wide(4, 4), wide(4), wide(4), DMA((16,)), DMA((16,)),
                DMA((4,)), DMA((4,)), DMA((4,)), DMA((4,))]

    def start(self):
        p = self.place
        self.sent1 = []
        for i in (2, 1, 3, 0):
            for a in range(4):
                b = (p.a + i) % 4
                k = b * 4 + a
                copy = copy_to(
                    self.view(self.src, p.at(b, a, 1 - p.c)),
                    self.got1.at[k],
                    self.send1.at[k],
                    self.recv1.at[k],
                    p.x,
                    p.partner,
                )
                copy.start()
                self.sent1.append(copy)

    def middle(self):
        p = self.place
        sent2 = []
        for i in (2, 1, 3, 0):
            b = (p.b + i) % 4
            for a in range(4):
                k = b * 4 + a
                copy_to(
                    self.got1.at[k], self.got1.at[k], self.send1.at[k], self.recv1.at[k],
                    p.x, p.partner,
                ).wait_recv()
                own = self.view(self.src, p.at(b, a, p.c))[...].astype(jnp.float32)
                self.sum1[b, a] = (own + self.got1[k].astype(jnp.float32)).astype(self.sum1.dtype)
            if i:
                copy = copy_to(
                    self.sum1.at[b], self.got2.at[p.b], self.send2.at[i], self.recv2.at[p.b],
                    p.x, p.b_peer(i),
                )
                copy.start()
                sent2.append(copy)
        for i in near_first:
            b = (p.b + i) % 4
            copy_to(
                self.got2.at[b], self.got2.at[b], self.send2.at[i], self.recv2.at[b],
                p.x, p.b_peer(i),
            ).wait_recv()
        sent3 = []
        for j in (2, 1, 3, 0):
            a = (p.a + j) % 4
            total = self.sum1[p.b, a].astype(jnp.float32)
            for i in near_first:
                total += self.got2[(p.b + i) % 4, a].astype(jnp.float32)
            if j:
                self.sum2[a] = total.astype(self.sum2.dtype)
                copy = copy_to(
                    self.sum2.at[a], self.got3.at[p.a], self.send3.at[j], self.recv3.at[p.a],
                    p.x, p.a_peer(j),
                )
                copy.start()
                sent3.append(copy)
        for j in near_first:
            a = (p.a + j) % 4
            copy_to(
                self.got3.at[a], self.got3.at[a], self.send3.at[j], self.recv3.at[a],
                p.x, p.a_peer(j),
            ).wait_recv()
            total += self.got3[a].astype(jnp.float32)
        for copy in self.sent1 + sent2 + sent3:
            copy.wait_send()
        return total


def across_gather(place, src, out, send, recv):
    own = pltpu.make_async_copy(src, out.at[place.x], send.at[0])
    own.start()
    sent = []
    for j in near_first:
        copy = copy_to(src, out.at[place.x], send.at[j], recv.at[place.x], (place.x + j) % 4, place.f)
        copy.start()
        sent.append(copy)

    def finish():
        for j in near_first:
            x = (place.x + j) % 4
            copy_to(out.at[x], out.at[x], send.at[j], recv.at[x], x, place.f).wait_recv()
        own.wait()
        for copy in sent:
            copy.wait_send()

    return finish


def params(collective_id, mib):
    return pltpu.CompilerParams(
        collective_id=collective_id, has_side_effects=True, vmem_limit_bytes=mib * 1024 * 1024
    )


def column_block(ref, f):
    return ref.at[:, pl.ds(pl.multiple_of(f * 128, 128), 128)]


def row_block(ref, f):
    return ref.at[f]


def gather_input(mlp_input, table):
    def kernel(src, tab, out, tab_x, tab_all, send, recv, x_send, x_recv, t_send, t_recv):
        place = Place()
        meet(place, True)
        finish_table = across_gather(place, tab, tab_x, x_send, x_recv)
        gather = PlaneGather(place, src, out, column_block, send, recv)
        gather.start()
        finish_table()
        tables = PlaneGather(place, tab_x, tab_all, row_block, t_send, t_recv)
        tables.start()
        gather.relay()
        tables.relay()
        gather.finish()
        tables.finish()

    rows, cols = mlp_input.shape
    ints = lambda *lead: jax.ShapeDtypeStruct(lead + table.shape, jnp.int32)
    out, _, tables = pl.pallas_call(
        kernel,
        out_shape=(jax.ShapeDtypeStruct((rows, cols * 32), jnp.bfloat16), ints(4), ints(32, 4)),
        in_specs=[ANY] * 2,
        out_specs=[ANY] * 3,
        scratch_shapes=[DMA((32,)), DMA((32,)), DMA((4,)), DMA((4,)), DMA((32,)), DMA((32,))],
        compiler_params=params(0, 4),
        name="gather_input",
    )(mlp_input, table)
    return out, tables


def scatter_branch(partial):
    def kernel(src, out, *scratch):
        place = Place()
        meet(place, False)
        scatter = PlaneScatter(place, src, row_block, scratch)
        scatter.start()
        out[...] = scatter.middle()

    return pl.pallas_call(
        kernel,
        out_shape=jax.ShapeDtypeStruct((8, 4096), jnp.float32),
        in_specs=[VMEM],
        out_specs=VMEM,
        scratch_shapes=PlaneScatter.scratch((8, 4096)),
        compiler_params=params(1, 12),
        name="scatter_branch",
    )(partial.reshape(32, 8, 4096))


def gather_queries(unit_rows, hidden, whole_input):
    def kernel(unit, hid, inp, out, unit_x, hid_x, inp_x, send, recv, u_send, u_recv,
               h_send, h_recv, i_send, i_recv, pair_send, pair_recv):
        place = Place()
        p = place
        meet(place, True)
        finish_unit = across_gather(place, unit, unit_x, u_send, u_recv)
        finish_unit()
        gather = PlaneGather(place, unit_x, out, row_block, send, recv)
        gather.start()
        half = lambda c: pl.ds(pl.multiple_of(c * 512, 512), 512)
        own_i = pltpu.make_async_copy(
            inp.at[:, pl.ds(pl.multiple_of(p.x * 1024, 1024), 1024)], inp_x.at[p.x], i_send.at[0]
        )
        own_i.start()
        sent = []
        finish_hidden = across_gather(place, hid, hid_x, h_send, h_recv)
        for j in near_first:
            x = (p.x + j) % 4
            copy = copy_to(
                inp.at[:, pl.ds(pl.multiple_of(x * 1024 + p.c * 512, 512), 512)],
                inp_x.at[p.x, :, half(p.c)], i_send.at[j], i_recv.at[p.x], x, p.f,
            )
            copy.start()
            sent.append(copy)
        gather.relay()
        gather.finish()
        for j in near_first:
            x = (p.x + j) % 4
            region = inp_x.at[x, :, half(p.c)]
            copy_to(region, region, i_send.at[j], i_recv.at[x], x, p.f).wait_recv()
            copy = copy_to(region, region, pair_send.at[j], pair_recv.at[x], p.x, p.partner)
            copy.start()
            sent.append(copy)
        for j in near_first:
            x = (p.x + j) % 4
            region = inp_x.at[x, :, half(1 - p.c)]
            copy_to(region, region, pair_send.at[j], pair_recv.at[x], p.x, p.partner).wait_recv()
        finish_hidden()
        own_i.wait()
        for copy in sent:
            copy.wait_send()

    bf = lambda *shape: jax.ShapeDtypeStruct(shape, jnp.bfloat16)
    out, _, hid_x, inp_x = pl.pallas_call(
        kernel,
        out_shape=(bf(32, 4, 8, 4096), bf(4, 8, 4096), bf(4, *hidden.shape), bf(4, 256, 1024)),
        in_specs=[ANY] * 3,
        out_specs=[ANY] * 4,
        scratch_shapes=[DMA((32,)), DMA((32,))] + [DMA((4,))] * 8,
        compiler_params=params(4, 4),
        name="gather_queries",
    )(unit_rows, hidden, whole_input)
    return out.reshape(1024, 4096), hid_x, inp_x


def across_sum(place, total, stage, got, send, recv):
    stage[...] = total.astype(stage.dtype)
    sent = []
    for j in near_first:
        x = (place.x + j) % 4
        copy = copy_to(stage.at[x], got.at[place.x], send.at[j], recv.at[place.x], x, place.f)
        copy.start()
        sent.append(copy)

    def finish():
        own = stage[place.x].astype(jnp.float32)
        for j in near_first:
            x = (place.x + j) % 4
            copy_to(got.at[x], got.at[x], send.at[j], recv.at[x], x, place.f).wait_recv()
            own += got[x].astype(jnp.float32)
        for copy in sent:
            copy.wait_send()
        return own

    return finish


def scatter_pull(pull, sums, factors):
    n = 11

    def kernel(pull_ref, sums_ref, fac, pull_out, sums_out, fac_x, f_send, f_recv,
               stage_p, got_p, sp, rp, stage_s, got_s, ss, rs, *scratch):
        place = Place()
        meet(place, True)
        finish_factors = across_gather(place, fac, fac_x, f_send, f_recv)
        first = PlaneScatter(place, pull_ref, row_block, scratch[:n])
        second = PlaneScatter(place, sums_ref, row_block, scratch[n:])
        first.start()
        second.start()
        finish_p = across_sum(place, first.middle(), stage_p, got_p, sp, rp)
        finish_s = across_sum(place, second.middle(), stage_s, got_s, ss, rs)
        pull_out[...] = finish_p()
        sums_out[...] = finish_s()
        finish_factors()

    return pl.pallas_call(
        kernel,
        out_shape=(
            jax.ShapeDtypeStruct((8, 4096), jnp.float32),
            jax.ShapeDtypeStruct((8, 128), jnp.float32),
            jax.ShapeDtypeStruct((4,) + factors.shape, jnp.bfloat16),
        ),
        in_specs=[VMEM, VMEM, ANY],
        out_specs=[VMEM, VMEM, ANY],
        scratch_shapes=[
            DMA((4,)), DMA((4,)),
            pltpu.VMEM((4, 8, 4096), jnp.bfloat16), pltpu.VMEM((4, 8, 4096), jnp.bfloat16),
            DMA((4,)), DMA((4,)),
            pltpu.VMEM((4, 8, 128), jnp.float32), pltpu.VMEM((4, 8, 128), jnp.float32),
            DMA((4,)), DMA((4,)),
        ]
        + PlaneScatter.scratch((4, 8, 4096))
        + PlaneScatter.scratch((4, 8, 128), jnp.float32),
        compiler_params=params(5, 20),
        name="scatter_pull",
    )(pull, sums, factors)


def gather_head(head_grad):
    def kernel(head, out, head_x, send, recv, hx_send, hx_recv):
        place = Place()
        p = place
        meet(place, True)
        gather = PlaneGather(place, head, out, row_block, send, recv)
        gather.start()
        wide = lambda x: pl.ds(pl.multiple_of(x * 1024, 1024), 1024)
        own = pltpu.make_async_copy(head.at[:, wide(p.x)], head_x.at[p.x], hx_send.at[0])
        own.start()
        sent = []
        for j in near_first:
            x = (p.x + j) % 4
            copy = copy_to(head.at[:, wide(x)], head_x.at[p.x], hx_send.at[j], hx_recv.at[p.x], x, p.f)
            copy.start()
            sent.append(copy)
        gather.relay()
        gather.finish()
        for j in near_first:
            x = (p.x + j) % 4
            copy_to(
                head_x.at[x], head_x.at[x], hx_send.at[j], hx_recv.at[x], x, p.f
            ).wait_recv()
        own.wait()
        for copy in sent:
            copy.wait_send()

    bf = lambda *shape: jax.ShapeDtypeStruct(shape, jnp.bfloat16)
    out, head_x = pl.pallas_call(
        kernel,
        out_shape=(bf(32, 8, 4096), bf(4, 8, 1024)),
        in_specs=[ANY],
        out_specs=[ANY] * 2,
        scratch_shapes=[DMA((32,)), DMA((32,)), DMA((4,)), DMA((4,))],
        compiler_params=params(2, 4),
        name="gather_head",
    )(head_grad)
    return out.reshape(256, 4096), head_x


def finish_links(partial, acts, head_x):
    def kernel(src, act, hx, out, act_x, head_cols, send, recv, x_send, x_recv, *scratch):
        place = Place()
        meet(place, True)
        finish_acts = across_gather(place, act, act_x, x_send, x_recv)
        scatter = PlaneScatter(place, src, column_block, scratch)
        scatter.start()
        gather = PlaneGather(
            place, hx, head_cols, lambda ref, f: ref.at[:, f], send, recv
        )
        gather.start()
        gather.relay()
        out[...] = scatter.middle().astype(jnp.bfloat16)
        gather.finish()
        finish_acts()

    bf = lambda *shape: jax.ShapeDtypeStruct(shape, jnp.bfloat16)
    return pl.pallas_call(
        kernel,
        out_shape=(bf(256, 128), bf(4, *acts.shape), bf(4, 32, 8, 1024)),
        in_specs=[VMEM, ANY, ANY],
        out_specs=[VMEM, ANY, ANY],
        scratch_shapes=[DMA((32,)), DMA((32,)), DMA((4,)), DMA((4,))]
        + PlaneScatter.scratch((256, 128)),
        compiler_params=params(3, 12),
        name="finish_links",
    )(partial, acts, head_x)


def owner_sums(unit_rows, span_index, codes):
    shard_rows = span_index.shape[0]
    wide = span_index.astype(jnp.float32)
    key_scale = lax.rsqrt(jnp.sum(wide * wide, axis=-1) + eps)
    raw = lax.dot_general(
        unit_rows, span_index, contract_last, preferred_element_type=jnp.float32
    )
    scores = inverse_temp * raw * key_scale[None, :]
    groups, slots = codes.shape
    queries = unit_rows.shape[0] // groups
    here = lax.broadcasted_iota(jnp.int32, (groups, queries, shard_rows), 2)
    here += shard_rows * lax.broadcasted_iota(jnp.int32, (groups, queries, shard_rows), 1)
    uses = jnp.zeros(here.shape, jnp.float32)
    for slot in range(slots):
        uses += (codes[:, slot][:, None, None] == here).astype(jnp.float32)
    uses = uses.reshape(raw.shape)
    weights = uses * jnp.exp(scores)
    pull = jnp.dot(
        (weights * key_scale[None, :]).astype(jnp.bfloat16),
        span_index,
        preferred_element_type=jnp.bfloat16,
    )
    return pull, jnp.sum(weights, axis=-1), jnp.sum(weights * scores, axis=-1)


def shards(
    mlp_input,
    residual_in,
    gate_weight,
    up_weight,
    down_weight,
    span_index,
    positive_keys,
    request_rows,
    request_counts,
    negative_slots,
):
    dp_count = lax.axis_size("dp")
    fsdp_count = lax.axis_size("fsdp")
    owners = dp_count * fsdp_count
    slot_cap = request_rows.shape[2]
    rows, width = positive_keys.shape

    shape = (1, 1, slot_cap, owners)
    slot_ids = lax.broadcasted_iota(jnp.int32, shape, 3) * slot_cap
    slot_ids += lax.broadcasted_iota(jnp.int32, shape, 2)
    used = jnp.any(negative_slots[:, :, None, None] == slot_ids, axis=1).astype(jnp.int32)
    table = jnp.sum(used * (lax.broadcasted_iota(jnp.int32, used.shape, 0) + 1), axis=0) - 1
    whole_input, tables = gather_input(mlp_input, table)

    me = lax.axis_index("dp") * fsdp_count + lax.axis_index("fsdp")
    mine = lax.broadcasted_iota(jnp.int32, tables.shape, 3) == me
    user = jnp.sum(jnp.where(mine, tables, 0), axis=3).reshape(owners, slot_cap)
    requests = jnp.where(
        lax.broadcasted_iota(jnp.int32, (owners, slot_cap), 1) < request_counts,
        request_rows[:, 0, :],
        -1,
    )
    requests = requests.reshape(dp_count, fsdp_count, slot_cap).transpose(1, 0, 2)
    requests = requests.reshape(owners, slot_cap)
    codes = jnp.where(
        (requests >= 0) & (user >= 0), requests + span_index.shape[0] * user, -1
    )

    gate_act = jnp.dot(whole_input, gate_weight, preferred_element_type=jnp.float32)
    up_act = jnp.dot(whole_input, up_weight, preferred_element_type=jnp.float32)
    sigmoid_gate = jax.nn.sigmoid(gate_act)
    silu_gate = gate_act * sigmoid_gate
    hidden = (silu_gate * up_act).astype(jnp.bfloat16)
    branch = scatter_branch(jnp.dot(hidden, down_weight, preferred_element_type=jnp.bfloat16))
    top_state = branch + residual_in.astype(jnp.float32)
    row_norm = jnp.sqrt(jnp.sum(top_state * top_state, axis=-1) + eps)
    unit_rows = top_state / row_norm[:, None]
    positive = positive_keys.astype(jnp.float32)
    positive_unit = positive / jnp.sqrt(jnp.sum(positive * positive, axis=-1, keepdims=True) + eps)
    positive_score = inverse_temp * jnp.sum(unit_rows * positive_unit, axis=-1)

    all_units, hidden_x, input_x = gather_queries(
        unit_rows.astype(jnp.bfloat16), hidden.T, whole_input
    )
    pull, exps, inners = owner_sums(all_units, span_index, codes)
    lanes = lax.broadcasted_iota(jnp.int32, (exps.shape[0], 128), 1)
    sums = jnp.where(lanes == 0, exps[:, None], jnp.where(lanes == 1, inners[:, None], 0.0))
    gate_factor = up_act * (sigmoid_gate * (1.0 + gate_act * (1.0 - sigmoid_gate)))
    pull, sums, factors_x = scatter_pull(
        pull.reshape(fsdp_count, dp_count, rows, width),
        sums.reshape(fsdp_count, dp_count, rows, 128),
        jnp.stack([gate_factor.T, silu_gate.T]).astype(jnp.bfloat16),
    )
    positive_weight = jnp.exp(positive_score)
    exp_total = sums[:, 0] + positive_weight
    query_loss = jnp.log(exp_total) - positive_score
    positive_coeff = positive_weight / exp_total - 1.0
    inner = sums[:, 1] / exp_total + positive_coeff * positive_score
    pull = inverse_temp * (pull / exp_total[:, None] + positive_coeff[:, None] * positive_unit)
    head_grad = ((pull - inner[:, None] * unit_rows) / row_norm[:, None]).astype(jnp.bfloat16)

    gathered_grad, head_x = gather_head(head_grad)
    hidden_grad = lax.dot_general(
        gathered_grad, down_weight, contract_last, preferred_element_type=jnp.float32
    )
    gate_grad_act = (hidden_grad * gate_factor).astype(jnp.bfloat16)
    up_grad_act = (hidden_grad * silu_gate).astype(jnp.bfloat16)
    input_term = lax.dot_general(
        gate_grad_act, gate_weight, contract_last, preferred_element_type=jnp.float32
    ) + lax.dot_general(up_grad_act, up_weight, contract_last, preferred_element_type=jnp.float32)
    input_grad, hidden_grad_x, head_cols = finish_links(
        input_term.astype(jnp.bfloat16), hidden_grad.T.astype(jnp.bfloat16), head_x
    )
    over_groups = (((0, 2), (0, 1)), ((), ()))
    hidden_grad_x = hidden_grad_x.astype(jnp.float32)
    weight_grads = [
        lax.dot_general(
            (hidden_grad_x * factors_x[:, k].astype(jnp.float32)).astype(jnp.bfloat16),
            input_x,
            over_groups,
            preferred_element_type=jnp.float32,
        ).astype(jnp.bfloat16)
        for k in range(2)
    ]
    down_grad = lax.dot_general(
        hidden_x, head_cols.reshape(4, 256, 1024), over_groups, preferred_element_type=jnp.float32
    ).astype(jnp.bfloat16)
    return (query_loss, input_grad, weight_grads[0].T, weight_grads[1].T, down_grad)


def solution(mesh):
    return jax.shard_map(
        shards,
        mesh=mesh,
        in_specs=(
            P("dp", "fsdp"),
            P(("dp", "fsdp"), None),
            P(None, "fsdp"),
            P(None, "fsdp"),
            P("fsdp", None),
            P(("dp", "fsdp"), None),
            P(("dp", "fsdp"), None),
            P(None, ("dp", "fsdp"), None),
            P(None, ("dp", "fsdp")),
            P(("dp", "fsdp"), None),
        ),
        out_specs=(
            P(("dp", "fsdp")),
            P("dp", "fsdp"),
            P("dp", "fsdp"),
            P("dp", "fsdp"),
            P("fsdp", "dp"),
        ),
        check_vma=False,
    )
```

```python
import functools

import jax
import jax.numpy as jnp
from jax import lax
from jax.experimental import pallas as pl
from jax.experimental.pallas import tpu as pltpu
from jax.sharding import PartitionSpec as P

inverse_temp = 50.0
eps = 1e-06
contract_first = (((0,), (0,)), ((), ()))
contract_last = (((1,), (1,)), ((), ()))
ANY = pl.BlockSpec(memory_space=pl.ANY)
VMEM = pl.BlockSpec(memory_space=pltpu.VMEM)
DMA = pltpu.SemaphoreType.DMA
near_first = (1, 3, 2)


class Place:
    def __init__(self):
        self.x = lax.axis_index("dp")
        self.f = lax.axis_index("fsdp")
        self.z = self.f // 8
        self.y = (self.f // 2) % 4
        self.c = self.f % 2
        self.a = self.y * (1 - self.c) + self.z * self.c
        self.b = self.z * (1 - self.c) + self.y * self.c
        self.partner = self.f + 1 - 2 * self.c

    def at(self, b, a, c):
        z = b * (1 - c) + a * c
        y = a * (1 - c) + b * c
        return (z * 4 + y) * 2 + c

    def a_peer(self, j):
        return self.at(self.b, (self.a + j) % 4, self.c)

    def b_peer(self, j):
        return self.at((self.b + j) % 4, self.a, self.c)


def copy_to(src, dst, send, recv, x, f):
    return pltpu.make_async_remote_copy(
        src_ref=src,
        dst_ref=dst,
        send_sem=send,
        recv_sem=recv,
        device_id=(x, f),
        device_id_type=pl.DeviceIdType.MESH,
    )


def meet(place, across):
    barrier = pltpu.get_barrier_semaphore()
    peers = [(place.x, place.partner)]
    peers += [(place.x, place.a_peer(j)) for j in near_first]
    peers += [(place.x, place.b_peer(j)) for j in near_first]
    if across:
        peers += [((place.x + j) % 4, place.f) for j in near_first]
    for x, f in peers:
        pl.semaphore_signal(barrier, inc=1, device_id=(x, f), device_id_type=pl.DeviceIdType.MESH)
    pl.semaphore_wait(barrier, len(peers))


class PlaneGather:
    copies = 32

    def __init__(self, place, src, out, view, send, recv):
        self.place, self.src, self.out, self.view = place, src, out, view
        self.send, self.recv = send, recv
        self.sent = []

    def push(self, ref, origin, f):
        copy = copy_to(
            ref,
            self.view(self.out, origin),
            self.send.at[len(self.sent)],
            self.recv.at[origin],
            self.place.x,
            f,
        )
        copy.start()
        self.sent.append(copy)

    def arrive(self, origin):
        block = self.view(self.out, origin)
        copy_to(
            block, block, self.send.at[31], self.recv.at[origin], self.place.x, self.place.partner
        ).wait_recv()
        return block

    def start(self):
        p = self.place
        self.own = pltpu.make_async_copy(self.src, self.view(self.out, p.f), self.send.at[31])
        for j in near_first:
            self.push(self.src, p.f, p.a_peer(j))
        for j in near_first:
            self.push(self.src, p.f, p.b_peer(j))
        self.push(self.src, p.f, p.partner)
        self.own.start()

    def relay(self):
        p = self.place
        for j in near_first:
            origin = p.a_peer(j)
            block = self.arrive(origin)
            for i in near_first:
                self.push(block, origin, p.b_peer(i))
            self.push(block, origin, p.partner)

    def finish(self):
        p = self.place
        for j in (0,) + near_first:
            for i in near_first:
                origin = p.at((p.b + i) % 4, (p.a + j) % 4, p.c)
                self.push(self.arrive(origin), origin, p.partner)
        for j in (0,) + near_first:
            for i in (0,) + near_first:
                z, y = (p.z + i) % 4, (p.y + j) % 4
                self.arrive((z * 4 + y) * 2 + 1 - p.c)
        self.own.wait()
        for copy in self.sent:
            copy.wait_send()


class PlaneScatter:
    def __init__(self, place, src, view, scratch):
        self.place, self.src, self.view = place, src, view
        (self.got1, self.sum1, self.got2, self.sum2, self.got3, self.send1, self.recv1,
         self.send2, self.recv2, self.send3, self.recv3) = scratch

    @staticmethod
    def scratch(block, dtype=jnp.bfloat16):
        wide = lambda *lead: pltpu.VMEM(lead + block, dtype)
        return [wide(16), wide(4, 4), wide(4, 4), wide(4), wide(4), DMA((16,)), DMA((16,)),
                DMA((4,)), DMA((4,)), DMA((4,)), DMA((4,))]

    def start(self):
        p = self.place
        self.sent1 = []
        for i in (2, 1, 3, 0):
            for a in range(4):
                b = (p.a + i) % 4
                k = b * 4 + a
                copy = copy_to(
                    self.view(self.src, p.at(b, a, 1 - p.c)),
                    self.got1.at[k],
                    self.send1.at[k],
                    self.recv1.at[k],
                    p.x,
                    p.partner,
                )
                copy.start()
                self.sent1.append(copy)

    def middle(self):
        p = self.place
        sent2 = []
        for i in (2, 1, 3, 0):
            b = (p.b + i) % 4
            for a in range(4):
                k = b * 4 + a
                copy_to(
                    self.got1.at[k], self.got1.at[k], self.send1.at[k], self.recv1.at[k],
                    p.x, p.partner,
                ).wait_recv()
                own = self.view(self.src, p.at(b, a, p.c))[...].astype(jnp.float32)
                self.sum1[b, a] = (own + self.got1[k].astype(jnp.float32)).astype(self.sum1.dtype)
            if i:
                copy = copy_to(
                    self.sum1.at[b], self.got2.at[p.b], self.send2.at[i], self.recv2.at[p.b],
                    p.x, p.b_peer(i),
                )
                copy.start()
                sent2.append(copy)
        for i in near_first:
            b = (p.b + i) % 4
            copy_to(
                self.got2.at[b], self.got2.at[b], self.send2.at[i], self.recv2.at[b],
                p.x, p.b_peer(i),
            ).wait_recv()
        sent3 = []
        for j in (2, 1, 3, 0):
            a = (p.a + j) % 4
            total = self.sum1[p.b, a].astype(jnp.float32)
            for i in near_first:
                total += self.got2[(p.b + i) % 4, a].astype(jnp.float32)
            if j:
                self.sum2[a] = total.astype(self.sum2.dtype)
                copy = copy_to(
                    self.sum2.at[a], self.got3.at[p.a], self.send3.at[j], self.recv3.at[p.a],
                    p.x, p.a_peer(j),
                )
                copy.start()
                sent3.append(copy)
        for j in near_first:
            a = (p.a + j) % 4
            copy_to(
                self.got3.at[a], self.got3.at[a], self.send3.at[j], self.recv3.at[a],
                p.x, p.a_peer(j),
            ).wait_recv()
            total += self.got3[a].astype(jnp.float32)
        for copy in self.sent1 + sent2 + sent3:
            copy.wait_send()
        return total


def across_gather(place, src, out, send, recv):
    own = pltpu.make_async_copy(src, out.at[place.x], send.at[0])
    own.start()
    sent = []
    for j in near_first:
        copy = copy_to(src, out.at[place.x], send.at[j], recv.at[place.x], (place.x + j) % 4, place.f)
        copy.start()
        sent.append(copy)

    def finish():
        for j in near_first:
            x = (place.x + j) % 4
            copy_to(out.at[x], out.at[x], send.at[j], recv.at[x], x, place.f).wait_recv()
        own.wait()
        for copy in sent:
            copy.wait_send()

    return finish


def params(collective_id, mib):
    return pltpu.CompilerParams(
        collective_id=collective_id, has_side_effects=True, vmem_limit_bytes=mib * 1024 * 1024
    )


def column_block(ref, f):
    return ref.at[:, pl.ds(pl.multiple_of(f * 128, 128), 128)]


def row_block(ref, f):
    return ref.at[f]


def gather_input(mlp_input, table):
    def kernel(src, tab, out, tab_x, tab_all, send, recv, x_send, x_recv, t_send, t_recv):
        place = Place()
        meet(place, True)
        finish_table = across_gather(place, tab, tab_x, x_send, x_recv)
        gather = PlaneGather(place, src, out, column_block, send, recv)
        gather.start()
        finish_table()
        tables = PlaneGather(place, tab_x, tab_all, row_block, t_send, t_recv)
        tables.start()
        gather.relay()
        tables.relay()
        gather.finish()
        tables.finish()

    rows, cols = mlp_input.shape
    ints = lambda *lead: jax.ShapeDtypeStruct(lead + table.shape, jnp.int32)
    out, _, tables = pl.pallas_call(
        kernel,
        out_shape=(jax.ShapeDtypeStruct((rows, cols * 32), jnp.bfloat16), ints(4), ints(32, 4)),
        in_specs=[ANY] * 2,
        out_specs=[ANY] * 3,
        scratch_shapes=[DMA((32,)), DMA((32,)), DMA((4,)), DMA((4,)), DMA((32,)), DMA((32,))],
        compiler_params=params(0, 4),
        name="gather_input",
    )(mlp_input, table)
    return out, tables


def scatter_branch(partial):
    def kernel(src, out, *scratch):
        place = Place()
        meet(place, False)
        scatter = PlaneScatter(place, src, row_block, scratch)
        scatter.start()
        out[...] = scatter.middle()

    return pl.pallas_call(
        kernel,
        out_shape=jax.ShapeDtypeStruct((8, 4096), jnp.float32),
        in_specs=[VMEM],
        out_specs=VMEM,
        scratch_shapes=PlaneScatter.scratch((8, 4096)),
        compiler_params=params(1, 12),
        name="scatter_branch",
    )(partial.reshape(32, 8, 4096))


def near_order(m):
    return m + m // 2 - 2 * (m // 3)


def owner_block(rows, query_ref, index_ref, scale_ref, code_ref, pull_ref, sums_ref):
    count = rows.size
    raw = lax.dot_general(
        query_ref[rows, :], index_ref[...], contract_last, preferred_element_type=jnp.float32
    )
    scale = scale_ref[...]
    scores = inverse_temp * raw * scale
    here = lax.broadcasted_iota(jnp.int32, scores.shape, 1)
    uses = jnp.zeros(scores.shape, jnp.float32)
    codes = code_ref[rows, :]
    for slot in range(8):
        uses += jnp.where(codes[:, slot : slot + 1] == here, 1.0, 0.0)
    weights = uses * jnp.exp(scores)
    exps = jnp.sum(weights, axis=1, keepdims=True)
    inners = jnp.sum(weights * scores, axis=1, keepdims=True)
    lane = lax.broadcasted_iota(jnp.int32, (count, 128), 1)
    sums_ref[rows, :] = jnp.where(lane == 0, exps, jnp.where(lane == 1, inners, 0.0))
    weights = (weights * scale).astype(jnp.bfloat16)
    for part in range(4):
        cols = pl.ds(part * 1024, 1024)
        pull_ref[rows, cols] = jnp.dot(
            weights, index_ref[:, cols], preferred_element_type=jnp.float32
        ).astype(jnp.bfloat16)


class AllSum:
    def __init__(self, place, src, scratch):
        self.place, self.src = place, src
        (self.got1, self.sum1, self.got2, self.sum2, self.got3, self.stage, self.got4, self.send1,
         self.recv1, self.send2, self.recv2, self.send3, self.recv3, self.send4,
         self.recv4) = scratch

    @staticmethod
    def scratch(width, dtype):
        wide = lambda *lead: pltpu.VMEM(lead + (32, width), dtype)
        last = pltpu.VMEM((4, 8, width), dtype)
        return [wide(16), wide(4, 4), wide(4, 4), wide(4), wide(4), last, last,
                DMA((16,)), DMA((16,))] + [DMA((4,))] * 6

    def rows(self, k, c):
        return self.src.at[pl.ds(pl.multiple_of(k * 64 + c * 32, 32), 32), :]

    def to_partner(self, k):
        p = self.place
        return copy_to(self.rows(k, 1 - p.c), self.got1.at[k], self.send1.at[k], self.recv1.at[k],
                       p.x, p.partner)

    def to_b(self, i):
        p = self.place
        return copy_to(self.sum1.at[(p.b + i) % 4], self.got2.at[p.b], self.send2.at[i],
                       self.recv2.at[p.b], p.x, p.b_peer(i))

    def to_a(self, j):
        p = self.place
        return copy_to(self.sum2.at[(p.a + j) % 4], self.got3.at[p.a], self.send3.at[j],
                       self.recv3.at[p.a], p.x, p.a_peer(j))

    def to_x(self, j):
        p = self.place
        x = (p.x + j) % 4
        return copy_to(self.stage.at[x], self.got4.at[p.x], self.send4.at[j], self.recv4.at[p.x],
                       x, p.f)

    def group(self, i):
        p = self.place
        b = (p.b + i) % 4

        def add(a, carry):
            k = p.at(b, a, p.c) // 2
            got = self.got1.at[k]
            copy_to(got, got, self.send1.at[k], self.recv1.at[k], p.x, p.partner).wait_recv()
            own = self.rows(k, p.c)[...].astype(jnp.float32)
            self.sum1[b, a] = (own + got[...].astype(jnp.float32)).astype(self.sum1.dtype)
            return carry

        lax.fori_loop(0, 4, add, 0)
        if i:
            self.to_b(i).start()

    def second(self):
        p = self.place
        for i in near_first:
            got = self.got2.at[(p.b + i) % 4]
            copy_to(got, got, self.send2.at[i], self.recv2.at[(p.b + i) % 4], p.x,
                    p.b_peer(i)).wait_recv()
        for j in (2, 1, 3, 0):
            a = (p.a + j) % 4
            total = self.sum1[p.b, a].astype(jnp.float32)
            for i in near_first:
                total += self.got2[(p.b + i) % 4, a].astype(jnp.float32)
            self.sum2[a] = total.astype(self.sum2.dtype)
            if j:
                self.to_a(j).start()

    def third(self):
        p = self.place
        total = self.sum2[p.a].astype(jnp.float32)
        for j in near_first:
            a = (p.a + j) % 4
            got = self.got3.at[a]
            copy_to(got, got, self.send3.at[j], self.recv3.at[a], p.x, p.a_peer(j)).wait_recv()
            total += got[...].astype(jnp.float32)
        for x in range(4):
            self.stage[x] = total[8 * x : 8 * x + 8].astype(self.stage.dtype)
        for j in near_first:
            self.to_x(j).start()

    def last(self):
        p = self.place
        own = self.stage[p.x].astype(jnp.float32)
        for j in near_first:
            x = (p.x + j) % 4
            got = self.got4.at[x]
            copy_to(got, got, self.send4.at[j], self.recv4.at[x], x, p.f).wait_recv()
            own += got[...].astype(jnp.float32)
        for j in near_first:
            self.to_b(j).wait_send()
            self.to_a(j).wait_send()
            self.to_x(j).wait_send()

        def sent(k, carry):
            self.to_partner(k).wait_send()
            return carry

        lax.fori_loop(0, 16, sent, 0)
        return own


def attend(unit_rows, span_index, key_scale, codes, hidden, factors, whole_input):
    n = 15

    def kernel(unit, index, scale, code, hid, fac, inp,
               pull_out, sums_out, hid_x, fac_x, inp_x,
               unit_x, query, pull, sums, u_send, u_recv, a_send, b_send, d_send, recv,
               h_send, h_recv, f_send, f_recv, i_send, i_recv, pair_send, pair_recv, *scratch):
        p = place = Place()
        meet(place, True)

        finish_unit = across_gather(place, unit, unit_x, u_send, u_recv)
        block = lambda f: query.at[pl.ds(pl.multiple_of(f * 32, 32), 32), :]
        half = lambda c: pl.ds(pl.multiple_of(c * 512, 512), 512)
        own_i = pltpu.make_async_copy(
            inp.at[:, pl.ds(pl.multiple_of(p.x * 1024, 1024), 1024)], inp_x.at[p.x], i_send.at[0]
        )
        own_i.start()
        finish_unit()
        block(p.f)[...] = jnp.concatenate(
            [unit_x[x].astype(jnp.float32) for x in range(4)], axis=0
        ).astype(jnp.bfloat16)

        def push(origin, f, send):
            copy = copy_to(block(origin), block(origin), send, recv.at[origin], p.x, f)
            copy.start()
            return copy

        def arrive(origin):
            copy_to(block(origin), block(origin), d_send.at[origin], recv.at[origin], p.x,
                    p.partner).wait_recv()

        sent = []
        for j in near_first:
            sent.append(push(p.f, p.a_peer(j), a_send.at[j]))
        for j in near_first:
            sent.append(push(p.f, p.b_peer(j), b_send.at[j]))
        push(p.f, p.partner, d_send.at[p.f])
        for j in near_first:
            origin = p.a_peer(j)
            arrive(origin)
            for i in near_first:
                sent.append(push(origin, p.b_peer(i), b_send.at[4 * j + i]))
            push(origin, p.partner, d_send.at[origin])

        finish_hidden = across_gather(place, hid, hid_x, h_send, h_recv)
        finish_factors = across_gather(place, fac, fac_x, f_send, f_recv)
        for j in near_first:
            x = (p.x + j) % 4
            copy = copy_to(
                inp.at[:, pl.ds(pl.multiple_of(x * 1024 + p.c * 512, 512), 512)],
                inp_x.at[p.x, :, half(p.c)], i_send.at[j], i_recv.at[p.x], x, p.f,
            )
            copy.start()
            sent.append(copy)

        first = AllSum(place, pull, scratch[:n])
        second = AllSum(place, sums, scratch[n:])

        for stage, group in enumerate((None, 1, 3, 2)):

            def chip(turn, carry):
                base, other = near_order(stage), near_order(stage + turn // 2)
                swap = turn % 2
                z = (p.z + base + (other - base) * swap) % 4
                y = (p.y + base + (other - base) * (1 - swap)) % 4
                k = z * 4 + y
                origin = k * 2 + p.c

                def forward():
                    arrive(origin)
                    push(origin, p.partner, d_send.at[origin])

                if stage:
                    forward()
                else:
                    pl.when(jnp.logical_and(turn > 1, (swap + p.c) % 2 == 1))(forward)
                arrive(k * 2 + 1 - p.c)
                rows = pl.ds(pl.multiple_of(k * 64, 64), 64)
                owner_block(rows, query, index, scale, code, pull, sums)
                first.to_partner(k).start()
                second.to_partner(k).start()
                return carry

            lax.fori_loop(1, 8 - 2 * stage, chip, 0)
            if group:
                first.group(group)
                second.group(group)
        first.group(0)
        second.group(0)
        first.second()
        second.second()
        first.third()
        second.third()

        for j in near_first:
            x = (p.x + j) % 4
            region = inp_x.at[x, :, half(p.c)]
            copy_to(region, region, i_send.at[j], i_recv.at[x], x, p.f).wait_recv()
            copy = copy_to(region, region, pair_send.at[j], pair_recv.at[x], p.x, p.partner)
            copy.start()
            sent.append(copy)
        finish_hidden()
        finish_factors()
        pull_out[...] = first.last()
        sums_out[...] = second.last()
        for j in near_first:
            x = (p.x + j) % 4
            region = inp_x.at[x, :, half(1 - p.c)]
            copy_to(region, region, pair_send.at[j], pair_recv.at[x], p.x, p.partner).wait_recv()
        own_i.wait()
        for copy in sent:
            copy.wait_send()

        def pushed(k, carry):
            origin = k * 2 + p.c
            copy_to(block(origin), block(origin), d_send.at[origin], recv.at[origin], p.x,
                    p.partner).wait_send()
            return carry

        lax.fori_loop(0, 16, pushed, 0)

    bf = lambda *shape: jax.ShapeDtypeStruct(shape, jnp.bfloat16)
    return pl.pallas_call(
        kernel,
        out_shape=(
            jax.ShapeDtypeStruct((8, 4096), jnp.float32),
            jax.ShapeDtypeStruct((8, 128), jnp.float32),
            bf(4, *hidden.shape),
            bf(4, *factors.shape),
            bf(4, 256, 1024),
        ),
        in_specs=[ANY, VMEM, VMEM, VMEM, ANY, ANY, ANY],
        out_specs=[VMEM, VMEM, ANY, ANY, ANY],
        scratch_shapes=[
            pltpu.VMEM((4, 8, 4096), jnp.bfloat16),
            pltpu.VMEM((1024, 4096), jnp.bfloat16),
            pltpu.VMEM((1024, 4096), jnp.bfloat16),
            pltpu.VMEM((1024, 128), jnp.float32),
            DMA((4,)), DMA((4,)), DMA((4,)), DMA((16,)), DMA((32,)), DMA((32,)),
        ]
        + [DMA((4,))] * 8
        + AllSum.scratch(4096, jnp.bfloat16)
        + AllSum.scratch(128, jnp.float32),
        compiler_params=params(4, 48),
        name="attend",
    )(unit_rows, span_index, key_scale, codes, hidden, factors, whole_input)


def gather_head(head_grad):
    def kernel(head, out, head_x, send, recv, hx_send, hx_recv):
        place = Place()
        p = place
        meet(place, True)
        gather = PlaneGather(place, head, out, row_block, send, recv)
        gather.start()
        wide = lambda x: pl.ds(pl.multiple_of(x * 1024, 1024), 1024)
        own = pltpu.make_async_copy(head.at[:, wide(p.x)], head_x.at[p.x], hx_send.at[0])
        own.start()
        sent = []
        for j in near_first:
            x = (p.x + j) % 4
            copy = copy_to(head.at[:, wide(x)], head_x.at[p.x], hx_send.at[j], hx_recv.at[p.x], x, p.f)
            copy.start()
            sent.append(copy)
        gather.relay()
        gather.finish()
        for j in near_first:
            x = (p.x + j) % 4
            copy_to(
                head_x.at[x], head_x.at[x], hx_send.at[j], hx_recv.at[x], x, p.f
            ).wait_recv()
        own.wait()
        for copy in sent:
            copy.wait_send()

    bf = lambda *shape: jax.ShapeDtypeStruct(shape, jnp.bfloat16)
    out, head_x = pl.pallas_call(
        kernel,
        out_shape=(bf(32, 8, 4096), bf(4, 8, 1024)),
        in_specs=[ANY],
        out_specs=[ANY] * 2,
        scratch_shapes=[DMA((32,)), DMA((32,)), DMA((4,)), DMA((4,))],
        compiler_params=params(2, 4),
        name="gather_head",
    )(head_grad)
    return out.reshape(256, 4096), head_x


def finish_links(partial, acts, head_x):
    def kernel(src, act, hx, out, act_x, head_cols, send, recv, x_send, x_recv, *scratch):
        place = Place()
        meet(place, True)
        finish_acts = across_gather(place, act, act_x, x_send, x_recv)
        scatter = PlaneScatter(place, src, column_block, scratch)
        scatter.start()
        gather = PlaneGather(
            place, hx, head_cols, lambda ref, f: ref.at[:, f], send, recv
        )
        gather.start()
        gather.relay()
        out[...] = scatter.middle().astype(jnp.bfloat16)
        gather.finish()
        finish_acts()

    bf = lambda *shape: jax.ShapeDtypeStruct(shape, jnp.bfloat16)
    return pl.pallas_call(
        kernel,
        out_shape=(bf(256, 128), bf(4, *acts.shape), bf(4, 32, 8, 1024)),
        in_specs=[VMEM, ANY, ANY],
        out_specs=[VMEM, ANY, ANY],
        scratch_shapes=[DMA((32,)), DMA((32,)), DMA((4,)), DMA((4,))]
        + PlaneScatter.scratch((256, 128)),
        compiler_params=params(3, 12),
        name="finish_links",
    )(partial, acts, head_x)


def shards(
    mlp_input,
    residual_in,
    gate_weight,
    up_weight,
    down_weight,
    span_index,
    positive_keys,
    request_rows,
    request_counts,
    negative_slots,
):
    dp_count = lax.axis_size("dp")
    fsdp_count = lax.axis_size("fsdp")
    owners = dp_count * fsdp_count
    slot_cap = request_rows.shape[2]
    rows, width = positive_keys.shape

    shape = (1, 1, slot_cap, owners)
    slot_ids = lax.broadcasted_iota(jnp.int32, shape, 3) * slot_cap
    slot_ids += lax.broadcasted_iota(jnp.int32, shape, 2)
    used = jnp.any(negative_slots[:, :, None, None] == slot_ids, axis=1).astype(jnp.int32)
    table = jnp.sum(used * (lax.broadcasted_iota(jnp.int32, used.shape, 0) + 1), axis=0) - 1
    whole_input, tables = gather_input(mlp_input, table)

    me = lax.axis_index("dp") * fsdp_count + lax.axis_index("fsdp")
    mine = lax.broadcasted_iota(jnp.int32, tables.shape, 3) == me
    user = jnp.sum(jnp.where(mine, tables, 0), axis=3).reshape(owners, slot_cap)
    requests = jnp.where(
        lax.broadcasted_iota(jnp.int32, (owners, slot_cap), 1) < request_counts,
        request_rows[:, 0, :],
        -1,
    )
    requests = requests.reshape(dp_count, fsdp_count, slot_cap).transpose(1, 0, 2)
    requests = requests.reshape(owners, slot_cap)
    ranks = lax.broadcasted_iota(jnp.int32, (1, rows, 1), 1)
    codes = jnp.where(user[:, None, :] == ranks, requests[:, None, :], -1)
    codes = codes.reshape(owners * rows, slot_cap)
    wide = span_index.astype(jnp.float32)
    key_scale = lax.rsqrt(jnp.sum(wide * wide, axis=-1) + eps)[None, :]

    gate_act = jnp.dot(whole_input, gate_weight, preferred_element_type=jnp.float32)
    up_act = jnp.dot(whole_input, up_weight, preferred_element_type=jnp.float32)
    sigmoid_gate = jax.nn.sigmoid(gate_act)
    silu_gate = gate_act * sigmoid_gate
    hidden = (silu_gate * up_act).astype(jnp.bfloat16)
    branch = scatter_branch(jnp.dot(hidden, down_weight, preferred_element_type=jnp.bfloat16))
    top_state = branch + residual_in.astype(jnp.float32)
    row_norm = jnp.sqrt(jnp.sum(top_state * top_state, axis=-1) + eps)
    unit_rows = top_state / row_norm[:, None]
    positive = positive_keys.astype(jnp.float32)
    positive_unit = positive / jnp.sqrt(jnp.sum(positive * positive, axis=-1, keepdims=True) + eps)
    positive_score = inverse_temp * jnp.sum(unit_rows * positive_unit, axis=-1)

    gate_factor = up_act * (sigmoid_gate * (1.0 + gate_act * (1.0 - sigmoid_gate)))
    pull, sums, hidden_x, factors_x, input_x = attend(
        unit_rows.astype(jnp.bfloat16),
        span_index,
        key_scale,
        codes,
        hidden.T,
        jnp.stack([gate_factor.T, silu_gate.T]).astype(jnp.bfloat16),
        whole_input,
    )
    positive_weight = jnp.exp(positive_score)
    exp_total = sums[:, 0] + positive_weight
    query_loss = jnp.log(exp_total) - positive_score
    positive_coeff = positive_weight / exp_total - 1.0
    inner = sums[:, 1] / exp_total + positive_coeff * positive_score
    pull = inverse_temp * (pull / exp_total[:, None] + positive_coeff[:, None] * positive_unit)
    head_grad = ((pull - inner[:, None] * unit_rows) / row_norm[:, None]).astype(jnp.bfloat16)

    gathered_grad, head_x = gather_head(head_grad)
    hidden_grad = lax.dot_general(
        gathered_grad, down_weight, contract_last, preferred_element_type=jnp.float32
    )
    gate_grad_act = (hidden_grad * gate_factor).astype(jnp.bfloat16)
    up_grad_act = (hidden_grad * silu_gate).astype(jnp.bfloat16)
    input_term = lax.dot_general(
        gate_grad_act, gate_weight, contract_last, preferred_element_type=jnp.float32
    ) + lax.dot_general(up_grad_act, up_weight, contract_last, preferred_element_type=jnp.float32)
    input_grad, hidden_grad_x, head_cols = finish_links(
        input_term.astype(jnp.bfloat16), hidden_grad.T.astype(jnp.bfloat16), head_x
    )
    over_groups = (((0, 2), (0, 1)), ((), ()))
    hidden_grad_x = hidden_grad_x.astype(jnp.float32)
    weight_grads = [
        lax.dot_general(
            (hidden_grad_x * factors_x[:, k].astype(jnp.float32)).astype(jnp.bfloat16),
            input_x,
            over_groups,
            preferred_element_type=jnp.float32,
        ).astype(jnp.bfloat16)
        for k in range(2)
    ]
    down_grad = lax.dot_general(
        hidden_x, head_cols.reshape(4, 256, 1024), over_groups, preferred_element_type=jnp.float32
    ).astype(jnp.bfloat16)
    return (query_loss, input_grad, weight_grads[0].T, weight_grads[1].T, down_grad)


def solution(mesh):
    return jax.shard_map(
        shards,
        mesh=mesh,
        in_specs=(
            P("dp", "fsdp"),
            P(("dp", "fsdp"), None),
            P(None, "fsdp"),
            P(None, "fsdp"),
            P("fsdp", None),
            P(("dp", "fsdp"), None),
            P(("dp", "fsdp"), None),
            P(None, ("dp", "fsdp"), None),
            P(None, ("dp", "fsdp")),
            P(("dp", "fsdp"), None),
        ),
        out_specs=(
            P(("dp", "fsdp")),
            P("dp", "fsdp"),
            P("dp", "fsdp"),
            P("dp", "fsdp"),
            P("fsdp", "dp"),
        ),
        check_vma=False,
    )
```

```python
import functools

import jax
import jax.numpy as jnp
from jax import lax
from jax.experimental import pallas as pl
from jax.experimental.pallas import tpu as pltpu
from jax.sharding import PartitionSpec as P

inverse_temp = 50.0
eps = 1e-06
contract_first = (((0,), (0,)), ((), ()))
contract_last = (((1,), (1,)), ((), ()))
ANY = pl.BlockSpec(memory_space=pl.ANY)
VMEM = pl.BlockSpec(memory_space=pltpu.VMEM)
DMA = pltpu.SemaphoreType.DMA
near_first = (1, 3, 2)


class Place:
    def __init__(self):
        self.x = lax.axis_index("dp")
        self.f = lax.axis_index("fsdp")
        self.z = self.f // 8
        self.y = (self.f // 2) % 4
        self.c = self.f % 2
        self.a = self.y * (1 - self.c) + self.z * self.c
        self.b = self.z * (1 - self.c) + self.y * self.c
        self.partner = self.f + 1 - 2 * self.c

    def at(self, b, a, c):
        z = b * (1 - c) + a * c
        y = a * (1 - c) + b * c
        return (z * 4 + y) * 2 + c

    def a_peer(self, j):
        return self.at(self.b, (self.a + j) % 4, self.c)

    def b_peer(self, j):
        return self.at((self.b + j) % 4, self.a, self.c)


def copy_to(src, dst, send, recv, x, f):
    return pltpu.make_async_remote_copy(
        src_ref=src,
        dst_ref=dst,
        send_sem=send,
        recv_sem=recv,
        device_id=(x, f),
        device_id_type=pl.DeviceIdType.MESH,
    )


def meet(place, across):
    barrier = pltpu.get_barrier_semaphore()
    peers = [(place.x, place.partner)]
    peers += [(place.x, place.a_peer(j)) for j in near_first]
    peers += [(place.x, place.b_peer(j)) for j in near_first]
    if across:
        peers += [((place.x + j) % 4, place.f) for j in near_first]
    for x, f in peers:
        pl.semaphore_signal(barrier, inc=1, device_id=(x, f), device_id_type=pl.DeviceIdType.MESH)
    pl.semaphore_wait(barrier, len(peers))


class PlaneGather:
    copies = 32

    def __init__(self, place, src, out, view, send, recv):
        self.place, self.src, self.out, self.view = place, src, out, view
        self.send, self.recv = send, recv
        self.sent = []

    def push(self, ref, origin, f):
        copy = copy_to(
            ref,
            self.view(self.out, origin),
            self.send.at[len(self.sent)],
            self.recv.at[origin],
            self.place.x,
            f,
        )
        copy.start()
        self.sent.append(copy)

    def arrive(self, origin):
        block = self.view(self.out, origin)
        copy_to(
            block, block, self.send.at[31], self.recv.at[origin], self.place.x, self.place.partner
        ).wait_recv()
        return block

    def start(self):
        p = self.place
        self.own = pltpu.make_async_copy(self.src, self.view(self.out, p.f), self.send.at[31])
        for j in near_first:
            self.push(self.src, p.f, p.a_peer(j))
        for j in near_first:
            self.push(self.src, p.f, p.b_peer(j))
        self.push(self.src, p.f, p.partner)
        self.own.start()

    def relay(self):
        p = self.place
        for j in near_first:
            origin = p.a_peer(j)
            block = self.arrive(origin)
            for i in near_first:
                self.push(block, origin, p.b_peer(i))
            self.push(block, origin, p.partner)

    def finish(self):
        p = self.place
        for j in (0,) + near_first:
            for i in near_first:
                origin = p.at((p.b + i) % 4, (p.a + j) % 4, p.c)
                self.push(self.arrive(origin), origin, p.partner)
        for j in (0,) + near_first:
            for i in (0,) + near_first:
                z, y = (p.z + i) % 4, (p.y + j) % 4
                self.arrive((z * 4 + y) * 2 + 1 - p.c)
        self.own.wait()
        for copy in self.sent:
            copy.wait_send()


class PlaneScatter:
    def __init__(self, place, src, view, scratch):
        self.place, self.src, self.view = place, src, view
        (self.got1, self.sum1, self.got2, self.sum2, self.got3, self.send1, self.recv1,
         self.send2, self.recv2, self.send3, self.recv3) = scratch

    @staticmethod
    def scratch(block, dtype=jnp.bfloat16):
        wide = lambda *lead: pltpu.VMEM(lead + block, dtype)
        return [wide(16), wide(4, 4), wide(4, 4), wide(4), wide(4), DMA((16,)), DMA((16,)),
                DMA((4,)), DMA((4,)), DMA((4,)), DMA((4,))]

    def start(self):
        p = self.place
        self.sent1 = []
        for i in (2, 1, 3, 0):
            for a in range(4):
                b = (p.a + i) % 4
                k = b * 4 + a
                copy = copy_to(
                    self.view(self.src, p.at(b, a, 1 - p.c)),
                    self.got1.at[k],
                    self.send1.at[k],
                    self.recv1.at[k],
                    p.x,
                    p.partner,
                )
                copy.start()
                self.sent1.append(copy)

    def middle(self):
        p = self.place
        sent2 = []
        for i in (2, 1, 3, 0):
            b = (p.b + i) % 4
            for a in range(4):
                k = b * 4 + a
                copy_to(
                    self.got1.at[k], self.got1.at[k], self.send1.at[k], self.recv1.at[k],
                    p.x, p.partner,
                ).wait_recv()
                own = self.view(self.src, p.at(b, a, p.c))[...].astype(jnp.float32)
                self.sum1[b, a] = (own + self.got1[k].astype(jnp.float32)).astype(self.sum1.dtype)
            if i:
                copy = copy_to(
                    self.sum1.at[b], self.got2.at[p.b], self.send2.at[i], self.recv2.at[p.b],
                    p.x, p.b_peer(i),
                )
                copy.start()
                sent2.append(copy)
        for i in near_first:
            b = (p.b + i) % 4
            copy_to(
                self.got2.at[b], self.got2.at[b], self.send2.at[i], self.recv2.at[b],
                p.x, p.b_peer(i),
            ).wait_recv()
        sent3 = []
        for j in (2, 1, 3, 0):
            a = (p.a + j) % 4
            total = self.sum1[p.b, a].astype(jnp.float32)
            for i in near_first:
                total += self.got2[(p.b + i) % 4, a].astype(jnp.float32)
            if j:
                self.sum2[a] = total.astype(self.sum2.dtype)
                copy = copy_to(
                    self.sum2.at[a], self.got3.at[p.a], self.send3.at[j], self.recv3.at[p.a],
                    p.x, p.a_peer(j),
                )
                copy.start()
                sent3.append(copy)
        for j in near_first:
            a = (p.a + j) % 4
            copy_to(
                self.got3.at[a], self.got3.at[a], self.send3.at[j], self.recv3.at[a],
                p.x, p.a_peer(j),
            ).wait_recv()
            total += self.got3[a].astype(jnp.float32)
        for copy in self.sent1 + sent2 + sent3:
            copy.wait_send()
        return total


def across_gather(place, src, out, send, recv):
    own = pltpu.make_async_copy(src, out.at[place.x], send.at[0])
    own.start()
    sent = []
    for j in near_first:
        copy = copy_to(src, out.at[place.x], send.at[j], recv.at[place.x], (place.x + j) % 4, place.f)
        copy.start()
        sent.append(copy)

    def finish():
        for j in near_first:
            x = (place.x + j) % 4
            copy_to(out.at[x], out.at[x], send.at[j], recv.at[x], x, place.f).wait_recv()
        own.wait()
        for copy in sent:
            copy.wait_send()

    return finish


def params(collective_id, mib):
    return pltpu.CompilerParams(
        collective_id=collective_id, has_side_effects=True, vmem_limit_bytes=mib * 1024 * 1024
    )


def column_block(ref, f):
    return ref.at[:, pl.ds(pl.multiple_of(f * 128, 128), 128)]


def row_block(ref, f):
    return ref.at[f]


def gather_input(mlp_input, table):
    def kernel(src, tab, out, tab_x, tab_all, send, recv, x_send, x_recv, t_send, t_recv):
        place = Place()
        meet(place, True)
        finish_table = across_gather(place, tab, tab_x, x_send, x_recv)
        gather = PlaneGather(place, src, out, column_block, send, recv)
        gather.start()
        finish_table()
        tables = PlaneGather(place, tab_x, tab_all, row_block, t_send, t_recv)
        tables.start()
        gather.relay()
        tables.relay()
        gather.finish()
        tables.finish()

    rows, cols = mlp_input.shape
    ints = lambda *lead: jax.ShapeDtypeStruct(lead + table.shape, jnp.int32)
    out, _, tables = pl.pallas_call(
        kernel,
        out_shape=(jax.ShapeDtypeStruct((rows, cols * 32), jnp.bfloat16), ints(4), ints(32, 4)),
        in_specs=[ANY] * 2,
        out_specs=[ANY] * 3,
        scratch_shapes=[DMA((32,)), DMA((32,)), DMA((4,)), DMA((4,)), DMA((32,)), DMA((32,))],
        compiler_params=params(0, 4),
        name="gather_input",
    )(mlp_input, table)
    return out, tables


def scatter_branch(partial):
    def kernel(src, out, *scratch):
        place = Place()
        meet(place, False)
        scatter = PlaneScatter(place, src, row_block, scratch)
        scatter.start()
        out[...] = scatter.middle()

    return pl.pallas_call(
        kernel,
        out_shape=jax.ShapeDtypeStruct((8, 4096), jnp.float32),
        in_specs=[VMEM],
        out_specs=VMEM,
        scratch_shapes=PlaneScatter.scratch((8, 4096)),
        compiler_params=params(1, 12),
        name="scatter_branch",
    )(partial.reshape(32, 8, 4096))


def near_order(m):
    return m + m // 2 - 2 * (m // 3)


def owner_batch(count, batch_ref, code_ref, index_ref, scale_ref, weight_ref):
    raw = lax.dot_general(
        batch_ref[:count, :], index_ref[...], contract_last, preferred_element_type=jnp.float32
    )
    scale = scale_ref[...]
    scores = inverse_temp * raw * scale
    here = lax.broadcasted_iota(jnp.int32, scores.shape, 1)
    uses = jnp.zeros(scores.shape, jnp.float32)
    codes = code_ref[:count, :]
    for slot in range(8):
        uses += jnp.where(codes[:, slot : slot + 1] == here, 1.0, 0.0)
    weights = uses * jnp.exp(scores)
    exps = jnp.sum(weights, axis=1, keepdims=True)
    inners = jnp.sum(weights * scores, axis=1, keepdims=True)
    lane = lax.broadcasted_iota(jnp.int32, (count, 128), 1)
    weight_ref[:count, :] = (weights * scale).astype(jnp.bfloat16)
    return jnp.where(lane == 0, exps, jnp.where(lane == 1, inners, 0.0))


class AllSum:
    def __init__(self, place, src, scratch):
        self.place, self.src = place, src
        (self.got1, self.sum1, self.got2, self.sum2, self.got3, self.stage, self.got4, self.send1,
         self.recv1, self.send2, self.recv2, self.send3, self.recv3, self.send4,
         self.recv4) = scratch

    @staticmethod
    def scratch(width, dtype):
        wide = lambda *lead: pltpu.VMEM(lead + (32, width), dtype)
        last = pltpu.VMEM((4, 8, width), dtype)
        return [wide(16), wide(4, 4), wide(4, 4), wide(4), wide(4), last, last,
                DMA((16,)), DMA((16,))] + [DMA((4,))] * 6

    def rows(self, k, c):
        return self.src.at[pl.ds(pl.multiple_of(k * 64 + c * 32, 32), 32), :]

    def to_partner(self, k):
        p = self.place
        return copy_to(self.rows(k, 1 - p.c), self.got1.at[k], self.send1.at[k], self.recv1.at[k],
                       p.x, p.partner)

    def to_b(self, i):
        p = self.place
        return copy_to(self.sum1.at[(p.b + i) % 4], self.got2.at[p.b], self.send2.at[i],
                       self.recv2.at[p.b], p.x, p.b_peer(i))

    def to_a(self, j):
        p = self.place
        return copy_to(self.sum2.at[(p.a + j) % 4], self.got3.at[p.a], self.send3.at[j],
                       self.recv3.at[p.a], p.x, p.a_peer(j))

    def to_x(self, j):
        p = self.place
        x = (p.x + j) % 4
        return copy_to(self.stage.at[x], self.got4.at[p.x], self.send4.at[j], self.recv4.at[p.x],
                       x, p.f)

    def group(self, i):
        p = self.place
        b = (p.b + i) % 4

        def add(a, carry):
            k = p.at(b, a, p.c) // 2
            got = self.got1.at[k]
            copy_to(got, got, self.send1.at[k], self.recv1.at[k], p.x, p.partner).wait_recv()
            own = self.rows(k, p.c)[...].astype(jnp.float32)
            self.sum1[b, a] = (own + got[...].astype(jnp.float32)).astype(self.sum1.dtype)
            return carry

        lax.fori_loop(0, 4, add, 0)
        if i:
            self.to_b(i).start()

    def second(self):
        p = self.place
        for i in near_first:
            got = self.got2.at[(p.b + i) % 4]
            copy_to(got, got, self.send2.at[i], self.recv2.at[(p.b + i) % 4], p.x,
                    p.b_peer(i)).wait_recv()
        for j in (2, 1, 3, 0):
            a = (p.a + j) % 4
            total = self.sum1[p.b, a].astype(jnp.float32)
            for i in near_first:
                total += self.got2[(p.b + i) % 4, a].astype(jnp.float32)
            self.sum2[a] = total.astype(self.sum2.dtype)
            if j:
                self.to_a(j).start()

    def third(self):
        p = self.place
        total = self.sum2[p.a].astype(jnp.float32)
        for j in near_first:
            a = (p.a + j) % 4
            got = self.got3.at[a]
            copy_to(got, got, self.send3.at[j], self.recv3.at[a], p.x, p.a_peer(j)).wait_recv()
            total += got[...].astype(jnp.float32)
        for x in range(4):
            self.stage[x] = total[8 * x : 8 * x + 8].astype(self.stage.dtype)
        for j in near_first:
            self.to_x(j).start()

    def last(self):
        p = self.place
        own = self.stage[p.x].astype(jnp.float32)
        for j in near_first:
            x = (p.x + j) % 4
            got = self.got4.at[x]
            copy_to(got, got, self.send4.at[j], self.recv4.at[x], x, p.f).wait_recv()
            own += got[...].astype(jnp.float32)
        for j in near_first:
            self.to_b(j).wait_send()
            self.to_a(j).wait_send()
            self.to_x(j).wait_send()

        def sent(k, carry):
            self.to_partner(k).wait_send()
            return carry

        lax.fori_loop(0, 16, sent, 0)
        return own


def attend(unit_rows, span_index, codes, hidden, factors, whole_input):
    n = 15

    def kernel(unit, index, code, hid, fac, inp,
               pull_out, sums_out, hid_x, fac_x, inp_x,
               unit_x, query, pull, sums, batch, batch_code, weight, scale, u_send, u_recv, a_send, b_send, d_send, recv,
               h_send, h_recv, f_send, f_recv, i_send, i_recv, pair_send, pair_recv, *scratch):
        p = place = Place()
        meet(place, True)

        finish_unit = across_gather(place, unit, unit_x, u_send, u_recv)
        block = lambda f: query.at[pl.ds(pl.multiple_of(f * 32, 32), 32), :]
        half = lambda c: pl.ds(pl.multiple_of(c * 512, 512), 512)
        own_i = pltpu.make_async_copy(
            inp.at[:, pl.ds(pl.multiple_of(p.x * 1024, 1024), 1024)], inp_x.at[p.x], i_send.at[0]
        )
        own_i.start()
        finish_unit()
        block(p.f)[...] = jnp.concatenate(
            [unit_x[x].astype(jnp.float32) for x in range(4)], axis=0
        ).astype(jnp.bfloat16)

        def push(origin, f, send):
            copy = copy_to(block(origin), block(origin), send, recv.at[origin], p.x, f)
            copy.start()
            return copy

        def arrive(origin):
            copy_to(block(origin), block(origin), d_send.at[origin], recv.at[origin], p.x,
                    p.partner).wait_recv()

        sent = []
        for j in near_first:
            sent.append(push(p.f, p.a_peer(j), a_send.at[j]))
        for j in near_first:
            sent.append(push(p.f, p.b_peer(j), b_send.at[j]))
        push(p.f, p.partner, d_send.at[p.f])

        def norms(part, carry):
            rows = pl.ds(pl.multiple_of(part * 128, 128), 128)
            wide = index[rows, :].astype(jnp.float32)
            total = jnp.sum(wide * wide, axis=1, keepdims=True)
            row = lax.broadcasted_iota(jnp.int32, (128, 128), 0)
            col = lax.broadcasted_iota(jnp.int32, (128, 128), 1)
            across = jnp.sum(jnp.where(row == col, total, 0.0), axis=0, keepdims=True)
            scale[:, rows] = lax.rsqrt(across + eps)
            return carry

        for j in near_first:
            origin = p.a_peer(j)
            arrive(origin)
            for i in near_first:
                sent.append(push(origin, p.b_peer(i), b_send.at[4 * j + i]))
            push(origin, p.partner, d_send.at[origin])

        finish_hidden = across_gather(place, hid, hid_x, h_send, h_recv)
        finish_factors = across_gather(place, fac, fac_x, f_send, f_recv)
        for j in near_first:
            x = (p.x + j) % 4
            copy = copy_to(
                inp.at[:, pl.ds(pl.multiple_of(x * 1024 + p.c * 512, 512), 512)],
                inp_x.at[p.x, :, half(p.c)], i_send.at[j], i_recv.at[p.x], x, p.f,
            )
            copy.start()
            sent.append(copy)

        lax.fori_loop(0, index.shape[0] // 128, norms, 0)
        first = AllSum(place, pull, scratch[:n])
        second = AllSum(place, sums, scratch[n:])

        def chip_of(stage, turn):
            base, other = near_order(stage), near_order(stage + turn // 2)
            swap = turn % 2
            z = (p.z + base + (other - base) * swap) % 4
            y = (p.y + base + (other - base) * (1 - swap)) % 4
            return z * 4 + y

        for stages, groups in (((0,), ()), ((1,), (1,)), ((2, 3), (3, 2))):
            filled = 0
            for stage in stages:
                turns = 7 - 2 * stage

                def bring(turn, carry, stage=stage, filled=filled):
                    k = chip_of(stage, turn)
                    origin = k * 2 + p.c

                    def forward():
                        arrive(origin)
                        push(origin, p.partner, d_send.at[origin])

                    if stage:
                        forward()
                    else:
                        pl.when(jnp.logical_and(turn > 1, (turn + p.c) % 2 == 1))(forward)
                    arrive(k * 2 + 1 - p.c)
                    rows = pl.ds(pl.multiple_of(k * 64, 64), 64)
                    to = pl.ds(pl.multiple_of((filled + turn - 1) * 64, 64), 64)
                    batch[to, :] = query[rows, :]
                    batch_code[to, :] = code[rows, :]
                    return carry

                lax.fori_loop(1, 1 + turns, bring, 0)
                filled += turns
            total = owner_batch(filled * 64, batch, batch_code, index, scale, weight)
            chips = [chip_of(stage, turn) for stage in stages for turn in range(1, 8 - 2 * stage)]
            for part in range(4):
                cols = slice(part * 1024, part * 1024 + 1024)
                result = jnp.dot(
                    weight[: filled * 64, :], index[:, cols], preferred_element_type=jnp.float32
                ).astype(jnp.bfloat16)
                for t, k in enumerate(chips):
                    pull[pl.ds(pl.multiple_of(k * 64, 64), 64), cols] = result[64 * t : 64 * t + 64]
            for t, k in enumerate(chips):
                sums[pl.ds(pl.multiple_of(k * 64, 64), 64), :] = total[64 * t : 64 * t + 64]
                first.to_partner(k).start()
                second.to_partner(k).start()
            for group in groups:
                first.group(group)
                second.group(group)
        first.group(0)
        second.group(0)
        first.second()
        second.second()
        first.third()
        second.third()

        for j in near_first:
            x = (p.x + j) % 4
            region = inp_x.at[x, :, half(p.c)]
            copy_to(region, region, i_send.at[j], i_recv.at[x], x, p.f).wait_recv()
            copy = copy_to(region, region, pair_send.at[j], pair_recv.at[x], p.x, p.partner)
            copy.start()
            sent.append(copy)
        finish_hidden()
        finish_factors()
        pull_out[...] = first.last()
        sums_out[...] = second.last()
        for j in near_first:
            x = (p.x + j) % 4
            region = inp_x.at[x, :, half(1 - p.c)]
            copy_to(region, region, pair_send.at[j], pair_recv.at[x], p.x, p.partner).wait_recv()
        own_i.wait()
        for copy in sent:
            copy.wait_send()

        def pushed(k, carry):
            origin = k * 2 + p.c
            copy_to(block(origin), block(origin), d_send.at[origin], recv.at[origin], p.x,
                    p.partner).wait_send()
            return carry

        lax.fori_loop(0, 16, pushed, 0)

    bf = lambda *shape: jax.ShapeDtypeStruct(shape, jnp.bfloat16)
    return pl.pallas_call(
        kernel,
        out_shape=(
            jax.ShapeDtypeStruct((8, 4096), jnp.float32),
            jax.ShapeDtypeStruct((8, 128), jnp.float32),
            bf(4, *hidden.shape),
            bf(4, *factors.shape),
            bf(4, 256, 1024),
        ),
        in_specs=[ANY, VMEM, VMEM, ANY, ANY, ANY],
        out_specs=[VMEM, VMEM, ANY, ANY, ANY],
        scratch_shapes=[
            pltpu.VMEM((4, 8, 4096), jnp.bfloat16),
            pltpu.VMEM((1024, 4096), jnp.bfloat16),
            pltpu.VMEM((1024, 4096), jnp.bfloat16),
            pltpu.VMEM((1024, 128), jnp.float32),
            pltpu.VMEM((448, 4096), jnp.bfloat16),
            pltpu.VMEM((448, 8), jnp.int32),
            pltpu.VMEM((448, 512), jnp.bfloat16),
            pltpu.VMEM((1, 512), jnp.float32),
            DMA((4,)), DMA((4,)), DMA((4,)), DMA((16,)), DMA((32,)), DMA((32,)),
        ]
        + [DMA((4,))] * 8
        + AllSum.scratch(4096, jnp.bfloat16)
        + AllSum.scratch(128, jnp.float32),
        compiler_params=params(4, 52),
        name="attend",
    )(unit_rows, span_index, codes, hidden, factors, whole_input)


def gather_head(head_grad):
    def kernel(head, out, head_x, send, recv, hx_send, hx_recv):
        place = Place()
        p = place
        meet(place, True)
        gather = PlaneGather(place, head, out, row_block, send, recv)
        gather.start()
        wide = lambda x: pl.ds(pl.multiple_of(x * 1024, 1024), 1024)
        own = pltpu.make_async_copy(head.at[:, wide(p.x)], head_x.at[p.x], hx_send.at[0])
        own.start()
        sent = []
        for j in near_first:
            x = (p.x + j) % 4
            copy = copy_to(head.at[:, wide(x)], head_x.at[p.x], hx_send.at[j], hx_recv.at[p.x], x, p.f)
            copy.start()
            sent.append(copy)
        gather.relay()
        gather.finish()
        for j in near_first:
            x = (p.x + j) % 4
            copy_to(
                head_x.at[x], head_x.at[x], hx_send.at[j], hx_recv.at[x], x, p.f
            ).wait_recv()
        own.wait()
        for copy in sent:
            copy.wait_send()

    bf = lambda *shape: jax.ShapeDtypeStruct(shape, jnp.bfloat16)
    out, head_x = pl.pallas_call(
        kernel,
        out_shape=(bf(32, 8, 4096), bf(4, 8, 1024)),
        in_specs=[ANY],
        out_specs=[ANY] * 2,
        scratch_shapes=[DMA((32,)), DMA((32,)), DMA((4,)), DMA((4,))],
        compiler_params=params(2, 4),
        name="gather_head",
    )(head_grad)
    return out.reshape(256, 4096), head_x


def finish_links(partial, acts, head_x):
    def kernel(src, act, hx, out, act_x, head_cols, send, recv, x_send, x_recv, *scratch):
        place = Place()
        meet(place, True)
        finish_acts = across_gather(place, act, act_x, x_send, x_recv)
        scatter = PlaneScatter(place, src, column_block, scratch)
        scatter.start()
        gather = PlaneGather(
            place, hx, head_cols, lambda ref, f: ref.at[:, f], send, recv
        )
        gather.start()
        gather.relay()
        out[...] = scatter.middle().astype(jnp.bfloat16)
        gather.finish()
        finish_acts()

    bf = lambda *shape: jax.ShapeDtypeStruct(shape, jnp.bfloat16)
    return pl.pallas_call(
        kernel,
        out_shape=(bf(256, 128), bf(4, *acts.shape), bf(4, 32, 8, 1024)),
        in_specs=[VMEM, ANY, ANY],
        out_specs=[VMEM, ANY, ANY],
        scratch_shapes=[DMA((32,)), DMA((32,)), DMA((4,)), DMA((4,))]
        + PlaneScatter.scratch((256, 128)),
        compiler_params=params(3, 12),
        name="finish_links",
    )(partial, acts, head_x)


def shards(
    mlp_input,
    residual_in,
    gate_weight,
    up_weight,
    down_weight,
    span_index,
    positive_keys,
    request_rows,
    request_counts,
    negative_slots,
):
    dp_count = lax.axis_size("dp")
    fsdp_count = lax.axis_size("fsdp")
    owners = dp_count * fsdp_count
    slot_cap = request_rows.shape[2]
    rows, width = positive_keys.shape

    shape = (1, 1, slot_cap, owners)
    slot_ids = lax.broadcasted_iota(jnp.int32, shape, 3) * slot_cap
    slot_ids += lax.broadcasted_iota(jnp.int32, shape, 2)
    used = jnp.any(negative_slots[:, :, None, None] == slot_ids, axis=1).astype(jnp.int32)
    table = jnp.sum(used * (lax.broadcasted_iota(jnp.int32, used.shape, 0) + 1), axis=0) - 1
    whole_input, tables = gather_input(mlp_input, table)

    me = lax.axis_index("dp") * fsdp_count + lax.axis_index("fsdp")
    mine = lax.broadcasted_iota(jnp.int32, tables.shape, 3) == me
    user = jnp.sum(jnp.where(mine, tables, 0), axis=3).reshape(owners, slot_cap)
    requests = jnp.where(
        lax.broadcasted_iota(jnp.int32, (owners, slot_cap), 1) < request_counts,
        request_rows[:, 0, :],
        -1,
    )
    requests = requests.reshape(dp_count, fsdp_count, slot_cap).transpose(1, 0, 2)
    requests = requests.reshape(owners, slot_cap)
    ranks = lax.broadcasted_iota(jnp.int32, (1, rows, 1), 1)
    codes = jnp.where(user[:, None, :] == ranks, requests[:, None, :], -1)
    codes = codes.reshape(owners * rows, slot_cap)

    gate_act = jnp.dot(whole_input, gate_weight, preferred_element_type=jnp.float32)
    up_act = jnp.dot(whole_input, up_weight, preferred_element_type=jnp.float32)
    sigmoid_gate = jax.nn.sigmoid(gate_act)
    silu_gate = gate_act * sigmoid_gate
    hidden = (silu_gate * up_act).astype(jnp.bfloat16)
    branch = scatter_branch(jnp.dot(hidden, down_weight, preferred_element_type=jnp.bfloat16))
    top_state = branch + residual_in.astype(jnp.float32)
    row_norm = jnp.sqrt(jnp.sum(top_state * top_state, axis=-1) + eps)
    unit_rows = top_state / row_norm[:, None]
    positive = positive_keys.astype(jnp.float32)
    positive_unit = positive / jnp.sqrt(jnp.sum(positive * positive, axis=-1, keepdims=True) + eps)
    positive_score = inverse_temp * jnp.sum(unit_rows * positive_unit, axis=-1)

    gate_factor = up_act * (sigmoid_gate * (1.0 + gate_act * (1.0 - sigmoid_gate)))
    pull, sums, hidden_x, factors_x, input_x = attend(
        unit_rows.astype(jnp.bfloat16),
        span_index,
        codes,
        hidden.T,
        jnp.stack([gate_factor.T, silu_gate.T]).astype(jnp.bfloat16),
        whole_input,
    )
    positive_weight = jnp.exp(positive_score)
    exp_total = sums[:, 0] + positive_weight
    query_loss = jnp.log(exp_total) - positive_score
    positive_coeff = positive_weight / exp_total - 1.0
    inner = sums[:, 1] / exp_total + positive_coeff * positive_score
    pull = inverse_temp * (pull / exp_total[:, None] + positive_coeff[:, None] * positive_unit)
    head_grad = ((pull - inner[:, None] * unit_rows) / row_norm[:, None]).astype(jnp.bfloat16)

    gathered_grad, head_x = gather_head(head_grad)
    hidden_grad = lax.dot_general(
        gathered_grad, down_weight, contract_last, preferred_element_type=jnp.float32
    )
    gate_grad_act = (hidden_grad * gate_factor).astype(jnp.bfloat16)
    up_grad_act = (hidden_grad * silu_gate).astype(jnp.bfloat16)
    input_term = lax.dot_general(
        gate_grad_act, gate_weight, contract_last, preferred_element_type=jnp.float32
    ) + lax.dot_general(up_grad_act, up_weight, contract_last, preferred_element_type=jnp.float32)
    input_grad, hidden_grad_x, head_cols = finish_links(
        input_term.astype(jnp.bfloat16), hidden_grad.T.astype(jnp.bfloat16), head_x
    )
    over_groups = (((0, 2), (0, 1)), ((), ()))
    hidden_grad_x = hidden_grad_x.astype(jnp.float32)
    weight_grads = [
        lax.dot_general(
            (hidden_grad_x * factors_x[:, k].astype(jnp.float32)).astype(jnp.bfloat16),
            input_x,
            over_groups,
            preferred_element_type=jnp.float32,
        ).astype(jnp.bfloat16)
        for k in range(2)
    ]
    down_grad = lax.dot_general(
        hidden_x, head_cols.reshape(4, 256, 1024), over_groups, preferred_element_type=jnp.float32
    ).astype(jnp.bfloat16)
    return (query_loss, input_grad, weight_grads[0].T, weight_grads[1].T, down_grad)


def solution(mesh):
    return jax.shard_map(
        shards,
        mesh=mesh,
        in_specs=(
            P("dp", "fsdp"),
            P(("dp", "fsdp"), None),
            P(None, "fsdp"),
            P(None, "fsdp"),
            P("fsdp", None),
            P(("dp", "fsdp"), None),
            P(("dp", "fsdp"), None),
            P(None, ("dp", "fsdp"), None),
            P(None, ("dp", "fsdp")),
            P(("dp", "fsdp"), None),
        ),
        out_specs=(
            P(("dp", "fsdp")),
            P("dp", "fsdp"),
            P("dp", "fsdp"),
            P("dp", "fsdp"),
            P("fsdp", "dp"),
        ),
        check_vma=False,
    )
```

```python
import functools

import jax
import jax.numpy as jnp
from jax import lax
from jax.experimental import pallas as pl
from jax.experimental.pallas import tpu as pltpu
from jax.sharding import PartitionSpec as P

inverse_temp = 50.0
eps = 1e-06
contract_first = (((0,), (0,)), ((), ()))
contract_last = (((1,), (1,)), ((), ()))
ANY = pl.BlockSpec(memory_space=pl.ANY)
VMEM = pl.BlockSpec(memory_space=pltpu.VMEM)
DMA = pltpu.SemaphoreType.DMA
near_first = (1, 3, 2)


class Place:
    def __init__(self):
        self.x = lax.axis_index("dp")
        self.f = lax.axis_index("fsdp")
        self.z = self.f // 8
        self.y = (self.f // 2) % 4
        self.c = self.f % 2
        self.a = self.y * (1 - self.c) + self.z * self.c
        self.b = self.z * (1 - self.c) + self.y * self.c
        self.partner = self.f + 1 - 2 * self.c

    def at(self, b, a, c):
        z = b * (1 - c) + a * c
        y = a * (1 - c) + b * c
        return (z * 4 + y) * 2 + c

    def a_peer(self, j):
        return self.at(self.b, (self.a + j) % 4, self.c)

    def b_peer(self, j):
        return self.at((self.b + j) % 4, self.a, self.c)


def copy_to(src, dst, send, recv, x, f):
    return pltpu.make_async_remote_copy(
        src_ref=src,
        dst_ref=dst,
        send_sem=send,
        recv_sem=recv,
        device_id=(x, f),
        device_id_type=pl.DeviceIdType.MESH,
    )


def meet(place, across):
    barrier = pltpu.get_barrier_semaphore()
    peers = [(place.x, place.partner)]
    peers += [(place.x, place.a_peer(j)) for j in near_first]
    peers += [(place.x, place.b_peer(j)) for j in near_first]
    if across:
        peers += [((place.x + j) % 4, place.f) for j in near_first]
    for x, f in peers:
        pl.semaphore_signal(barrier, inc=1, device_id=(x, f), device_id_type=pl.DeviceIdType.MESH)
    pl.semaphore_wait(barrier, len(peers))


class PlaneGather:
    def __init__(self, place, src, out, view, send, recv):
        self.place, self.src, self.out, self.view = place, src, out, view
        self.send, self.recv = send, recv
        self.sent = []

    def push(self, origin, f, half=None, src=None):
        to = self.view(self.out, origin, half)
        copy = copy_to(
            to if src is None else src,
            to,
            self.send.at[len(self.sent)],
            self.recv.at[half or 0, origin],
            self.place.x,
            f,
        )
        copy.start()
        self.sent.append(copy)

    def arrive(self, origin, halves=(None,)):
        for half in halves:
            block = self.view(self.out, origin, half)
            copy_to(
                block, block, self.send.at[0], self.recv.at[half or 0, origin], self.place.x,
                self.place.partner,
            ).wait_recv()

    def start(self):
        p = self.place
        self.own = pltpu.make_async_copy(self.src, self.view(self.out, p.f, None), self.send.at[40])
        for peer in (p.a_peer(1), p.a_peer(3), p.b_peer(1), p.b_peer(3), p.partner):
            self.push(p.f, peer, src=self.src)
        self.own.start()

    def relay(self):
        p = self.place
        for j in near_first:
            origin = p.a_peer(j)
            if j == 2:
                self.arrive(origin, (0, 1))
            else:
                self.arrive(origin)
                self.push(origin, p.a_peer(4 - j), half=(3 - j) // 2)
            for peer in (p.b_peer(1), p.b_peer(3), p.partner):
                self.push(origin, peer)

    def finish(self):
        p = self.place
        for j in (0,) + near_first:
            for i in (1, 3):
                origin = p.at((p.b + i) % 4, (p.a + j) % 4, p.c)
                self.arrive(origin)
                self.push(origin, p.b_peer(4 - i), half=(3 - i) // 2)
                self.push(origin, p.partner)
        for j in (0,) + near_first:
            origin = p.at((p.b + 2) % 4, (p.a + j) % 4, p.c)
            self.arrive(origin, (0, 1))
            self.push(origin, p.partner)
        for j in (0,) + near_first:
            for i in (0,) + near_first:
                z, y = (p.z + i) % 4, (p.y + j) % 4
                self.arrive((z * 4 + y) * 2 + 1 - p.c)
        self.own.wait()
        for copy in self.sent:
            copy.wait_send()


gather_sems = [DMA((41,)), DMA((2, 32))]


class RingSum:
    def __init__(self, x, me, peer, parts, axis, scratch):
        self.x, self.me, self.peer, self.parts, self.axis = x, me, peer, parts, axis
        self.relay, self.got, self.relay_send, self.relay_recv, self.send, self.recv = scratch

    @staticmethod
    def scratch(part, dtype):
        return [pltpu.VMEM((2,) + part, dtype), pltpu.VMEM((2,) + part, dtype),
                DMA((2,)), DMA((2,)), DMA((4,)), DMA((4,))]

    def cut(self, ref, at, half):
        index = [slice(None)] * (len(ref.shape) - 1)
        size = ref.shape[1 + self.axis] // 2
        index[self.axis] = slice(half * size, half * size + size)
        return ref.at[(at,) + tuple(index)]

    def near_copy(self, side, half):
        step = 3 if side else 1
        return copy_to(
            self.cut(self.parts, (self.me + step) % 4, half), self.cut(self.got, side, half),
            self.send.at[side * 2 + half], self.recv.at[side * 2 + half], self.x, self.peer(step),
        )

    def far_copy(self, side):
        step = 3 if side else 1
        return copy_to(
            self.cut(self.parts, (self.me + 2) % 4, side), self.cut(self.relay, side, side),
            self.relay_send.at[side], self.relay_recv.at[side], self.x, self.peer(step),
        )

    def near(self, side):
        self.near_copy(side, 1 - side).start()

    def far(self):
        self.far_copy(0).start()
        self.far_copy(1).start()

    def combine(self):
        for side in range(2):
            self.far_copy(side).wait_recv()
            own = self.cut(self.parts, (self.me + (3 if side else 1)) % 4, side)
            got = self.cut(self.relay, side, side)
            for row in range(own.shape[0]):
                total = own[row].astype(jnp.float32) + got[row].astype(jnp.float32)
                own[row] = total.astype(own.dtype)
            self.near_copy(side, side).start()

    def arrive(self):
        for side in range(2):
            for half in range(2):
                self.near_copy(side, half).wait_recv()

    def total(self, row):
        return (
            self.parts[self.me, row].astype(jnp.float32)
            + self.got[0, row].astype(jnp.float32)
            + self.got[1, row].astype(jnp.float32)
        )

    def close(self):
        for side in range(2):
            self.far_copy(side).wait_send()
            for half in range(2):
                self.near_copy(side, half).wait_send()


class PlaneScatter:
    def __init__(self, place, src, view, axis, scratch):
        self.place, self.src, self.view = place, src, view
        p = place
        self.got1, self.sum1, self.sum2, self.send1, self.recv1 = scratch[:5]
        self.ring_b = RingSum(p.x, p.b, p.b_peer, self.sum1, axis + 1, scratch[5:11])
        self.ring_a = RingSum(p.x, p.a, p.a_peer, self.sum2, axis + 1, scratch[11:17])

    @staticmethod
    def scratch(block, dtype=jnp.bfloat16):
        wide = lambda *lead: pltpu.VMEM(lead + block, dtype)
        return (
            [wide(16), wide(4, 4), wide(4, 1), DMA((16,)), DMA((16,))]
            + RingSum.scratch((4,) + block, dtype)
            + RingSum.scratch((1,) + block, dtype)
        )

    def to_partner(self, b, a):
        p = self.place
        k = b * 4 + a
        return copy_to(self.view(self.src, p.at(b, a, 1 - p.c), None), self.got1.at[k],
                       self.send1.at[k], self.recv1.at[k], p.x, p.partner)

    def start(self):
        p = self.place
        for i in (2, 1, 3, 0):
            for a in range(4):
                self.to_partner((p.a + i) % 4, a).start()

    def middle(self):
        p = self.place
        for i in (2, 1, 3, 0):
            b = (p.b + i) % 4
            for a in range(4):
                k = b * 4 + a
                got = self.got1.at[k]
                copy_to(got, got, self.send1.at[k], self.recv1.at[k], p.x, p.partner).wait_recv()
                own = self.view(self.src, p.at(b, a, p.c), None)[...].astype(jnp.float32)
                self.sum1[b, a] = (own + got[...].astype(jnp.float32)).astype(self.sum1.dtype)
            if i == 2:
                self.ring_b.far()
            elif i:
                self.ring_b.near(i // 2)
        self.ring_b.combine()
        self.ring_b.arrive()
        for j in (2, 1, 3, 0):
            a = (p.a + j) % 4
            self.sum2[a, 0] = self.ring_b.total(a).astype(self.sum2.dtype)
            if j == 2:
                self.ring_a.far()
            elif j:
                self.ring_a.near(j // 2)
        self.ring_a.combine()
        self.ring_a.arrive()
        total = self.ring_a.total(0)
        self.ring_b.close()
        self.ring_a.close()
        for i in range(4):
            for a in range(4):
                self.to_partner(i, a).wait_send()
        return total


def across_gather(place, src, out, send, recv):
    own = pltpu.make_async_copy(src, out.at[place.x], send.at[0])
    own.start()
    sent = []
    for j in near_first:
        copy = copy_to(src, out.at[place.x], send.at[j], recv.at[place.x], (place.x + j) % 4, place.f)
        copy.start()
        sent.append(copy)

    def finish():
        for j in near_first:
            x = (place.x + j) % 4
            copy_to(out.at[x], out.at[x], send.at[j], recv.at[x], x, place.f).wait_recv()
        own.wait()
        for copy in sent:
            copy.wait_send()

    return finish


def params(collective_id, mib):
    return pltpu.CompilerParams(
        collective_id=collective_id, has_side_effects=True, vmem_limit_bytes=mib * 1024 * 1024
    )


def part_of(size, half):
    return slice(None) if half is None else slice(half * size // 2, (half + 1) * size // 2)


def column_block(ref, f, half):
    return ref.at[part_of(256, half), pl.ds(pl.multiple_of(f * 128, 128), 128)]


def row_block(ref, f, half):
    return ref.at[f, :, part_of(4096, half)]


def lead_block(ref, f, half):
    return ref.at[f, part_of(4, half)]


def second_block(ref, f, half):
    return ref.at[part_of(4, half), f]


def gather_input(mlp_input, table):
    def kernel(src, tab, out, tab_x, tab_all, send, recv, x_send, x_recv, t_send, t_recv):
        place = Place()
        meet(place, True)
        finish_table = across_gather(place, tab, tab_x, x_send, x_recv)
        gather = PlaneGather(place, src, out, column_block, send, recv)
        gather.start()
        finish_table()
        tables = PlaneGather(place, tab_x, tab_all, lead_block, t_send, t_recv)
        tables.start()
        gather.relay()
        tables.relay()
        gather.finish()
        tables.finish()

    rows, cols = mlp_input.shape
    ints = lambda *lead: jax.ShapeDtypeStruct(lead + table.shape, jnp.int32)
    out, _, tables = pl.pallas_call(
        kernel,
        out_shape=(jax.ShapeDtypeStruct((rows, cols * 32), jnp.bfloat16), ints(4), ints(32, 4)),
        in_specs=[ANY] * 2,
        out_specs=[ANY] * 3,
        scratch_shapes=gather_sems + [DMA((4,)), DMA((4,))] + gather_sems,
        compiler_params=params(0, 4),
        name="gather_input",
    )(mlp_input, table)
    return out, tables


def scatter_branch(partial):
    def kernel(src, out, *scratch):
        place = Place()
        meet(place, False)
        scatter = PlaneScatter(place, src, row_block, 1, scratch)
        scatter.start()
        out[...] = scatter.middle()

    return pl.pallas_call(
        kernel,
        out_shape=jax.ShapeDtypeStruct((8, 4096), jnp.float32),
        in_specs=[VMEM],
        out_specs=VMEM,
        scratch_shapes=PlaneScatter.scratch((8, 4096)),
        compiler_params=params(1, 12),
        name="scatter_branch",
    )(partial.reshape(32, 8, 4096))


def near_order(m):
    return m + m // 2 - 2 * (m // 3)


def owner_batch(count, batch_ref, code_ref, index_ref, scale_ref, weight_ref):
    raw = lax.dot_general(
        batch_ref[:count, :], index_ref[...], contract_last, preferred_element_type=jnp.float32
    )
    scale = scale_ref[...]
    scores = inverse_temp * raw * scale
    here = lax.broadcasted_iota(jnp.int32, scores.shape, 1)
    uses = jnp.zeros(scores.shape, jnp.float32)
    codes = code_ref[:count, :]
    for slot in range(8):
        uses += jnp.where(codes[:, slot : slot + 1] == here, 1.0, 0.0)
    weights = uses * jnp.exp(scores)
    exps = jnp.sum(weights, axis=1, keepdims=True)
    inners = jnp.sum(weights * scores, axis=1, keepdims=True)
    lane = lax.broadcasted_iota(jnp.int32, (count, 128), 1)
    weight_ref[:count, :] = (weights * scale).astype(jnp.bfloat16)
    return jnp.where(lane == 0, exps, jnp.where(lane == 1, inners, 0.0))


class AllSum:
    def __init__(self, place, src, scratch):
        self.place, self.src = place, src
        p = place
        (self.got1, self.sum1, self.sum2, self.stage, self.got4, self.send1, self.recv1, self.send4,
         self.recv4) = scratch[:9]
        self.ring_b = RingSum(p.x, p.b, p.b_peer, self.sum1, 1, scratch[9:15])
        self.ring_a = RingSum(p.x, p.a, p.a_peer, self.sum2, 1, scratch[15:21])

    @staticmethod
    def scratch(width, dtype):
        wide = lambda *lead: pltpu.VMEM(lead + (32, width), dtype)
        last = pltpu.VMEM((4, 8, width), dtype)
        return (
            [wide(16), wide(4, 4), wide(4, 1), last, last, DMA((16,)), DMA((16,)), DMA((4,)),
             DMA((4,))]
            + RingSum.scratch((4, 32, width), dtype)
            + RingSum.scratch((1, 32, width), dtype)
        )

    def rows(self, k, c):
        return self.src.at[pl.ds(pl.multiple_of(k * 64 + c * 32, 32), 32), :]

    def to_partner(self, k):
        p = self.place
        return copy_to(self.rows(k, 1 - p.c), self.got1.at[k], self.send1.at[k], self.recv1.at[k],
                       p.x, p.partner)

    def to_x(self, j):
        p = self.place
        x = (p.x + j) % 4
        return copy_to(self.stage.at[x], self.got4.at[p.x], self.send4.at[j], self.recv4.at[p.x],
                       x, p.f)

    def group(self, i):
        p = self.place
        b = (p.b + i) % 4

        def add(a, carry):
            k = p.at(b, a, p.c) // 2
            got = self.got1.at[k]
            copy_to(got, got, self.send1.at[k], self.recv1.at[k], p.x, p.partner).wait_recv()
            own = self.rows(k, p.c)[...].astype(jnp.float32)
            self.sum1[b, a] = (own + got[...].astype(jnp.float32)).astype(self.sum1.dtype)
            return carry

        lax.fori_loop(0, 4, add, 0)
        if i == 2:
            self.ring_b.far()
        elif i:
            self.ring_b.near(i // 2)

    def second(self):
        p = self.place
        self.ring_b.arrive()
        for j in (2, 1, 3, 0):
            a = (p.a + j) % 4
            self.sum2[a, 0] = self.ring_b.total(a).astype(self.sum2.dtype)
            if j == 2:
                self.ring_a.far()
            elif j:
                self.ring_a.near(j // 2)
        self.ring_a.combine()

    def third(self):
        self.ring_a.arrive()
        total = self.ring_a.total(0)
        for x in range(4):
            self.stage[x] = total[8 * x : 8 * x + 8].astype(self.stage.dtype)
        for j in near_first:
            self.to_x(j).start()

    def last(self):
        p = self.place
        own = self.stage[p.x].astype(jnp.float32)
        for j in near_first:
            x = (p.x + j) % 4
            got = self.got4.at[x]
            copy_to(got, got, self.send4.at[j], self.recv4.at[x], x, p.f).wait_recv()
            own += got[...].astype(jnp.float32)
        for j in near_first:
            self.to_x(j).wait_send()
        self.ring_b.close()
        self.ring_a.close()

        def sent(k, carry):
            self.to_partner(k).wait_send()
            return carry

        lax.fori_loop(0, 16, sent, 0)
        return own


def attend(unit_rows, span_index, codes, hidden, factors, whole_input):
    n = 21

    def kernel(unit, index, code, hid, fac, inp,
               pull_out, sums_out, hid_x, fac_x, inp_x,
               unit_x, query, pull, sums, batch, batch_code, weight, scale, u_send, u_recv, a_send, b_send, c_send, d_send, recv,
               h_send, h_recv, f_send, f_recv, i_send, i_recv, pair_send, pair_recv, *scratch):
        p = place = Place()
        meet(place, True)

        finish_unit = across_gather(place, unit, unit_x, u_send, u_recv)
        block = lambda f: query.at[pl.ds(pl.multiple_of(f * 32, 32), 32), :]
        half = lambda c: pl.ds(pl.multiple_of(c * 512, 512), 512)
        own_i = pltpu.make_async_copy(
            inp.at[:, pl.ds(pl.multiple_of(p.x * 1024, 1024), 1024)], inp_x.at[p.x], i_send.at[0]
        )
        own_i.start()
        finish_unit()
        block(p.f)[...] = jnp.concatenate(
            [unit_x[x].astype(jnp.float32) for x in range(4)], axis=0
        ).astype(jnp.bfloat16)

        def half_block(f, half):
            return query.at[pl.ds(pl.multiple_of(f * 32 + half * 16, 16), 16), :]

        def push(origin, f, send):
            copy = copy_to(block(origin), block(origin), send, recv.at[0, origin], p.x, f)
            copy.start()
            return copy

        def push_half(origin, f, half, send):
            part = half_block(origin, half)
            copy = copy_to(part, part, send, recv.at[half, origin], p.x, f)
            copy.start()
            return copy

        def arrive(origin):
            copy_to(block(origin), block(origin), d_send.at[origin], recv.at[0, origin], p.x,
                    p.partner).wait_recv()

        def arrive_halves(origin):
            for half in range(2):
                part = half_block(origin, half)
                copy_to(part, part, d_send.at[origin], recv.at[half, origin], p.x,
                        p.partner).wait_recv()

        sent = []
        for j in (1, 3):
            sent.append(push(p.f, p.a_peer(j), a_send.at[j]))
        for i in (1, 3):
            sent.append(push(p.f, p.b_peer(i), b_send.at[i]))
        push(p.f, p.partner, d_send.at[p.f])

        def norms(part, carry):
            rows = pl.ds(pl.multiple_of(part * 128, 128), 128)
            wide = index[rows, :].astype(jnp.float32)
            total = jnp.sum(wide * wide, axis=1, keepdims=True)
            row = lax.broadcasted_iota(jnp.int32, (128, 128), 0)
            col = lax.broadcasted_iota(jnp.int32, (128, 128), 1)
            across = jnp.sum(jnp.where(row == col, total, 0.0), axis=0, keepdims=True)
            scale[:, rows] = lax.rsqrt(across + eps)
            return carry

        for j in near_first:
            origin = p.a_peer(j)
            if j == 2:
                arrive_halves(origin)
            else:
                arrive(origin)
                side = (3 - j) // 2
                sent.append(push_half(origin, p.a_peer(4 - j), side, a_send.at[2 * side]))
            for i in (1, 3):
                sent.append(push(origin, p.b_peer(i), b_send.at[4 * j + i]))
            push(origin, p.partner, d_send.at[origin])

        finish_hidden = across_gather(place, hid, hid_x, h_send, h_recv)
        finish_factors = across_gather(place, fac, fac_x, f_send, f_recv)
        for j in near_first:
            x = (p.x + j) % 4
            copy = copy_to(
                inp.at[:, pl.ds(pl.multiple_of(x * 1024 + p.c * 512, 512), 512)],
                inp_x.at[p.x, :, half(p.c)], i_send.at[j], i_recv.at[p.x], x, p.f,
            )
            copy.start()
            sent.append(copy)

        lax.fori_loop(0, index.shape[0] // 128, norms, 0)
        first = AllSum(place, pull, scratch[:n])
        second = AllSum(place, sums, scratch[n:])

        def chip_of(stage, turn):
            base, other = near_order(stage), near_order(stage + turn // 2)
            swap = turn % 2
            z = (p.z + base + (other - base) * swap) % 4
            y = (p.y + base + (other - base) * (1 - swap)) % 4
            return z * 4 + y

        for stages, groups in (((0,), ()), ((1,), (1,)), ((2, 3), (3, 2))):
            filled = 0
            for stage in stages:
                turns = 7 - 2 * stage

                def bring(turn, carry, stage=stage, filled=filled):
                    k = chip_of(stage, turn)
                    origin = k * 2 + p.c

                    away = (origin // 8 - p.z) * (1 - p.c) + (origin // 2 % 4 - p.y) * p.c
                    away = (away + 4) % 4

                    def forward():
                        @pl.when(away == 2)
                        def _():
                            arrive_halves(origin)

                        @pl.when(away != 2)
                        def _():
                            arrive(origin)
                            side = (3 - away) // 2
                            push_half(origin, p.at((p.b + 4 - away) % 4, p.a, p.c), side,
                                      c_send.at[origin])

                        push(origin, p.partner, d_send.at[origin])

                    if stage:
                        forward()
                    else:
                        pl.when(jnp.logical_and(turn > 1, (turn + p.c) % 2 == 1))(forward)
                    arrive(k * 2 + 1 - p.c)
                    rows = pl.ds(pl.multiple_of(k * 64, 64), 64)
                    to = pl.ds(pl.multiple_of((filled + turn - 1) * 64, 64), 64)
                    batch[to, :] = query[rows, :]
                    batch_code[to, :] = code[rows, :]
                    return carry

                lax.fori_loop(1, 1 + turns, bring, 0)
                filled += turns
            total = owner_batch(filled * 64, batch, batch_code, index, scale, weight)
            chips = [chip_of(stage, turn) for stage in stages for turn in range(1, 8 - 2 * stage)]
            for part in range(4):
                cols = slice(part * 1024, part * 1024 + 1024)
                result = jnp.dot(
                    weight[: filled * 64, :], index[:, cols], preferred_element_type=jnp.float32
                ).astype(jnp.bfloat16)
                for t, k in enumerate(chips):
                    pull[pl.ds(pl.multiple_of(k * 64, 64), 64), cols] = result[64 * t : 64 * t + 64]
            for t, k in enumerate(chips):
                sums[pl.ds(pl.multiple_of(k * 64, 64), 64), :] = total[64 * t : 64 * t + 64]
                first.to_partner(k).start()
                second.to_partner(k).start()
            for group in groups:
                first.group(group)
                second.group(group)
        first.group(0)
        second.group(0)
        first.ring_b.combine()
        second.ring_b.combine()
        first.second()
        second.second()
        first.third()
        second.third()

        for j in near_first:
            x = (p.x + j) % 4
            region = inp_x.at[x, :, half(p.c)]
            copy_to(region, region, i_send.at[j], i_recv.at[x], x, p.f).wait_recv()
            copy = copy_to(region, region, pair_send.at[j], pair_recv.at[x], p.x, p.partner)
            copy.start()
            sent.append(copy)
        finish_hidden()
        finish_factors()
        pull_out[...] = first.last()
        sums_out[...] = second.last()
        for j in near_first:
            x = (p.x + j) % 4
            region = inp_x.at[x, :, half(1 - p.c)]
            copy_to(region, region, pair_send.at[j], pair_recv.at[x], p.x, p.partner).wait_recv()
        own_i.wait()
        for copy in sent:
            copy.wait_send()

        def pushed(k, carry):
            origin = k * 2 + p.c
            copy_to(block(origin), block(origin), d_send.at[origin], recv.at[0, origin], p.x,
                    p.partner).wait_send()
            return carry

        lax.fori_loop(0, 16, pushed, 0)

        def handed(a, carry):
            for i in (1, 3):
                origin = p.at((p.b + i) % 4, a, p.c)
                part = half_block(origin, (3 - i) // 2)
                copy_to(part, part, c_send.at[origin], recv.at[(3 - i) // 2, origin], p.x,
                        p.partner).wait_send()
            return carry

        lax.fori_loop(0, 4, handed, 0)

    bf = lambda *shape: jax.ShapeDtypeStruct(shape, jnp.bfloat16)
    return pl.pallas_call(
        kernel,
        out_shape=(
            jax.ShapeDtypeStruct((8, 4096), jnp.float32),
            jax.ShapeDtypeStruct((8, 128), jnp.float32),
            bf(4, *hidden.shape),
            bf(4, *factors.shape),
            bf(4, 256, 1024),
        ),
        in_specs=[ANY, VMEM, VMEM, ANY, ANY, ANY],
        out_specs=[VMEM, VMEM, ANY, ANY, ANY],
        scratch_shapes=[
            pltpu.VMEM((4, 8, 4096), jnp.bfloat16),
            pltpu.VMEM((1024, 4096), jnp.bfloat16),
            pltpu.VMEM((1024, 4096), jnp.bfloat16),
            pltpu.VMEM((1024, 128), jnp.float32),
            pltpu.VMEM((448, 4096), jnp.bfloat16),
            pltpu.VMEM((448, 8), jnp.int32),
            pltpu.VMEM((448, 512), jnp.bfloat16),
            pltpu.VMEM((1, 512), jnp.float32),
            DMA((4,)), DMA((4,)), DMA((4,)), DMA((16,)), DMA((32,)), DMA((32,)), DMA((2, 32)),
        ]
        + [DMA((4,))] * 8
        + AllSum.scratch(4096, jnp.bfloat16)
        + AllSum.scratch(128, jnp.float32),
        compiler_params=params(4, 52),
        name="attend",
    )(unit_rows, span_index, codes, hidden, factors, whole_input)


def gather_head(head_grad):
    def kernel(head, out, head_x, send, recv, hx_send, hx_recv):
        place = Place()
        p = place
        meet(place, True)
        gather = PlaneGather(place, head, out, row_block, send, recv)
        gather.start()
        wide = lambda x: pl.ds(pl.multiple_of(x * 1024, 1024), 1024)
        own = pltpu.make_async_copy(head.at[:, wide(p.x)], head_x.at[p.x], hx_send.at[0])
        own.start()
        sent = []
        for j in near_first:
            x = (p.x + j) % 4
            copy = copy_to(head.at[:, wide(x)], head_x.at[p.x], hx_send.at[j], hx_recv.at[p.x], x, p.f)
            copy.start()
            sent.append(copy)
        gather.relay()
        gather.finish()
        for j in near_first:
            x = (p.x + j) % 4
            copy_to(
                head_x.at[x], head_x.at[x], hx_send.at[j], hx_recv.at[x], x, p.f
            ).wait_recv()
        own.wait()
        for copy in sent:
            copy.wait_send()

    bf = lambda *shape: jax.ShapeDtypeStruct(shape, jnp.bfloat16)
    out, head_x = pl.pallas_call(
        kernel,
        out_shape=(bf(32, 8, 4096), bf(4, 8, 1024)),
        in_specs=[ANY],
        out_specs=[ANY] * 2,
        scratch_shapes=gather_sems + [DMA((4,)), DMA((4,))],
        compiler_params=params(2, 4),
        name="gather_head",
    )(head_grad)
    return out.reshape(256, 4096), head_x


def finish_links(partial, acts, head_x):
    def kernel(src, act, hx, out, act_x, head_cols, send, recv, x_send, x_recv, *scratch):
        place = Place()
        meet(place, True)
        finish_acts = across_gather(place, act, act_x, x_send, x_recv)
        scatter = PlaneScatter(place, src, column_block, 0, scratch)
        scatter.start()
        gather = PlaneGather(place, hx, head_cols, second_block, send, recv)
        gather.start()
        gather.relay()
        out[...] = scatter.middle().astype(jnp.bfloat16)
        gather.finish()
        finish_acts()

    bf = lambda *shape: jax.ShapeDtypeStruct(shape, jnp.bfloat16)
    return pl.pallas_call(
        kernel,
        out_shape=(bf(256, 128), bf(4, *acts.shape), bf(4, 32, 8, 1024)),
        in_specs=[VMEM, ANY, ANY],
        out_specs=[VMEM, ANY, ANY],
        scratch_shapes=gather_sems
        + [DMA((4,)), DMA((4,))]
        + PlaneScatter.scratch((256, 128)),
        compiler_params=params(3, 12),
        name="finish_links",
    )(partial, acts, head_x)


def shards(
    mlp_input,
    residual_in,
    gate_weight,
    up_weight,
    down_weight,
    span_index,
    positive_keys,
    request_rows,
    request_counts,
    negative_slots,
):
    dp_count = lax.axis_size("dp")
    fsdp_count = lax.axis_size("fsdp")
    owners = dp_count * fsdp_count
    slot_cap = request_rows.shape[2]
    rows, width = positive_keys.shape

    shape = (1, 1, slot_cap, owners)
    slot_ids = lax.broadcasted_iota(jnp.int32, shape, 3) * slot_cap
    slot_ids += lax.broadcasted_iota(jnp.int32, shape, 2)
    used = jnp.any(negative_slots[:, :, None, None] == slot_ids, axis=1).astype(jnp.int32)
    table = jnp.sum(used * (lax.broadcasted_iota(jnp.int32, used.shape, 0) + 1), axis=0) - 1
    whole_input, tables = gather_input(mlp_input, table)

    me = lax.axis_index("dp") * fsdp_count + lax.axis_index("fsdp")
    mine = lax.broadcasted_iota(jnp.int32, tables.shape, 3) == me
    user = jnp.sum(jnp.where(mine, tables, 0), axis=3).reshape(owners, slot_cap)
    requests = jnp.where(
        lax.broadcasted_iota(jnp.int32, (owners, slot_cap), 1) < request_counts,
        request_rows[:, 0, :],
        -1,
    )
    requests = requests.reshape(dp_count, fsdp_count, slot_cap).transpose(1, 0, 2)
    requests = requests.reshape(owners, slot_cap)
    ranks = lax.broadcasted_iota(jnp.int32, (1, rows, 1), 1)
    codes = jnp.where(user[:, None, :] == ranks, requests[:, None, :], -1)
    codes = codes.reshape(owners * rows, slot_cap)

    gate_act = jnp.dot(whole_input, gate_weight, preferred_element_type=jnp.float32)
    up_act = jnp.dot(whole_input, up_weight, preferred_element_type=jnp.float32)
    sigmoid_gate = jax.nn.sigmoid(gate_act)
    silu_gate = gate_act * sigmoid_gate
    hidden = (silu_gate * up_act).astype(jnp.bfloat16)
    branch = scatter_branch(jnp.dot(hidden, down_weight, preferred_element_type=jnp.bfloat16))
    top_state = branch + residual_in.astype(jnp.float32)
    row_norm = jnp.sqrt(jnp.sum(top_state * top_state, axis=-1) + eps)
    unit_rows = top_state / row_norm[:, None]
    positive = positive_keys.astype(jnp.float32)
    positive_unit = positive / jnp.sqrt(jnp.sum(positive * positive, axis=-1, keepdims=True) + eps)
    positive_score = inverse_temp * jnp.sum(unit_rows * positive_unit, axis=-1)

    gate_factor = up_act * (sigmoid_gate * (1.0 + gate_act * (1.0 - sigmoid_gate)))
    pull, sums, hidden_x, factors_x, input_x = attend(
        unit_rows.astype(jnp.bfloat16),
        span_index,
        codes,
        hidden.T,
        jnp.stack([gate_factor.T, silu_gate.T]).astype(jnp.bfloat16),
        whole_input,
    )
    positive_weight = jnp.exp(positive_score)
    exp_total = sums[:, 0] + positive_weight
    query_loss = jnp.log(exp_total) - positive_score
    positive_coeff = positive_weight / exp_total - 1.0
    inner = sums[:, 1] / exp_total + positive_coeff * positive_score
    pull = inverse_temp * (pull / exp_total[:, None] + positive_coeff[:, None] * positive_unit)
    head_grad = ((pull - inner[:, None] * unit_rows) / row_norm[:, None]).astype(jnp.bfloat16)

    gathered_grad, head_x = gather_head(head_grad)
    hidden_grad = lax.dot_general(
        gathered_grad, down_weight, contract_last, preferred_element_type=jnp.float32
    )
    gate_grad_act = (hidden_grad * gate_factor).astype(jnp.bfloat16)
    up_grad_act = (hidden_grad * silu_gate).astype(jnp.bfloat16)
    input_term = lax.dot_general(
        gate_grad_act, gate_weight, contract_last, preferred_element_type=jnp.float32
    ) + lax.dot_general(up_grad_act, up_weight, contract_last, preferred_element_type=jnp.float32)
    input_grad, hidden_grad_x, head_cols = finish_links(
        input_term.astype(jnp.bfloat16), hidden_grad.T.astype(jnp.bfloat16), head_x
    )
    over_groups = (((0, 2), (0, 1)), ((), ()))
    hidden_grad_x = hidden_grad_x.astype(jnp.float32)
    weight_grads = [
        lax.dot_general(
            (hidden_grad_x * factors_x[:, k].astype(jnp.float32)).astype(jnp.bfloat16),
            input_x,
            over_groups,
            preferred_element_type=jnp.float32,
        ).astype(jnp.bfloat16)
        for k in range(2)
    ]
    down_grad = lax.dot_general(
        hidden_x, head_cols.reshape(4, 256, 1024), over_groups, preferred_element_type=jnp.float32
    ).astype(jnp.bfloat16)
    return (query_loss, input_grad, weight_grads[0].T, weight_grads[1].T, down_grad)


def solution(mesh):
    return jax.shard_map(
        shards,
        mesh=mesh,
        in_specs=(
            P("dp", "fsdp"),
            P(("dp", "fsdp"), None),
            P(None, "fsdp"),
            P(None, "fsdp"),
            P("fsdp", None),
            P(("dp", "fsdp"), None),
            P(("dp", "fsdp"), None),
            P(None, ("dp", "fsdp"), None),
            P(None, ("dp", "fsdp")),
            P(("dp", "fsdp"), None),
        ),
        out_specs=(
            P(("dp", "fsdp")),
            P("dp", "fsdp"),
            P("dp", "fsdp"),
            P("dp", "fsdp"),
            P("fsdp", "dp"),
        ),
        check_vma=False,
    )
```

```python
import functools

import jax
import jax.numpy as jnp
from jax import lax
from jax.experimental import pallas as pl
from jax.experimental.pallas import tpu as pltpu
from jax.sharding import PartitionSpec as P

inverse_temp = 50.0
eps = 1e-06
contract_first = (((0,), (0,)), ((), ()))
contract_last = (((1,), (1,)), ((), ()))
ANY = pl.BlockSpec(memory_space=pl.ANY)
VMEM = pl.BlockSpec(memory_space=pltpu.VMEM)
DMA = pltpu.SemaphoreType.DMA
near_first = (1, 3, 2)
far_first = (2, 3, 1, 0)


class Place:
    def __init__(self):
        self.x = lax.axis_index("dp")
        self.f = lax.axis_index("fsdp")
        self.z = self.f // 8
        self.y = (self.f // 2) % 4
        self.c = self.f % 2
        self.a = self.y * (1 - self.c) + self.z * self.c
        self.b = self.z * (1 - self.c) + self.y * self.c
        self.partner = self.f + 1 - 2 * self.c

    def at(self, b, a, c):
        z = b * (1 - c) + a * c
        y = a * (1 - c) + b * c
        return (z * 4 + y) * 2 + c

    def a_peer(self, j):
        return self.at(self.b, (self.a + j) % 4, self.c)

    def b_peer(self, j):
        return self.at((self.b + j) % 4, self.a, self.c)


def copy_to(src, dst, send, recv, x, f):
    return pltpu.make_async_remote_copy(
        src_ref=src,
        dst_ref=dst,
        send_sem=send,
        recv_sem=recv,
        device_id=(x, f),
        device_id_type=pl.DeviceIdType.MESH,
    )


def meet(place, across):
    barrier = pltpu.get_barrier_semaphore()
    peers = [(place.x, place.partner)]
    peers += [(place.x, place.a_peer(j)) for j in near_first]
    peers += [(place.x, place.b_peer(j)) for j in near_first]
    if across:
        peers += [((place.x + j) % 4, place.f) for j in near_first]
    for x, f in peers:
        pl.semaphore_signal(barrier, inc=1, device_id=(x, f), device_id_type=pl.DeviceIdType.MESH)
    pl.semaphore_wait(barrier, len(peers))


class PlaneGather:
    copies = 32

    def __init__(self, place, src, out, view, send, recv):
        self.place, self.src, self.out, self.view = place, src, out, view
        self.send, self.recv = send, recv
        self.sent = []

    def push(self, ref, origin, f):
        copy = copy_to(
            ref,
            self.view(self.out, origin),
            self.send.at[len(self.sent)],
            self.recv.at[origin],
            self.place.x,
            f,
        )
        copy.start()
        self.sent.append(copy)

    def arrive(self, origin):
        block = self.view(self.out, origin)
        copy_to(
            block, block, self.send.at[31], self.recv.at[origin], self.place.x, self.place.partner
        ).wait_recv()
        return block

    def start(self):
        p = self.place
        self.own = pltpu.make_async_copy(self.src, self.view(self.out, p.f), self.send.at[31])
        for j in near_first:
            self.push(self.src, p.f, p.a_peer(j))
        for j in near_first:
            self.push(self.src, p.f, p.b_peer(j))
        self.push(self.src, p.f, p.partner)
        self.own.start()

    def relay(self):
        p = self.place
        for j in near_first:
            origin = p.a_peer(j)
            block = self.arrive(origin)
            for i in near_first:
                self.push(block, origin, p.b_peer(i))
            self.push(block, origin, p.partner)

    def hand(self):
        p = self.place
        for j in (0,) + near_first:
            for i in near_first:
                origin = p.at((p.b + i) % 4, (p.a + j) % 4, p.c)
                self.push(self.arrive(origin), origin, p.partner)

    def close(self):
        p = self.place
        for j in (0,) + near_first:
            for i in (0,) + near_first:
                z, y = (p.z + i) % 4, (p.y + j) % 4
                self.arrive((z * 4 + y) * 2 + 1 - p.c)
        self.own.wait()
        for copy in self.sent:
            copy.wait_send()


class PlaneScatter:
    def __init__(self, place, src, view, scratch):
        self.place, self.src, self.view = place, src, view
        (self.got1, self.sum1, self.got2, self.sum2, self.got3, self.send1, self.recv1,
         self.send2, self.recv2, self.send3, self.recv3) = scratch

    @staticmethod
    def scratch(block, dtype=jnp.bfloat16):
        wide = lambda *lead: pltpu.VMEM(lead + block, dtype)
        return [wide(16), wide(4, 4), wide(4, 4), wide(4), wide(4), DMA((16,)), DMA((16,)),
                DMA((4, 4)), DMA((4, 4)), DMA((4,)), DMA((4,))]

    def start(self):
        p = self.place
        self.sent1 = []
        for i in far_first:
            for j in far_first:
                b, a = (p.a + i) % 4, (p.b + j) % 4
                k = b * 4 + a
                copy = copy_to(
                    self.view(self.src, p.at(b, a, 1 - p.c)),
                    self.got1.at[k],
                    self.send1.at[k],
                    self.recv1.at[k],
                    p.x,
                    p.partner,
                )
                copy.start()
                self.sent1.append(copy)

    def middle(self):
        p = self.place
        sent2 = []
        for i in far_first:
            b = (p.b + i) % 4
            for j in far_first:
                a = (p.a + j) % 4
                k = b * 4 + a
                copy_to(
                    self.got1.at[k], self.got1.at[k], self.send1.at[k], self.recv1.at[k],
                    p.x, p.partner,
                ).wait_recv()
                own = self.view(self.src, p.at(b, a, p.c))[...].astype(jnp.float32)
                self.sum1[b, a] = (own + self.got1[k].astype(jnp.float32)).astype(self.sum1.dtype)
                if i:
                    copy = copy_to(
                        self.sum1.at[b, a], self.got2.at[p.b, a], self.send2.at[i, j],
                        self.recv2.at[p.b, a], p.x, p.b_peer(i),
                    )
                    copy.start()
                    sent2.append(copy)
        sent3 = []
        for j in far_first:
            a = (p.a + j) % 4
            total = self.sum1[p.b, a].astype(jnp.float32)
            for i in far_first[:3]:
                b = (p.b + i) % 4
                got = self.got2.at[b, a]
                copy_to(
                    got, got, self.send2.at[i, j], self.recv2.at[b, a], p.x, p.b_peer(i)
                ).wait_recv()
                total += got[...].astype(jnp.float32)
            if j:
                self.sum2[a] = total.astype(self.sum2.dtype)
                copy = copy_to(
                    self.sum2.at[a], self.got3.at[p.a], self.send3.at[j], self.recv3.at[p.a],
                    p.x, p.a_peer(j),
                )
                copy.start()
                sent3.append(copy)
        for j in near_first:
            a = (p.a + j) % 4
            copy_to(
                self.got3.at[a], self.got3.at[a], self.send3.at[j], self.recv3.at[a],
                p.x, p.a_peer(j),
            ).wait_recv()
            total += self.got3[a].astype(jnp.float32)
        for copy in self.sent1 + sent2 + sent3:
            copy.wait_send()
        return total


def across_gather(place, src, out, send, recv):
    own = pltpu.make_async_copy(src, out.at[place.x], send.at[0])
    own.start()
    sent = []
    for j in near_first:
        copy = copy_to(src, out.at[place.x], send.at[j], recv.at[place.x], (place.x + j) % 4, place.f)
        copy.start()
        sent.append(copy)

    def finish():
        for j in near_first:
            x = (place.x + j) % 4
            copy_to(out.at[x], out.at[x], send.at[j], recv.at[x], x, place.f).wait_recv()
        own.wait()
        for copy in sent:
            copy.wait_send()

    return finish


def params(collective_id, mib):
    return pltpu.CompilerParams(
        collective_id=collective_id, has_side_effects=True, vmem_limit_bytes=mib * 1024 * 1024
    )


def column_block(ref, f):
    return ref.at[:, pl.ds(pl.multiple_of(f * 128, 128), 128)]


def row_block(ref, f):
    return ref.at[f]


def gather_input(mlp_input, table):
    def kernel(src, tab, out, tab_x, tab_all, send, recv, x_send, x_recv, t_send, t_recv):
        place = Place()
        meet(place, True)
        finish_table = across_gather(place, tab, tab_x, x_send, x_recv)
        gather = PlaneGather(place, src, out, column_block, send, recv)
        gather.start()
        finish_table()
        tables = PlaneGather(place, tab_x, tab_all, row_block, t_send, t_recv)
        tables.start()
        gather.relay()
        tables.relay()
        gather.hand()
        tables.hand()
        gather.close()
        tables.close()

    rows, cols = mlp_input.shape
    ints = lambda *lead: jax.ShapeDtypeStruct(lead + table.shape, jnp.int32)
    out, _, tables = pl.pallas_call(
        kernel,
        out_shape=(jax.ShapeDtypeStruct((rows, cols * 32), jnp.bfloat16), ints(4), ints(32, 4)),
        in_specs=[ANY] * 2,
        out_specs=[ANY] * 3,
        scratch_shapes=[DMA((32,)), DMA((32,)), DMA((4,)), DMA((4,)), DMA((32,)), DMA((32,))],
        compiler_params=params(0, 4),
        name="gather_input",
    )(mlp_input, table)
    return out, tables


def scatter_branch(partial):
    def kernel(src, out, *scratch):
        place = Place()
        meet(place, False)
        scatter = PlaneScatter(place, src, row_block, scratch)
        scatter.start()
        out[...] = scatter.middle()

    return pl.pallas_call(
        kernel,
        out_shape=jax.ShapeDtypeStruct((8, 4096), jnp.float32),
        in_specs=[VMEM],
        out_specs=VMEM,
        scratch_shapes=PlaneScatter.scratch((8, 4096)),
        compiler_params=params(1, 12),
        name="scatter_branch",
    )(partial.reshape(32, 8, 4096))


def near_order(m):
    return m + m // 2 - 2 * (m // 3)


def owner_batch(count, batch_ref, code_ref, index_ref, scale_ref, weight_ref):
    raw = lax.dot_general(
        batch_ref[:count, :], index_ref[...], contract_last, preferred_element_type=jnp.float32
    )
    scale = scale_ref[...]
    scores = inverse_temp * raw * scale
    here = lax.broadcasted_iota(jnp.int32, scores.shape, 1)
    uses = jnp.zeros(scores.shape, jnp.float32)
    codes = code_ref[:count, :]
    for slot in range(8):
        uses += jnp.where(codes[:, slot : slot + 1] == here, 1.0, 0.0)
    weights = uses * jnp.exp(scores)
    exps = jnp.sum(weights, axis=1, keepdims=True)
    inners = jnp.sum(weights * scores, axis=1, keepdims=True)
    lane = lax.broadcasted_iota(jnp.int32, (count, 128), 1)
    weight_ref[:count, :] = (weights * scale).astype(jnp.bfloat16)
    return jnp.where(lane == 0, exps, jnp.where(lane == 1, inners, 0.0))


class AllSum:
    def __init__(self, place, src, scratch):
        self.place, self.src = place, src
        (self.got1, self.sum1, self.got2, self.sum2, self.got3, self.stage, self.got4, self.send1,
         self.recv1, self.send2, self.recv2, self.send3, self.recv3, self.send4,
         self.recv4) = scratch

    @staticmethod
    def scratch(width, dtype):
        wide = lambda *lead: pltpu.VMEM(lead + (32, width), dtype)
        last = pltpu.VMEM((4, 8, width), dtype)
        return [wide(16), wide(4, 4), wide(4, 4), wide(4), wide(4), last, last,
                DMA((16,)), DMA((16,)), DMA((4, 4)), DMA((4, 4))] + [DMA((4,))] * 4

    def rows(self, k, c):
        return self.src.at[pl.ds(pl.multiple_of(k * 64 + c * 32, 32), 32), :]

    def to_partner(self, k):
        p = self.place
        return copy_to(self.rows(k, 1 - p.c), self.got1.at[k], self.send1.at[k], self.recv1.at[k],
                       p.x, p.partner)

    def to_b(self, i, j):
        p = self.place
        b, a = (p.b + i) % 4, (p.a + j) % 4
        return copy_to(self.sum1.at[b, a], self.got2.at[p.b, a], self.send2.at[i, j],
                       self.recv2.at[p.b, a], p.x, p.b_peer(i))

    def to_a(self, j):
        p = self.place
        return copy_to(self.sum2.at[(p.a + j) % 4], self.got3.at[p.a], self.send3.at[j],
                       self.recv3.at[p.a], p.x, p.a_peer(j))

    def to_x(self, j):
        p = self.place
        x = (p.x + j) % 4
        return copy_to(self.stage.at[x], self.got4.at[p.x], self.send4.at[j], self.recv4.at[p.x],
                       x, p.f)

    def group(self, i):
        p = self.place
        b = (p.b + i) % 4

        def add(turn, carry):
            j = near_order(3 - turn)
            a = (p.a + j) % 4
            k = p.at(b, a, p.c) // 2
            got = self.got1.at[k]
            copy_to(got, got, self.send1.at[k], self.recv1.at[k], p.x, p.partner).wait_recv()
            own = self.rows(k, p.c)[...].astype(jnp.float32)
            self.sum1[b, a] = (own + got[...].astype(jnp.float32)).astype(self.sum1.dtype)
            if i:
                self.to_b(i, j).start()
            return carry

        lax.fori_loop(0, 4, add, 0)

    def second(self):
        p = self.place
        for j in far_first:
            a = (p.a + j) % 4
            total = self.sum1[p.b, a].astype(jnp.float32)
            for i in near_first:
                b = (p.b + i) % 4
                got = self.got2.at[b, a]
                copy_to(got, got, self.send2.at[i, j], self.recv2.at[b, a], p.x,
                        p.b_peer(i)).wait_recv()
                total += got[...].astype(jnp.float32)
            self.sum2[a] = total.astype(self.sum2.dtype)
            if j:
                self.to_a(j).start()

    def third(self):
        p = self.place
        total = self.sum2[p.a].astype(jnp.float32)
        for j in near_first:
            a = (p.a + j) % 4
            got = self.got3.at[a]
            copy_to(got, got, self.send3.at[j], self.recv3.at[a], p.x, p.a_peer(j)).wait_recv()
            total += got[...].astype(jnp.float32)
        for x in range(4):
            self.stage[x] = total[8 * x : 8 * x + 8].astype(self.stage.dtype)
        for j in near_first:
            self.to_x(j).start()

    def last(self):
        p = self.place
        own = self.stage[p.x].astype(jnp.float32)
        for j in near_first:
            x = (p.x + j) % 4
            got = self.got4.at[x]
            copy_to(got, got, self.send4.at[j], self.recv4.at[x], x, p.f).wait_recv()
            own += got[...].astype(jnp.float32)
        for j in near_first:
            for i in (0,) + near_first:
                self.to_b(j, i).wait_send()
            self.to_a(j).wait_send()
            self.to_x(j).wait_send()

        def sent(k, carry):
            self.to_partner(k).wait_send()
            return carry

        lax.fori_loop(0, 16, sent, 0)
        return own


def attend(unit_rows, span_index, codes, hidden, factors, whole_input):
    n = 15

    def kernel(unit, index, code, hid, fac, inp,
               pull_out, sums_out, hid_x, fac_x, inp_x,
               unit_x, query, pull, sums, batch, batch_code, weight, scale, u_send, u_recv, a_send, b_send, d_send, recv,
               h_send, h_recv, f_send, f_recv, i_send, i_recv, pair_send, pair_recv, *scratch):
        p = place = Place()
        meet(place, True)

        finish_unit = across_gather(place, unit, unit_x, u_send, u_recv)
        block = lambda f: query.at[pl.ds(pl.multiple_of(f * 32, 32), 32), :]
        half = lambda c: pl.ds(pl.multiple_of(c * 512, 512), 512)
        own_i = pltpu.make_async_copy(
            inp.at[:, pl.ds(pl.multiple_of(p.x * 1024, 1024), 1024)], inp_x.at[p.x], i_send.at[0]
        )
        own_i.start()
        finish_unit()
        block(p.f)[...] = jnp.concatenate(
            [unit_x[x].astype(jnp.float32) for x in range(4)], axis=0
        ).astype(jnp.bfloat16)

        def push(origin, f, send):
            copy = copy_to(block(origin), block(origin), send, recv.at[origin], p.x, f)
            copy.start()
            return copy

        def arrive(origin):
            copy_to(block(origin), block(origin), d_send.at[origin], recv.at[origin], p.x,
                    p.partner).wait_recv()

        sent = []
        for j in near_first:
            sent.append(push(p.f, p.a_peer(j), a_send.at[j]))
        for j in near_first:
            sent.append(push(p.f, p.b_peer(j), b_send.at[j]))
        push(p.f, p.partner, d_send.at[p.f])

        def norms(part, carry):
            rows = pl.ds(pl.multiple_of(part * 128, 128), 128)
            wide = index[rows, :].astype(jnp.float32)
            total = jnp.sum(wide * wide, axis=1, keepdims=True)
            row = lax.broadcasted_iota(jnp.int32, (128, 128), 0)
            col = lax.broadcasted_iota(jnp.int32, (128, 128), 1)
            across = jnp.sum(jnp.where(row == col, total, 0.0), axis=0, keepdims=True)
            scale[:, rows] = lax.rsqrt(across + eps)
            return carry

        for j in near_first:
            origin = p.a_peer(j)
            arrive(origin)
            for i in near_first:
                sent.append(push(origin, p.b_peer(i), b_send.at[4 * j + i]))
            push(origin, p.partner, d_send.at[origin])

        finish_hidden = across_gather(place, hid, hid_x, h_send, h_recv)
        finish_factors = across_gather(place, fac, fac_x, f_send, f_recv)
        for j in near_first:
            x = (p.x + j) % 4
            copy = copy_to(
                inp.at[:, pl.ds(pl.multiple_of(x * 1024 + p.c * 512, 512), 512)],
                inp_x.at[p.x, :, half(p.c)], i_send.at[j], i_recv.at[p.x], x, p.f,
            )
            copy.start()
            sent.append(copy)

        lax.fori_loop(0, index.shape[0] // 128, norms, 0)
        first = AllSum(place, pull, scratch[:n])
        second = AllSum(place, sums, scratch[n:])

        def chip_of(stage, turn):
            base, other = near_order(stage), near_order(stage + turn // 2)
            swap = turn % 2
            z = (p.z + base + (other - base) * swap) % 4
            y = (p.y + base + (other - base) * (1 - swap)) % 4
            return z * 4 + y

        for stages, groups in (((0,), ()), ((1,), (1,)), ((2, 3), (3, 2))):
            filled = 0
            for stage in stages:
                turns = 7 - 2 * stage

                def bring(turn, carry, stage=stage, filled=filled):
                    k = chip_of(stage, turn)
                    origin = k * 2 + p.c

                    def forward():
                        arrive(origin)
                        push(origin, p.partner, d_send.at[origin])

                    if stage:
                        forward()
                    else:
                        pl.when(jnp.logical_and(turn > 1, (turn + p.c) % 2 == 1))(forward)
                    arrive(k * 2 + 1 - p.c)
                    rows = pl.ds(pl.multiple_of(k * 64, 64), 64)
                    to = pl.ds(pl.multiple_of((filled + turn - 1) * 64, 64), 64)
                    batch[to, :] = query[rows, :]
                    batch_code[to, :] = code[rows, :]
                    return carry

                lax.fori_loop(1, 1 + turns, bring, 0)
                filled += turns
            total = owner_batch(filled * 64, batch, batch_code, index, scale, weight)
            chips = [chip_of(stage, turn) for stage in stages for turn in range(1, 8 - 2 * stage)]
            for part in range(4):
                cols = slice(part * 1024, part * 1024 + 1024)
                result = jnp.dot(
                    weight[: filled * 64, :], index[:, cols], preferred_element_type=jnp.float32
                ).astype(jnp.bfloat16)
                for t, k in enumerate(chips):
                    pull[pl.ds(pl.multiple_of(k * 64, 64), 64), cols] = result[64 * t : 64 * t + 64]
            for t, k in enumerate(chips):
                sums[pl.ds(pl.multiple_of(k * 64, 64), 64), :] = total[64 * t : 64 * t + 64]
                first.to_partner(k).start()
                second.to_partner(k).start()
            for group in groups:
                first.group(group)
                second.group(group)
        first.group(0)
        second.group(0)
        first.second()
        second.second()
        first.third()
        second.third()

        for j in near_first:
            x = (p.x + j) % 4
            region = inp_x.at[x, :, half(p.c)]
            copy_to(region, region, i_send.at[j], i_recv.at[x], x, p.f).wait_recv()
            copy = copy_to(region, region, pair_send.at[j], pair_recv.at[x], p.x, p.partner)
            copy.start()
            sent.append(copy)
        finish_hidden()
        finish_factors()
        pull_out[...] = first.last()
        sums_out[...] = second.last()
        for j in near_first:
            x = (p.x + j) % 4
            region = inp_x.at[x, :, half(1 - p.c)]
            copy_to(region, region, pair_send.at[j], pair_recv.at[x], p.x, p.partner).wait_recv()
        own_i.wait()
        for copy in sent:
            copy.wait_send()

        def pushed(k, carry):
            origin = k * 2 + p.c
            copy_to(block(origin), block(origin), d_send.at[origin], recv.at[origin], p.x,
                    p.partner).wait_send()
            return carry

        lax.fori_loop(0, 16, pushed, 0)

    bf = lambda *shape: jax.ShapeDtypeStruct(shape, jnp.bfloat16)
    return pl.pallas_call(
        kernel,
        out_shape=(
            jax.ShapeDtypeStruct((8, 4096), jnp.float32),
            jax.ShapeDtypeStruct((8, 128), jnp.float32),
            bf(4, *hidden.shape),
            bf(4, *factors.shape),
            bf(4, 256, 1024),
        ),
        in_specs=[ANY, VMEM, VMEM, ANY, ANY, ANY],
        out_specs=[VMEM, VMEM, ANY, ANY, ANY],
        scratch_shapes=[
            pltpu.VMEM((4, 8, 4096), jnp.bfloat16),
            pltpu.VMEM((1024, 4096), jnp.bfloat16),
            pltpu.VMEM((1024, 4096), jnp.bfloat16),
            pltpu.VMEM((1024, 128), jnp.float32),
            pltpu.VMEM((448, 4096), jnp.bfloat16),
            pltpu.VMEM((448, 8), jnp.int32),
            pltpu.VMEM((448, 512), jnp.bfloat16),
            pltpu.VMEM((1, 512), jnp.float32),
            DMA((4,)), DMA((4,)), DMA((4,)), DMA((16,)), DMA((32,)), DMA((32,)),
        ]
        + [DMA((4,))] * 8
        + AllSum.scratch(4096, jnp.bfloat16)
        + AllSum.scratch(128, jnp.float32),
        compiler_params=params(4, 52),
        name="attend",
    )(unit_rows, span_index, codes, hidden, factors, whole_input)


def gather_head(head_grad):
    def kernel(head, out, send, recv):
        place = Place()
        meet(place, False)
        gather = PlaneGather(place, head, out, row_block, send, recv)
        gather.start()
        gather.relay()
        gather.hand()
        gather.close()

    return pl.pallas_call(
        kernel,
        out_shape=jax.ShapeDtypeStruct((32, 8, 4096), jnp.bfloat16),
        in_specs=[ANY],
        out_specs=ANY,
        scratch_shapes=[DMA((32,)), DMA((32,))],
        compiler_params=params(2, 4),
        name="gather_head",
    )(head_grad).reshape(256, 4096)


class ColumnExchange:
    def __init__(self, place, src, out, sems):
        self.place, self.src, self.out = place, src, out
        self.send, self.recv, self.pair_send, self.pair_recv = sems

    def half(self, x, c):
        return self.out.at[x, :, pl.ds(pl.multiple_of(c * 512, 512), 512)]

    def start(self):
        p = self.place
        self.own = pltpu.make_async_copy(
            self.src.at[:, pl.ds(pl.multiple_of(p.x * 1024, 1024), 1024)], self.out.at[p.x],
            self.send.at[0],
        )
        self.own.start()
        self.sent = []
        for j in near_first:
            x = (p.x + j) % 4
            copy = copy_to(
                self.src.at[:, pl.ds(pl.multiple_of(x * 1024 + p.c * 512, 512), 512)],
                self.half(p.x, p.c), self.send.at[j], self.recv.at[p.x], x, p.f,
            )
            copy.start()
            self.sent.append(copy)

    def share(self):
        p = self.place
        for j in near_first:
            x = (p.x + j) % 4
            part = self.half(x, p.c)
            copy_to(part, part, self.send.at[j], self.recv.at[x], x, p.f).wait_recv()
            copy = copy_to(part, part, self.pair_send.at[j], self.pair_recv.at[x], p.x, p.partner)
            copy.start()
            self.sent.append(copy)

    def finish(self):
        p = self.place
        for j in near_first:
            x = (p.x + j) % 4
            part = self.half(x, 1 - p.c)
            copy_to(part, part, self.pair_send.at[j], self.pair_recv.at[x], p.x,
                    p.partner).wait_recv()
        self.own.wait()
        for copy in self.sent:
            copy.wait_send()


def finish_links(partial, acts, head):
    def kernel(src, act, head_ref, out, act_x, head_cols, x_send, x_recv, c0, c1, c2, c3, *scratch):
        place = Place()
        meet(place, True)
        scatter = PlaneScatter(place, src, column_block, scratch)
        scatter.start()
        finish_acts = across_gather(place, act, act_x, x_send, x_recv)
        columns = ColumnExchange(place, head_ref, head_cols, (c0, c1, c2, c3))
        columns.start()
        out[...] = scatter.middle().astype(jnp.bfloat16)
        finish_acts()
        columns.share()
        columns.finish()

    bf = lambda *shape: jax.ShapeDtypeStruct(shape, jnp.bfloat16)
    return pl.pallas_call(
        kernel,
        out_shape=(bf(256, 128), bf(4, *acts.shape), bf(4, 256, 1024)),
        in_specs=[VMEM, ANY, ANY],
        out_specs=[VMEM, ANY, ANY],
        scratch_shapes=[DMA((4,))] * 6 + PlaneScatter.scratch((256, 128)),
        compiler_params=params(3, 12),
        name="finish_links",
    )(partial, acts, head)


def shards(
    mlp_input,
    residual_in,
    gate_weight,
    up_weight,
    down_weight,
    span_index,
    positive_keys,
    request_rows,
    request_counts,
    negative_slots,
):
    dp_count = lax.axis_size("dp")
    fsdp_count = lax.axis_size("fsdp")
    owners = dp_count * fsdp_count
    slot_cap = request_rows.shape[2]
    rows, width = positive_keys.shape

    shape = (1, 1, slot_cap, owners)
    slot_ids = lax.broadcasted_iota(jnp.int32, shape, 3) * slot_cap
    slot_ids += lax.broadcasted_iota(jnp.int32, shape, 2)
    used = jnp.any(negative_slots[:, :, None, None] == slot_ids, axis=1).astype(jnp.int32)
    table = jnp.sum(used * (lax.broadcasted_iota(jnp.int32, used.shape, 0) + 1), axis=0) - 1
    whole_input, tables = gather_input(mlp_input, table)

    me = lax.axis_index("dp") * fsdp_count + lax.axis_index("fsdp")
    mine = lax.broadcasted_iota(jnp.int32, tables.shape, 3) == me
    user = jnp.sum(jnp.where(mine, tables, 0), axis=3).reshape(owners, slot_cap)
    requests = jnp.where(
        lax.broadcasted_iota(jnp.int32, (owners, slot_cap), 1) < request_counts,
        request_rows[:, 0, :],
        -1,
    )
    requests = requests.reshape(dp_count, fsdp_count, slot_cap).transpose(1, 0, 2)
    requests = requests.reshape(owners, slot_cap)
    ranks = lax.broadcasted_iota(jnp.int32, (1, rows, 1), 1)
    codes = jnp.where(user[:, None, :] == ranks, requests[:, None, :], -1)
    codes = codes.reshape(owners * rows, slot_cap)

    gate_act = jnp.dot(whole_input, gate_weight, preferred_element_type=jnp.float32)
    up_act = jnp.dot(whole_input, up_weight, preferred_element_type=jnp.float32)
    sigmoid_gate = jax.nn.sigmoid(gate_act)
    silu_gate = gate_act * sigmoid_gate
    hidden = (silu_gate * up_act).astype(jnp.bfloat16)
    branch = scatter_branch(jnp.dot(hidden, down_weight, preferred_element_type=jnp.bfloat16))
    top_state = branch + residual_in.astype(jnp.float32)
    row_norm = jnp.sqrt(jnp.sum(top_state * top_state, axis=-1) + eps)
    unit_rows = top_state / row_norm[:, None]
    positive = positive_keys.astype(jnp.float32)
    positive_unit = positive / jnp.sqrt(jnp.sum(positive * positive, axis=-1, keepdims=True) + eps)
    positive_score = inverse_temp * jnp.sum(unit_rows * positive_unit, axis=-1)

    gate_factor = up_act * (sigmoid_gate * (1.0 + gate_act * (1.0 - sigmoid_gate)))
    pull, sums, hidden_x, factors_x, input_x = attend(
        unit_rows.astype(jnp.bfloat16),
        span_index,
        codes,
        hidden.T,
        jnp.stack([gate_factor.T, silu_gate.T]).astype(jnp.bfloat16),
        whole_input,
    )
    positive_weight = jnp.exp(positive_score)
    exp_total = sums[:, 0] + positive_weight
    query_loss = jnp.log(exp_total) - positive_score
    positive_coeff = positive_weight / exp_total - 1.0
    inner = sums[:, 1] / exp_total + positive_coeff * positive_score
    pull = inverse_temp * (pull / exp_total[:, None] + positive_coeff[:, None] * positive_unit)
    head_grad = ((pull - inner[:, None] * unit_rows) / row_norm[:, None]).astype(jnp.bfloat16)

    gathered_grad = gather_head(head_grad)
    hidden_grad = lax.dot_general(
        gathered_grad, down_weight, contract_last, preferred_element_type=jnp.float32
    )
    gate_grad_act = (hidden_grad * gate_factor).astype(jnp.bfloat16)
    up_grad_act = (hidden_grad * silu_gate).astype(jnp.bfloat16)
    input_term = lax.dot_general(
        gate_grad_act, gate_weight, contract_last, preferred_element_type=jnp.float32
    ) + lax.dot_general(up_grad_act, up_weight, contract_last, preferred_element_type=jnp.float32)
    input_grad, hidden_grad_x, head_cols = finish_links(
        input_term.astype(jnp.bfloat16), hidden_grad.T.astype(jnp.bfloat16), gathered_grad
    )
    over_groups = (((0, 2), (0, 1)), ((), ()))
    hidden_grad_x = hidden_grad_x.astype(jnp.float32)
    weight_grads = [
        lax.dot_general(
            (hidden_grad_x * factors_x[:, k].astype(jnp.float32)).astype(jnp.bfloat16),
            input_x,
            over_groups,
            preferred_element_type=jnp.float32,
        ).astype(jnp.bfloat16)
        for k in range(2)
    ]
    down_grad = lax.dot_general(
        hidden_x, head_cols, over_groups, preferred_element_type=jnp.float32
    ).astype(jnp.bfloat16)
    return (query_loss, input_grad, weight_grads[0].T, weight_grads[1].T, down_grad)


def solution(mesh):
    return jax.shard_map(
        shards,
        mesh=mesh,
        in_specs=(
            P("dp", "fsdp"),
            P(("dp", "fsdp"), None),
            P(None, "fsdp"),
            P(None, "fsdp"),
            P("fsdp", None),
            P(("dp", "fsdp"), None),
            P(("dp", "fsdp"), None),
            P(None, ("dp", "fsdp"), None),
            P(None, ("dp", "fsdp")),
            P(("dp", "fsdp"), None),
        ),
        out_specs=(
            P(("dp", "fsdp")),
            P("dp", "fsdp"),
            P("dp", "fsdp"),
            P("dp", "fsdp"),
            P("fsdp", "dp"),
        ),
        check_vma=False,
    )
```

```python
import functools

import jax
import jax.numpy as jnp
from jax import lax
from jax.experimental import pallas as pl
from jax.experimental.pallas import tpu as pltpu
from jax.sharding import PartitionSpec as P

inverse_temp = 50.0
eps = 1e-06
contract_first = (((0,), (0,)), ((), ()))
contract_last = (((1,), (1,)), ((), ()))
ANY = pl.BlockSpec(memory_space=pl.ANY)
VMEM = pl.BlockSpec(memory_space=pltpu.VMEM)
DMA = pltpu.SemaphoreType.DMA
near_first = (1, 3, 2)
far_first = (2, 3, 1, 0)


class Place:
    def __init__(self):
        self.x = lax.axis_index("dp")
        self.f = lax.axis_index("fsdp")
        self.z = self.f // 8
        self.y = (self.f // 2) % 4
        self.c = self.f % 2
        self.a = self.y * (1 - self.c) + self.z * self.c
        self.b = self.z * (1 - self.c) + self.y * self.c
        self.partner = self.f + 1 - 2 * self.c

    def at(self, b, a, c):
        z = b * (1 - c) + a * c
        y = a * (1 - c) + b * c
        return (z * 4 + y) * 2 + c

    def a_peer(self, j):
        return self.at(self.b, (self.a + j) % 4, self.c)

    def b_peer(self, j):
        return self.at((self.b + j) % 4, self.a, self.c)


def copy_to(src, dst, send, recv, x, f):
    return pltpu.make_async_remote_copy(
        src_ref=src,
        dst_ref=dst,
        send_sem=send,
        recv_sem=recv,
        device_id=(x, f),
        device_id_type=pl.DeviceIdType.MESH,
    )


def meet(place, across):
    barrier = pltpu.get_barrier_semaphore()
    peers = [(place.x, place.partner)]
    peers += [(place.x, place.a_peer(j)) for j in near_first]
    peers += [(place.x, place.b_peer(j)) for j in near_first]
    if across:
        peers += [((place.x + j) % 4, place.f) for j in near_first]
    for x, f in peers:
        pl.semaphore_signal(barrier, inc=1, device_id=(x, f), device_id_type=pl.DeviceIdType.MESH)
    pl.semaphore_wait(barrier, len(peers))


class PlaneGather:
    copies = 32

    def __init__(self, place, src, out, view, send, recv):
        self.place, self.src, self.out, self.view = place, src, out, view
        self.send, self.recv = send, recv
        self.sent = []

    def push(self, ref, origin, f):
        copy = copy_to(
            ref,
            self.view(self.out, origin),
            self.send.at[len(self.sent)],
            self.recv.at[origin],
            self.place.x,
            f,
        )
        copy.start()
        self.sent.append(copy)

    def arrive(self, origin):
        block = self.view(self.out, origin)
        copy_to(
            block, block, self.send.at[31], self.recv.at[origin], self.place.x, self.place.partner
        ).wait_recv()
        return block

    def start(self):
        p = self.place
        self.own = pltpu.make_async_copy(self.src, self.view(self.out, p.f), self.send.at[31])
        for j in near_first:
            self.push(self.src, p.f, p.a_peer(j))
        for j in near_first:
            self.push(self.src, p.f, p.b_peer(j))
        self.push(self.src, p.f, p.partner)
        self.own.start()

    def relay(self):
        p = self.place
        for j in near_first:
            origin = p.a_peer(j)
            block = self.arrive(origin)
            for i in near_first:
                self.push(block, origin, p.b_peer(i))
            self.push(block, origin, p.partner)

    def hand(self):
        p = self.place
        for j in (0,) + near_first:
            for i in near_first:
                origin = p.at((p.b + i) % 4, (p.a + j) % 4, p.c)
                self.push(self.arrive(origin), origin, p.partner)

    def close(self):
        p = self.place
        for j in (0,) + near_first:
            for i in (0,) + near_first:
                z, y = (p.z + i) % 4, (p.y + j) % 4
                self.arrive((z * 4 + y) * 2 + 1 - p.c)
        self.own.wait()
        for copy in self.sent:
            copy.wait_send()


class PlaneScatter:
    def __init__(self, place, src, view, scratch):
        self.place, self.src, self.view = place, src, view
        (self.got1, self.sum1, self.got2, self.sum2, self.got3, self.send1, self.recv1,
         self.send2, self.recv2, self.send3, self.recv3) = scratch

    @staticmethod
    def scratch(block, dtype=jnp.bfloat16):
        wide = lambda *lead: pltpu.VMEM(lead + block, dtype)
        return [wide(16), wide(4, 4), wide(4, 4), wide(4), wide(4), DMA((16,)), DMA((16,)),
                DMA((4, 4)), DMA((4, 4)), DMA((4,)), DMA((4,))]

    def start(self):
        p = self.place
        self.sent1 = []
        for i in far_first:
            for j in far_first:
                b, a = (p.a + i) % 4, (p.b + j) % 4
                k = b * 4 + a
                copy = copy_to(
                    self.view(self.src, p.at(b, a, 1 - p.c)),
                    self.got1.at[k],
                    self.send1.at[k],
                    self.recv1.at[k],
                    p.x,
                    p.partner,
                )
                copy.start()
                self.sent1.append(copy)

    def middle(self):
        p = self.place
        sent2 = []
        for i in far_first:
            b = (p.b + i) % 4
            for j in far_first:
                a = (p.a + j) % 4
                k = b * 4 + a
                copy_to(
                    self.got1.at[k], self.got1.at[k], self.send1.at[k], self.recv1.at[k],
                    p.x, p.partner,
                ).wait_recv()
                own = self.view(self.src, p.at(b, a, p.c))[...].astype(jnp.float32)
                self.sum1[b, a] = (own + self.got1[k].astype(jnp.float32)).astype(self.sum1.dtype)
                if i:
                    copy = copy_to(
                        self.sum1.at[b, a], self.got2.at[p.b, a], self.send2.at[i, j],
                        self.recv2.at[p.b, a], p.x, p.b_peer(i),
                    )
                    copy.start()
                    sent2.append(copy)
        sent3 = []
        for j in far_first:
            a = (p.a + j) % 4
            total = self.sum1[p.b, a].astype(jnp.float32)
            for i in far_first[:3]:
                b = (p.b + i) % 4
                got = self.got2.at[b, a]
                copy_to(
                    got, got, self.send2.at[i, j], self.recv2.at[b, a], p.x, p.b_peer(i)
                ).wait_recv()
                total += got[...].astype(jnp.float32)
            if j:
                self.sum2[a] = total.astype(self.sum2.dtype)
                copy = copy_to(
                    self.sum2.at[a], self.got3.at[p.a], self.send3.at[j], self.recv3.at[p.a],
                    p.x, p.a_peer(j),
                )
                copy.start()
                sent3.append(copy)
        for j in near_first:
            a = (p.a + j) % 4
            copy_to(
                self.got3.at[a], self.got3.at[a], self.send3.at[j], self.recv3.at[a],
                p.x, p.a_peer(j),
            ).wait_recv()
            total += self.got3[a].astype(jnp.float32)
        for copy in self.sent1 + sent2 + sent3:
            copy.wait_send()
        return total


def across_gather(place, src, out, send, recv):
    own = pltpu.make_async_copy(src, out.at[place.x], send.at[0])
    own.start()
    sent = []
    for j in near_first:
        copy = copy_to(src, out.at[place.x], send.at[j], recv.at[place.x], (place.x + j) % 4, place.f)
        copy.start()
        sent.append(copy)

    def finish():
        for j in near_first:
            x = (place.x + j) % 4
            copy_to(out.at[x], out.at[x], send.at[j], recv.at[x], x, place.f).wait_recv()
        own.wait()
        for copy in sent:
            copy.wait_send()

    return finish


def params(collective_id, mib):
    return pltpu.CompilerParams(
        collective_id=collective_id, has_side_effects=True, vmem_limit_bytes=mib * 1024 * 1024
    )


def column_block(ref, f):
    return ref.at[:, pl.ds(pl.multiple_of(f * 128, 128), 128)]


def row_block(ref, f):
    return ref.at[f]


def gather_input(mlp_input, table):
    def kernel(src, tab, out, tab_x, tab_all, send, recv, x_send, x_recv, t_send, t_recv):
        place = Place()
        meet(place, True)
        finish_table = across_gather(place, tab, tab_x, x_send, x_recv)
        gather = PlaneGather(place, src, out, column_block, send, recv)
        gather.start()
        finish_table()
        tables = PlaneGather(place, tab_x, tab_all, row_block, t_send, t_recv)
        tables.start()
        gather.relay()
        tables.relay()
        gather.hand()
        tables.hand()
        gather.close()
        tables.close()

    rows, cols = mlp_input.shape
    ints = lambda *lead: jax.ShapeDtypeStruct(lead + table.shape, jnp.int32)
    out, _, tables = pl.pallas_call(
        kernel,
        out_shape=(jax.ShapeDtypeStruct((rows, cols * 32), jnp.bfloat16), ints(4), ints(32, 4)),
        in_specs=[ANY] * 2,
        out_specs=[ANY] * 3,
        scratch_shapes=[DMA((32,)), DMA((32,)), DMA((4,)), DMA((4,)), DMA((32,)), DMA((32,))],
        compiler_params=params(0, 4),
        name="gather_input",
    )(mlp_input, table)
    return out, tables


def scatter_branch(partial):
    def kernel(src, out, *scratch):
        place = Place()
        meet(place, False)
        scatter = PlaneScatter(place, src, row_block, scratch)
        scatter.start()
        out[...] = scatter.middle()

    return pl.pallas_call(
        kernel,
        out_shape=jax.ShapeDtypeStruct((8, 4096), jnp.float32),
        in_specs=[VMEM],
        out_specs=VMEM,
        scratch_shapes=PlaneScatter.scratch((8, 4096)),
        compiler_params=params(1, 12),
        name="scatter_branch",
    )(partial.reshape(32, 8, 4096))


def near_order(m):
    return m + m // 2 - 2 * (m // 3)


def owner_batch(count, batch_ref, code_ref, index_ref, scale_ref, weight_ref):
    raw = lax.dot_general(
        batch_ref[:count, :], index_ref[...], contract_last, preferred_element_type=jnp.float32
    )
    scale = scale_ref[...]
    scores = inverse_temp * raw * scale
    here = lax.broadcasted_iota(jnp.int32, scores.shape, 1)
    uses = jnp.zeros(scores.shape, jnp.float32)
    codes = code_ref[:count, :]
    for slot in range(8):
        uses += jnp.where(codes[:, slot : slot + 1] == here, 1.0, 0.0)
    weights = uses * jnp.exp(scores)
    exps = jnp.sum(weights, axis=1, keepdims=True)
    inners = jnp.sum(weights * scores, axis=1, keepdims=True)
    lane = lax.broadcasted_iota(jnp.int32, (count, 128), 1)
    weight_ref[:count, :] = (weights * scale).astype(jnp.bfloat16)
    return jnp.where(lane == 0, exps, jnp.where(lane == 1, inners, 0.0))


class AllSum:
    def __init__(self, place, src, scratch):
        self.place, self.src = place, src
        (self.got1, self.sum1, self.got2, self.sum2, self.got3, self.stage, self.got4, self.send1,
         self.recv1, self.send2, self.recv2, self.send3, self.recv3, self.send4,
         self.recv4) = scratch

    @staticmethod
    def scratch(width, dtype):
        wide = lambda *lead: pltpu.VMEM(lead + (32, width), dtype)
        last = pltpu.VMEM((4, 8, width), dtype)
        return [wide(16), wide(4, 4), wide(4, 4), wide(4), wide(4), last, last,
                DMA((16,)), DMA((16,)), DMA((4, 4)), DMA((4, 4))] + [DMA((4,))] * 4

    def rows(self, k, c):
        return self.src.at[pl.ds(pl.multiple_of(k * 64 + c * 32, 32), 32), :]

    def to_partner(self, k):
        p = self.place
        return copy_to(self.rows(k, 1 - p.c), self.got1.at[k], self.send1.at[k], self.recv1.at[k],
                       p.x, p.partner)

    def to_b(self, i, j):
        p = self.place
        b, a = (p.b + i) % 4, (p.a + j) % 4
        return copy_to(self.sum1.at[b, a], self.got2.at[p.b, a], self.send2.at[i, j],
                       self.recv2.at[p.b, a], p.x, p.b_peer(i))

    def to_a(self, j):
        p = self.place
        return copy_to(self.sum2.at[(p.a + j) % 4], self.got3.at[p.a], self.send3.at[j],
                       self.recv3.at[p.a], p.x, p.a_peer(j))

    def to_x(self, j):
        p = self.place
        x = (p.x + j) % 4
        return copy_to(self.stage.at[x], self.got4.at[p.x], self.send4.at[j], self.recv4.at[p.x],
                       x, p.f)

    def group(self, i):
        p = self.place
        b = (p.b + i) % 4

        def add(turn, carry):
            j = near_order(3 - turn)
            a = (p.a + j) % 4
            k = p.at(b, a, p.c) // 2
            got = self.got1.at[k]
            copy_to(got, got, self.send1.at[k], self.recv1.at[k], p.x, p.partner).wait_recv()
            own = self.rows(k, p.c)[...].astype(jnp.float32)
            self.sum1[b, a] = (own + got[...].astype(jnp.float32)).astype(self.sum1.dtype)
            if i:
                self.to_b(i, j).start()
            return carry

        lax.fori_loop(0, 4, add, 0)

    def second(self):
        p = self.place
        for j in far_first:
            a = (p.a + j) % 4
            total = self.sum1[p.b, a].astype(jnp.float32)
            for i in near_first:
                b = (p.b + i) % 4
                got = self.got2.at[b, a]
                copy_to(got, got, self.send2.at[i, j], self.recv2.at[b, a], p.x,
                        p.b_peer(i)).wait_recv()
                total += got[...].astype(jnp.float32)
            self.sum2[a] = total.astype(self.sum2.dtype)
            if j:
                self.to_a(j).start()

    def third(self):
        p = self.place
        total = self.sum2[p.a].astype(jnp.float32)
        for j in near_first:
            a = (p.a + j) % 4
            got = self.got3.at[a]
            copy_to(got, got, self.send3.at[j], self.recv3.at[a], p.x, p.a_peer(j)).wait_recv()
            total += got[...].astype(jnp.float32)
        for x in range(4):
            self.stage[x] = total[8 * x : 8 * x + 8].astype(self.stage.dtype)
        for j in near_first:
            self.to_x(j).start()

    def last(self):
        p = self.place
        own = self.stage[p.x].astype(jnp.float32)
        for j in near_first:
            x = (p.x + j) % 4
            got = self.got4.at[x]
            copy_to(got, got, self.send4.at[j], self.recv4.at[x], x, p.f).wait_recv()
            own += got[...].astype(jnp.float32)
        for j in near_first:
            for i in (0,) + near_first:
                self.to_b(j, i).wait_send()
            self.to_a(j).wait_send()
            self.to_x(j).wait_send()

        def sent(k, carry):
            self.to_partner(k).wait_send()
            return carry

        lax.fori_loop(0, 16, sent, 0)
        return own


def attend(unit_rows, span_index, codes, hidden, factors, whole_input):
    n = 15

    def kernel(unit, index, code, hid, fac, inp,
               pull_out, sums_out, hid_x, fac_x, inp_x,
               unit_x, query, pull, sums, batch, batch_code, weight, scale, u_send, u_recv, a_send, b_send, d_send, recv,
               h_send, h_recv, f_send, f_recv, i_send, i_recv, pair_send, pair_recv, *scratch):
        p = place = Place()
        meet(place, True)

        finish_unit = across_gather(place, unit, unit_x, u_send, u_recv)
        block = lambda f: query.at[pl.ds(pl.multiple_of(f * 32, 32), 32), :]
        half = lambda c: pl.ds(pl.multiple_of(c * 512, 512), 512)
        own_i = pltpu.make_async_copy(
            inp.at[:, pl.ds(pl.multiple_of(p.x * 1024, 1024), 1024)], inp_x.at[p.x], i_send.at[0]
        )
        own_i.start()
        finish_unit()
        block(p.f)[...] = jnp.concatenate(
            [unit_x[x].astype(jnp.float32) for x in range(4)], axis=0
        ).astype(jnp.bfloat16)

        def push(origin, f, send):
            copy = copy_to(block(origin), block(origin), send, recv.at[origin], p.x, f)
            copy.start()
            return copy

        def arrive(origin):
            copy_to(block(origin), block(origin), d_send.at[origin], recv.at[origin], p.x,
                    p.partner).wait_recv()

        sent = []
        for j in near_first:
            sent.append(push(p.f, p.a_peer(j), a_send.at[j]))
        for j in near_first:
            sent.append(push(p.f, p.b_peer(j), b_send.at[j]))
        push(p.f, p.partner, d_send.at[p.f])

        def norms(part, carry):
            rows = pl.ds(pl.multiple_of(part * 128, 128), 128)
            wide = index[rows, :].astype(jnp.float32)
            total = jnp.sum(wide * wide, axis=1, keepdims=True)
            row = lax.broadcasted_iota(jnp.int32, (128, 128), 0)
            col = lax.broadcasted_iota(jnp.int32, (128, 128), 1)
            across = jnp.sum(jnp.where(row == col, total, 0.0), axis=0, keepdims=True)
            scale[:, rows] = lax.rsqrt(across + eps)
            return carry

        for j in near_first:
            origin = p.a_peer(j)
            arrive(origin)
            for i in near_first:
                sent.append(push(origin, p.b_peer(i), b_send.at[4 * j + i]))
            push(origin, p.partner, d_send.at[origin])

        finish_hidden = across_gather(place, hid, hid_x, h_send, h_recv)
        finish_factors = across_gather(place, fac, fac_x, f_send, f_recv)
        for j in near_first:
            x = (p.x + j) % 4
            copy = copy_to(
                inp.at[:, pl.ds(pl.multiple_of(x * 1024 + p.c * 512, 512), 512)],
                inp_x.at[p.x, :, half(p.c)], i_send.at[j], i_recv.at[p.x], x, p.f,
            )
            copy.start()
            sent.append(copy)

        lax.fori_loop(0, index.shape[0] // 128, norms, 0)
        first = AllSum(place, pull, scratch[:n])
        second = AllSum(place, sums, scratch[n:])

        def chip_of(stage, turn):
            base, other = near_order(stage), near_order(stage + turn // 2)
            swap = turn % 2
            z = (p.z + base + (other - base) * swap) % 4
            y = (p.y + base + (other - base) * (1 - swap)) % 4
            return z * 4 + y

        for stages, groups in (((0,), ()), ((1,), (1,)), ((2, 3), (2, 3))):
            filled = 0
            for stage in stages:
                turns = 7 - 2 * stage

                def bring(turn, carry, stage=stage, filled=filled):
                    k = chip_of(stage, turn)
                    origin = k * 2 + p.c

                    def forward():
                        arrive(origin)
                        push(origin, p.partner, d_send.at[origin])

                    if stage:
                        forward()
                    else:
                        pl.when(jnp.logical_and(turn > 1, (turn + p.c) % 2 == 1))(forward)
                    arrive(k * 2 + 1 - p.c)
                    rows = pl.ds(pl.multiple_of(k * 64, 64), 64)
                    to = pl.ds(pl.multiple_of((filled + turn - 1) * 64, 64), 64)
                    batch[to, :] = query[rows, :]
                    batch_code[to, :] = code[rows, :]
                    return carry

                lax.fori_loop(1, 1 + turns, bring, 0)
                filled += turns
            total = owner_batch(filled * 64, batch, batch_code, index, scale, weight)
            chips = [chip_of(stage, turn) for stage in stages for turn in range(1, 8 - 2 * stage)]
            for part in range(4):
                cols = slice(part * 1024, part * 1024 + 1024)
                result = jnp.dot(
                    weight[: filled * 64, :], index[:, cols], preferred_element_type=jnp.float32
                ).astype(jnp.bfloat16)
                for t, k in enumerate(chips):
                    pull[pl.ds(pl.multiple_of(k * 64, 64), 64), cols] = result[64 * t : 64 * t + 64]
            for t, k in enumerate(chips):
                sums[pl.ds(pl.multiple_of(k * 64, 64), 64), :] = total[64 * t : 64 * t + 64]
                first.to_partner(k).start()
                second.to_partner(k).start()
            for group in groups:
                first.group(group)
                second.group(group)
        first.group(0)
        second.group(0)
        first.second()
        second.second()
        first.third()
        second.third()

        for j in near_first:
            x = (p.x + j) % 4
            region = inp_x.at[x, :, half(p.c)]
            copy_to(region, region, i_send.at[j], i_recv.at[x], x, p.f).wait_recv()
            copy = copy_to(region, region, pair_send.at[j], pair_recv.at[x], p.x, p.partner)
            copy.start()
            sent.append(copy)
        finish_hidden()
        finish_factors()
        pull_out[...] = first.last()
        sums_out[...] = second.last()
        for j in near_first:
            x = (p.x + j) % 4
            region = inp_x.at[x, :, half(1 - p.c)]
            copy_to(region, region, pair_send.at[j], pair_recv.at[x], p.x, p.partner).wait_recv()
        own_i.wait()
        for copy in sent:
            copy.wait_send()

        def pushed(k, carry):
            origin = k * 2 + p.c
            copy_to(block(origin), block(origin), d_send.at[origin], recv.at[origin], p.x,
                    p.partner).wait_send()
            return carry

        lax.fori_loop(0, 16, pushed, 0)

    bf = lambda *shape: jax.ShapeDtypeStruct(shape, jnp.bfloat16)
    return pl.pallas_call(
        kernel,
        out_shape=(
            jax.ShapeDtypeStruct((8, 4096), jnp.float32),
            jax.ShapeDtypeStruct((8, 128), jnp.float32),
            bf(4, *hidden.shape),
            bf(4, *factors.shape),
            bf(4, 256, 1024),
        ),
        in_specs=[ANY, VMEM, VMEM, ANY, ANY, ANY],
        out_specs=[VMEM, VMEM, ANY, ANY, ANY],
        scratch_shapes=[
            pltpu.VMEM((4, 8, 4096), jnp.bfloat16),
            pltpu.VMEM((1024, 4096), jnp.bfloat16),
            pltpu.VMEM((1024, 4096), jnp.bfloat16),
            pltpu.VMEM((1024, 128), jnp.float32),
            pltpu.VMEM((448, 4096), jnp.bfloat16),
            pltpu.VMEM((448, 8), jnp.int32),
            pltpu.VMEM((448, 512), jnp.bfloat16),
            pltpu.VMEM((1, 512), jnp.float32),
            DMA((4,)), DMA((4,)), DMA((4,)), DMA((16,)), DMA((32,)), DMA((32,)),
        ]
        + [DMA((4,))] * 8
        + AllSum.scratch(4096, jnp.bfloat16)
        + AllSum.scratch(128, jnp.float32),
        compiler_params=params(4, 52),
        name="attend",
    )(unit_rows, span_index, codes, hidden, factors, whole_input)


def gather_head(head_grad):
    def kernel(head, out, send, recv):
        place = Place()
        meet(place, False)
        gather = PlaneGather(place, head, out, row_block, send, recv)
        gather.start()
        gather.relay()
        gather.hand()
        gather.close()

    return pl.pallas_call(
        kernel,
        out_shape=jax.ShapeDtypeStruct((32, 8, 4096), jnp.bfloat16),
        in_specs=[ANY],
        out_specs=ANY,
        scratch_shapes=[DMA((32,)), DMA((32,))],
        compiler_params=params(2, 4),
        name="gather_head",
    )(head_grad).reshape(256, 4096)


class ColumnExchange:
    def __init__(self, place, src, out, sems):
        self.place, self.src, self.out = place, src, out
        self.send, self.recv, self.pair_send, self.pair_recv = sems

    def half(self, x, c):
        return self.out.at[x, :, pl.ds(pl.multiple_of(c * 512, 512), 512)]

    def start(self):
        p = self.place
        self.own = pltpu.make_async_copy(
            self.src.at[:, pl.ds(pl.multiple_of(p.x * 1024, 1024), 1024)], self.out.at[p.x],
            self.send.at[0],
        )
        self.own.start()
        self.sent = []
        for j in near_first:
            x = (p.x + j) % 4
            copy = copy_to(
                self.src.at[:, pl.ds(pl.multiple_of(x * 1024 + p.c * 512, 512), 512)],
                self.half(p.x, p.c), self.send.at[j], self.recv.at[p.x], x, p.f,
            )
            copy.start()
            self.sent.append(copy)

    def share(self):
        p = self.place
        for j in near_first:
            x = (p.x + j) % 4
            part = self.half(x, p.c)
            copy_to(part, part, self.send.at[j], self.recv.at[x], x, p.f).wait_recv()
            copy = copy_to(part, part, self.pair_send.at[j], self.pair_recv.at[x], p.x, p.partner)
            copy.start()
            self.sent.append(copy)

    def finish(self):
        p = self.place
        for j in near_first:
            x = (p.x + j) % 4
            part = self.half(x, 1 - p.c)
            copy_to(part, part, self.pair_send.at[j], self.pair_recv.at[x], p.x,
                    p.partner).wait_recv()
        self.own.wait()
        for copy in self.sent:
            copy.wait_send()


def finish_links(partial, acts, head):
    def kernel(src, act, head_ref, out, act_x, head_cols, x_send, x_recv, c0, c1, c2, c3, *scratch):
        place = Place()
        meet(place, True)
        scatter = PlaneScatter(place, src, column_block, scratch)
        scatter.start()
        finish_acts = across_gather(place, act, act_x, x_send, x_recv)
        columns = ColumnExchange(place, head_ref, head_cols, (c0, c1, c2, c3))
        columns.start()
        out[...] = scatter.middle().astype(jnp.bfloat16)
        finish_acts()
        columns.share()
        columns.finish()

    bf = lambda *shape: jax.ShapeDtypeStruct(shape, jnp.bfloat16)
    return pl.pallas_call(
        kernel,
        out_shape=(bf(256, 128), bf(4, *acts.shape), bf(4, 256, 1024)),
        in_specs=[VMEM, ANY, ANY],
        out_specs=[VMEM, ANY, ANY],
        scratch_shapes=[DMA((4,))] * 6 + PlaneScatter.scratch((256, 128)),
        compiler_params=params(3, 12),
        name="finish_links",
    )(partial, acts, head)


def shards(
    mlp_input,
    residual_in,
    gate_weight,
    up_weight,
    down_weight,
    span_index,
    positive_keys,
    request_rows,
    request_counts,
    negative_slots,
):
    dp_count = lax.axis_size("dp")
    fsdp_count = lax.axis_size("fsdp")
    owners = dp_count * fsdp_count
    slot_cap = request_rows.shape[2]
    rows, width = positive_keys.shape

    shape = (1, 1, slot_cap, owners)
    slot_ids = lax.broadcasted_iota(jnp.int32, shape, 3) * slot_cap
    slot_ids += lax.broadcasted_iota(jnp.int32, shape, 2)
    used = jnp.any(negative_slots[:, :, None, None] == slot_ids, axis=1).astype(jnp.int32)
    table = jnp.sum(used * (lax.broadcasted_iota(jnp.int32, used.shape, 0) + 1), axis=0) - 1
    whole_input, tables = gather_input(mlp_input, table)

    me = lax.axis_index("dp") * fsdp_count + lax.axis_index("fsdp")
    mine = lax.broadcasted_iota(jnp.int32, tables.shape, 3) == me
    user = jnp.sum(jnp.where(mine, tables, 0), axis=3).reshape(owners, slot_cap)
    requests = jnp.where(
        lax.broadcasted_iota(jnp.int32, (owners, slot_cap), 1) < request_counts,
        request_rows[:, 0, :],
        -1,
    )
    requests = requests.reshape(dp_count, fsdp_count, slot_cap).transpose(1, 0, 2)
    requests = requests.reshape(owners, slot_cap)
    ranks = lax.broadcasted_iota(jnp.int32, (1, rows, 1), 1)
    codes = jnp.where(user[:, None, :] == ranks, requests[:, None, :], -1)
    codes = codes.reshape(owners * rows, slot_cap)

    gate_act = jnp.dot(whole_input, gate_weight, preferred_element_type=jnp.float32)
    up_act = jnp.dot(whole_input, up_weight, preferred_element_type=jnp.float32)
    sigmoid_gate = jax.nn.sigmoid(gate_act)
    silu_gate = gate_act * sigmoid_gate
    hidden = (silu_gate * up_act).astype(jnp.bfloat16)
    branch = scatter_branch(jnp.dot(hidden, down_weight, preferred_element_type=jnp.bfloat16))
    top_state = branch + residual_in.astype(jnp.float32)
    row_norm = jnp.sqrt(jnp.sum(top_state * top_state, axis=-1) + eps)
    unit_rows = top_state / row_norm[:, None]
    positive = positive_keys.astype(jnp.float32)
    positive_unit = positive / jnp.sqrt(jnp.sum(positive * positive, axis=-1, keepdims=True) + eps)
    positive_score = inverse_temp * jnp.sum(unit_rows * positive_unit, axis=-1)

    gate_factor = up_act * (sigmoid_gate * (1.0 + gate_act * (1.0 - sigmoid_gate)))
    pull, sums, hidden_x, factors_x, input_x = attend(
        unit_rows.astype(jnp.bfloat16),
        span_index,
        codes,
        hidden.T,
        jnp.stack([gate_factor.T, silu_gate.T]).astype(jnp.bfloat16),
        whole_input,
    )
    positive_weight = jnp.exp(positive_score)
    exp_total = sums[:, 0] + positive_weight
    query_loss = jnp.log(exp_total) - positive_score
    positive_coeff = positive_weight / exp_total - 1.0
    inner = sums[:, 1] / exp_total + positive_coeff * positive_score
    pull = inverse_temp * (pull / exp_total[:, None] + positive_coeff[:, None] * positive_unit)
    head_grad = ((pull - inner[:, None] * unit_rows) / row_norm[:, None]).astype(jnp.bfloat16)

    gathered_grad = gather_head(head_grad)
    hidden_grad = lax.dot_general(
        gathered_grad, down_weight, contract_last, preferred_element_type=jnp.float32
    )
    gate_grad_act = (hidden_grad * gate_factor).astype(jnp.bfloat16)
    up_grad_act = (hidden_grad * silu_gate).astype(jnp.bfloat16)
    input_term = lax.dot_general(
        gate_grad_act, gate_weight, contract_last, preferred_element_type=jnp.float32
    ) + lax.dot_general(up_grad_act, up_weight, contract_last, preferred_element_type=jnp.float32)
    input_grad, hidden_grad_x, head_cols = finish_links(
        input_term.astype(jnp.bfloat16), hidden_grad.T.astype(jnp.bfloat16), gathered_grad
    )
    over_groups = (((0, 2), (0, 1)), ((), ()))
    hidden_grad_x = hidden_grad_x.astype(jnp.float32)
    weight_grads = [
        lax.dot_general(
            (hidden_grad_x * factors_x[:, k].astype(jnp.float32)).astype(jnp.bfloat16),
            input_x,
            over_groups,
            preferred_element_type=jnp.float32,
        ).astype(jnp.bfloat16)
        for k in range(2)
    ]
    down_grad = lax.dot_general(
        hidden_x, head_cols, over_groups, preferred_element_type=jnp.float32
    ).astype(jnp.bfloat16)
    return (query_loss, input_grad, weight_grads[0].T, weight_grads[1].T, down_grad)


def solution(mesh):
    return jax.shard_map(
        shards,
        mesh=mesh,
        in_specs=(
            P("dp", "fsdp"),
            P(("dp", "fsdp"), None),
            P(None, "fsdp"),
            P(None, "fsdp"),
            P("fsdp", None),
            P(("dp", "fsdp"), None),
            P(("dp", "fsdp"), None),
            P(None, ("dp", "fsdp"), None),
            P(None, ("dp", "fsdp")),
            P(("dp", "fsdp"), None),
        ),
        out_specs=(
            P(("dp", "fsdp")),
            P("dp", "fsdp"),
            P("dp", "fsdp"),
            P("dp", "fsdp"),
            P("fsdp", "dp"),
        ),
        check_vma=False,
    )
```
